32 devices in a mesh: ctx: 2 (over core), dp: 16 (over z, y, x).
Axes of the slice: x: 2, y: 2, z: 4, core: 2. Of those that a mesh axis runs over, the one named last changes fastest.
Arguments:
- tokens: bfloat16 [16, 1024, 768], P('dp', 'ctx'), may hold values from -6 to 6
- lengths: int32 [16], P('dp'), may hold values from 256 to 1024, as said below
- qkv_weight: bfloat16 [768, 2304], P('dp'), may hold values from -0.21875 to 0.21875
- query_bias: bfloat16 [768], P('dp'), may hold values from -3 to 3
- value_bias: bfloat16 [768], P('dp'), may hold values from -0.1796875 to 0.1796875
- out_weight: bfloat16 [768, 768], P('dp'), may hold values from -4 to 4
- out_bias: bfloat16 [768], P('dp'), may hold values from -0.59765625 to 0.59765625
- norm1_gain: bfloat16 [768], P('dp'), may hold values from 0.5 to 1.5
- norm1_shift: bfloat16 [768], P('dp'), may hold values from -0.59765625 to 0.59765625
- up_weight: bfloat16 [768, 3072], P('dp'), may hold values from -0.21875 to 0.21875
- up_bias: bfloat16 [3072], P('dp'), may hold values from -3 to 3
- down_weight: bfloat16 [3072, 768], P('dp'), may hold values from -0.109375 to 0.109375
- down_bias: bfloat16 [768], P('dp'), may hold values from -0.59765625 to 0.59765625
- norm2_gain: bfloat16 [768], P('dp'), may hold values from 0.5 to 1.5
- norm2_shift: bfloat16 [768], P('dp'), may hold values from -0.59765625 to 0.59765625
- cotangent: bfloat16 [16, 1024, 768], P('dp', 'ctx'), may hold values from -6 to 6
Outputs:
- output: bfloat16 [16, 1024, 768], P('dp', 'ctx')
- input_grad: float32 [16, 1024, 768], P('dp', 'ctx')
- stream_rms: float32 [3], replicated
- grad_qkv_weight: float32 [768, 2304], P('dp')
- grad_query_bias: float32 [768], P('dp')
- grad_value_bias: float32 [768], P('dp')
- grad_out_weight: float32 [768, 768], P('dp')
- grad_out_bias: float32 [768], P('dp')
- grad_norm1_gain: float32 [768], P('dp')
- grad_norm1_shift: float32 [768], P('dp')
- grad_up_weight: float32 [768, 3072], P('dp')
- grad_up_bias: float32 [3072], P('dp')
- grad_down_weight: float32 [3072, 768], P('dp')
- grad_down_bias: float32 [768], P('dp')
- grad_norm2_gain: float32 [768], P('dp')
- grad_norm2_shift: float32 [768], P('dp')
The draws below stay inside these ranges and needn't reach their ends.
Inputs may be any that keep to these rules, and one draw needn't show every extreme that they name: The first lengths[b] tokens of sequence b are real and the rest is padding; in every draw some sequence has 1024 valid tokens and some has 256.
All inputs are finite; a program needn't handle non-finite values.
Results may differ from the reference program's by a relative error of at most 0.02.
Values may be sent and summed in bfloat16 or wider, within the bound.
No kernel may reach another device: no remote copies, remote signals or barrier semaphores. Data moves between devices by JAX's collectives and lax.ppermute only.
A program may use at most 128 MiB of HBM per device.

```python
import math
import jax
import jax.numpy as jnp
from jax import lax

HEADS = 12
HEAD_DIM = 64
D = 768
FF = 3072
SEQ_LEN = 1024
SEQS = 16


def draw_lengths(key, part):
    first_key, second_key = jax.random.split(key)
    length_draw = jax.random.randint(first_key, (SEQS,), SEQ_LEN // 4, SEQ_LEN + 1, dtype=jnp.int32)
    chosen = jax.random.permutation(second_key, SEQS)
    length_draw = length_draw.at[chosen[0]].set(SEQ_LEN)
    return length_draw.at[chosen[1]].set(SEQ_LEN // 4)


def with_spikes(array, rng, source, target, parts, factor):
    def block_of(dim):
        return (jnp.arange(array.shape[dim]) // (array.shape[dim] // parts)).reshape((-1,) + (1,) * (array.ndim - 1 - dim))

    near = jax.random.permutation(rng, parts)[block_of(target)]
    other_side = (block_of(target) + parts // 2) % parts
    return jnp.where((block_of(source) == near) | (block_of(source) == other_side), factor * array, array)


def levels(stream_key, extent, cuts, least, largest):
    def one(position, shards_of):
        steps = jax.random.uniform(jax.random.fold_in(jax.random.fold_in(stream_key, 6), position), (shards_of,), jnp.float32, least / len(cuts), largest / len(cuts))
        return jnp.repeat(jnp.exp(steps), extent[position] // shards_of).reshape((-1,) + (1,) * (len(extent) - position - 1))

    level = one(*cuts[0])
    for cut in cuts[1:]:
        level = level * one(*cut)
    return level


def scatter_about(own_key, dims, deviation, limit, cuts=(), held_as=jnp.bfloat16):
    entries = deviation * jax.random.normal(own_key, dims, jnp.float32)
    if cuts:
        entries = entries * levels(own_key, dims, cuts, -0.22, 0.18)
    return jnp.clip(entries, -limit, limit).astype(held_as)


def heavy_noise(rng, extent, deviation, bound, cuts, heavy, held_as=jnp.bfloat16):
    values = deviation * jax.random.normal(rng, extent, jnp.float32)
    if cuts:
        values = values * levels(rng, extent, cuts, -0.22, 0.18)
    return jnp.clip(with_spikes(values, jax.random.fold_in(rng, 3), *heavy), -bound, bound).astype(held_as)


def setup_inputs(seed: int = 0) -> dict:
    key_of = jax.random.split(jax.random.key(seed), 17)
    tokens = scatter_about(key_of[0], (SEQS, SEQ_LEN, D), 1.0, 6.0, ((0, 16), (1, 2)))
    lengths = draw_lengths(jax.random.fold_in(key_of[16], 71), 0)
    qkv_weight = scatter_about(key_of[2], (D, 3 * D), D ** -0.5, 0.21875, ((0, 16),))
    query_bias = scatter_about(key_of[3], (D,), 0.5, 3.0, ((0, 16),))
    value_bias = scatter_about(key_of[4], (D,), 0.03, 0.1796875, ((0, 16),))
    out_weight = scatter_about(key_of[5], (D, D), (max(D // 384, 1)) ** -0.5, 4.0, ((0, 16),))
    out_bias = scatter_about(key_of[6], (D,), 0.1, 0.59765625, ((0, 16),))
    norm1_gain = jnp.clip(1.0 + 0.1 * jax.random.normal(key_of[7], (D,), jnp.float32), 0.5, 1.5).astype(jnp.bfloat16)
    norm1_shift = scatter_about(key_of[8], (D,), 0.1, 0.59765625, ((0, 16),))
    up_weight = scatter_about(key_of[9], (D, FF), D ** -0.5, 0.21875, ((0, 16),))
    up_bias = scatter_about(key_of[10], (FF,), 0.5, 3.0, ((0, 16),))
    down_weight = scatter_about(key_of[11], (FF, D), FF ** -0.5, 0.109375, ((0, 16),))
    down_bias = scatter_about(key_of[12], (D,), 0.1, 0.59765625, ((0, 16),))
    norm2_gain = jnp.clip(1.0 + 0.1 * jax.random.normal(key_of[13], (D,), jnp.float32), 0.5, 1.5).astype(jnp.bfloat16)
    norm2_shift = scatter_about(key_of[14], (D,), 0.1, 0.59765625, ((0, 16),))
    cotangent = heavy_noise(key_of[15], (SEQS, SEQ_LEN, D), 1.0, 6.0, ((0, 16), (1, 2)), (0, 2, 16, 2.0))
    return dict(tokens=tokens, lengths=lengths, qkv_weight=qkv_weight, query_bias=query_bias, value_bias=value_bias, out_weight=out_weight, out_bias=out_bias, norm1_gain=norm1_gain, norm1_shift=norm1_shift, up_weight=up_weight, up_bias=up_bias, down_weight=down_weight, down_bias=down_bias, norm2_gain=norm2_gain, norm2_shift=norm2_shift, cotangent=cotangent)


@jax.custom_vjp
def low(v):
    return lax.optimization_barrier(v.astype(jnp.bfloat16)).astype(jnp.float32)

@jax.custom_vjp
def low_back(v):
    return v

def low_keep(v):
    return (low(v), None)

def low_pass(kept, grad):
    return (grad,)

def back_keep(v):
    return (v, None)

def back_low(kept, grad):
    return (low(grad),)
low.defvjp(low_keep, low_pass)
low_back.defvjp(back_keep, back_low)

def exact_dot(left, right):
    return jnp.dot(left, right, precision=lax.Precision.HIGHEST, preferred_element_type=jnp.float32)

def layer_norm(resid, gain, shift):
    center = resid - lax.optimization_barrier(jnp.mean(resid, axis=-1, keepdims=True))
    spread = lax.optimization_barrier(jnp.mean(center * center, axis=-1, keepdims=True))
    return center * lax.rsqrt(spread + 1e-05) * gain + shift

def group_layer(float_params, block_in, block_len):
    qkv_weight, query_bias, value_bias, out_weight, out_bias, norm1_gain, norm1_shift, up_weight, up_bias, down_weight, down_bias, norm2_gain, norm2_shift = float_params
    group_size, seq_len, model_width = block_in.shape
    rows_in = block_in.reshape(group_size * seq_len, model_width)
    projected = exact_dot(rows_in, qkv_weight)
    query = low(low_back(projected[:, :model_width] + query_bias))
    key_rows = low(low_back(projected[:, model_width:2 * model_width]))
    value_rows = low(low_back(projected[:, 2 * model_width:] + value_bias))
    four_shape = (group_size, seq_len, HEADS, HEAD_DIM)
    raw_scores = jnp.einsum('gqhd,gkhd->ghqk', query.reshape(four_shape), key_rows.reshape(four_shape), precision=lax.Precision.HIGHEST) * HEAD_DIM ** (-0.5)
    scores = low_back(raw_scores)
    valid_key = lax.iota(jnp.int32, seq_len)[None, :] < block_len[:, None]
    masked = jnp.where(valid_key[:, None, None, :], scores, -1e+30)
    weights = low(jax.nn.softmax(masked, axis=-1))
    mixed = jnp.einsum('ghqk,gkhd->gqhd', weights, value_rows.reshape(four_shape), precision=lax.Precision.HIGHEST).reshape(group_size * seq_len, model_width)
    mixed = low(low_back(mixed))
    attn_branch = low_back(exact_dot(mixed, out_weight) + out_bias)
    hidden1 = layer_norm(rows_in + attn_branch, norm1_gain, norm1_shift)
    upper_pre = low_back(exact_dot(low(hidden1), up_weight) + up_bias)
    activated = low(jax.nn.gelu(upper_pre, approximate=False))
    ffn_branch = low_back(exact_dot(activated, down_weight) + down_bias)
    result = layer_norm(hidden1 + ffn_branch, norm2_gain, norm2_shift)
    valid_row = valid_key.reshape(group_size * seq_len, 1)
    square_sums = jnp.stack([jnp.sum(jnp.where(valid_row, rows_in * rows_in, 0.0)), jnp.sum(jnp.where(valid_row, attn_branch * attn_branch, 0.0)), jnp.sum(jnp.where(valid_row, ffn_branch * ffn_branch, 0.0))])
    return (result.reshape(group_size, seq_len, model_width), square_sums)

def reference(tokens, lengths, qkv_weight, query_bias, value_bias, out_weight, out_bias, norm1_gain, norm1_shift, up_weight, up_bias, down_weight, down_bias, norm2_gain, norm2_shift, cotangent):
    model_width = HEADS * HEAD_DIM
    group_size = math.gcd(SEQS, max(1, 4096 // SEQ_LEN))
    group_steps = SEQS // group_size
    stacked_rows = tokens.astype(jnp.float32).reshape(group_steps, group_size, SEQ_LEN, model_width)
    grouped_len = lengths.astype(jnp.int32).reshape(group_steps, group_size)
    float_params = tuple((tensor.astype(jnp.float32) for tensor in (qkv_weight, query_bias, value_bias, out_weight, out_bias, norm1_gain, norm1_shift, up_weight, up_bias, down_weight, down_bias, norm2_gain, norm2_shift)))
    checked_layer = jax.checkpoint(group_layer)

    def forward(layer_rows, *layer_params):

        def one_group(paired):
            return checked_layer(layer_params, paired[0], paired[1])
        result, square_sums = lax.map(one_group, (layer_rows, grouped_len))
        return (result, lax.optimization_barrier(jnp.sum(square_sums, axis=0)))
    primal, pullback, square_sums = jax.vjp(forward, stacked_rows, *float_params, has_aux=True)
    gradients = pullback(cotangent.astype(jnp.float32).reshape(group_steps, group_size, SEQ_LEN, model_width))
    valid_count = jnp.sum(lengths).astype(jnp.float32)
    stream_rms = jnp.sqrt(square_sums / (valid_count * model_width) + 1e-06)
    output = primal.reshape(SEQS, SEQ_LEN, model_width).astype(jnp.bfloat16)
    input_grad = gradients[0].reshape(SEQS, SEQ_LEN, model_width)
    return (output, input_grad, stream_rms, gradients[1], gradients[2], gradients[3], gradients[4], gradients[5], gradients[6], gradients[7], gradients[8], gradients[9], gradients[10], gradients[11], gradients[12], gradients[13])
```

```python
import math

import jax
import jax.numpy as jnp
from jax import lax
from jax.experimental import pallas as pl
from jax.experimental.pallas import tpu as pltpu
from jax.sharding import PartitionSpec as P

HEADS = 12


masked_score = -1e30
norm_eps = 1e-05


def layer_norm(resid, gain, shift):
    center = resid - jnp.mean(resid, axis=-1, keepdims=True)
    spread = jnp.mean(center * center, axis=-1, keepdims=True)
    return center * lax.rsqrt(spread + norm_eps) * gain + shift


def exact_gelu(upper_pre):
    return jax.nn.gelu(upper_pre, approximate=False)


def matmul(left, right):
    return jnp.dot(left, right, preferred_element_type=jnp.float32)


def inner_rows(left, right):
    return lax.dot_general(
        left, right, (((0,), (0,)), ((), ())), preferred_element_type=jnp.float32
    )


def outer_rows(left, right):
    return lax.dot_general(
        left, right, (((1,), (1,)), ((), ())), preferred_element_type=jnp.float32
    )


def head_slice(source, key_start, key_span, head_count):
    piece = lax.dynamic_slice_in_dim(source, key_start, key_span, 0)
    return piece.reshape(key_span, head_count, -1)


def block_scores(query, keys, key_start, key_span, length, score_scale):
    head_count = query.shape[1]
    key_block = head_slice(keys, key_start, key_span, head_count)
    raw_scores = (
        jnp.einsum("qhd,khd->hqk", query, key_block, preferred_element_type=jnp.float32)
        * score_scale
    )
    position = key_start + lax.iota(jnp.int32, key_span)
    return jnp.where((position < length)[None, None, :], raw_scores, masked_score)


def attend_forward(query, keys, values, length, key_span, score_scale):
    query_count, head_count, head_dim = query.shape
    block_count = (length + key_span - 1) // key_span

    def first_sweep(block_index, carry):
        running_max, running_sum = carry
        scores = block_scores(query, keys, block_index * key_span, key_span, length, score_scale)
        new_max = jnp.maximum(running_max, jnp.max(scores, axis=-1))
        running_sum = running_sum * jnp.exp(running_max - new_max) + jnp.sum(
            jnp.exp(scores - new_max[..., None]), axis=-1
        )
        return (new_max, running_sum)

    initial = (
        jnp.full((head_count, query_count), masked_score, jnp.float32),
        jnp.zeros((head_count, query_count), jnp.float32),
    )
    row_peak, row_total = lax.fori_loop(0, block_count, first_sweep, initial)
    log_total = row_peak + jnp.log(row_total)

    def second_sweep(block_index, accumulated):
        key_start = block_index * key_span
        scores = block_scores(query, keys, key_start, key_span, length, score_scale)
        weights = jnp.exp(scores - log_total[..., None]).astype(jnp.bfloat16)
        value_block = head_slice(values, key_start, key_span, head_count)
        return accumulated + jnp.einsum(
            "hqk,khd->qhd", weights, value_block, preferred_element_type=jnp.float32
        )

    mixed_heads = lax.fori_loop(
        0, block_count, second_sweep, jnp.zeros((query_count, head_count, head_dim), jnp.float32)
    )
    return (mixed_heads, log_total)


def attend_backward(
    query, keys, values, grad_mixed, mixed_heads, log_total, length, key_span, score_scale
):
    query_count, head_count, head_dim = query.shape
    seq_len = keys.shape[0]
    block_count = (length + key_span - 1) // key_span
    row_delta = jnp.transpose(jnp.sum(grad_mixed.astype(jnp.float32) * mixed_heads, axis=-1))

    def grad_sweep(block_index, carry):
        grad_query, grad_keys, grad_values = carry
        key_start = block_index * key_span
        scores = block_scores(query, keys, key_start, key_span, length, score_scale)
        block_probs = jnp.exp(scores - log_total[..., None])
        value_block = head_slice(values, key_start, key_span, head_count)
        grad_probs = jnp.einsum(
            "qhd,khd->hqk", grad_mixed, value_block, preferred_element_type=jnp.float32
        )
        grad_scores = (block_probs * (grad_probs - row_delta[..., None])).astype(jnp.bfloat16)
        key_block = head_slice(keys, key_start, key_span, head_count)
        grad_query = grad_query + score_scale * jnp.einsum(
            "hqk,khd->qhd", grad_scores, key_block, preferred_element_type=jnp.float32
        )
        key_part = score_scale * jnp.einsum(
            "hqk,qhd->khd", grad_scores, query, preferred_element_type=jnp.float32
        )
        value_part = jnp.einsum(
            "hqk,qhd->khd",
            block_probs.astype(jnp.bfloat16),
            grad_mixed,
            preferred_element_type=jnp.float32,
        )
        grad_keys = lax.dynamic_update_slice_in_dim(
            grad_keys, key_part.reshape(key_span, head_count * head_dim), key_start, 0
        )
        grad_values = lax.dynamic_update_slice_in_dim(
            grad_values, value_part.reshape(key_span, head_count * head_dim), key_start, 0
        )
        return (grad_query, grad_keys, grad_values)

    initial = (
        jnp.zeros((query_count, head_count, head_dim), jnp.float32),
        jnp.zeros((seq_len, head_count * head_dim), jnp.float32),
        jnp.zeros((seq_len, head_count * head_dim), jnp.float32),
    )
    grad_query, grad_keys, grad_values = lax.fori_loop(0, block_count, grad_sweep, initial)
    return (grad_query.reshape(query_count, head_count * head_dim), grad_keys, grad_values)


def low_precision(value):
    return lax.reduce_precision(value, exponent_bits=8, mantissa_bits=7)


class Links:
    def __init__(self):
        self.dp = lax.axis_size("dp")
        self.ctx = lax.axis_size("ctx")
        self.bits = self.dp.bit_length() - 1
        assert self.dp == 1 << self.bits and self.bits >= 2 and self.ctx % 2 == 0
        self.core = lax.axis_index("ctx") % 2
        self.me = lax.axis_index("dp")
        self.upper = []
        bit = 2
        while bit < self.bits:
            self.upper.append((bit, min(2, self.bits - bit)))
            bit += 2

    def swap(self, value):
        return lax.ppermute(value, "ctx", [(i, i ^ 1) for i in range(self.ctx)])

    def hop(self, value, mask_even, mask_odd):
        pairs = []
        for block in range(self.ctx):
            mask = mask_odd if block % 2 else mask_even
            pairs += [(block * self.dp + i, block * self.dp + (i ^ mask)) for i in range(self.dp)]
        return lax.ppermute(value, ("ctx", "dp"), pairs)

    def places(self, core):
        position = lax.iota(jnp.int32, self.dp)
        quarter = self.dp // 4
        first = (position // quarter) % 2
        second = position // (2 * quarter)
        mask = (position % quarter) * 4 + first * (1 + core) + second * (2 - core)
        return jnp.bitwise_xor(self.me, mask)

    def gather(self, piece):
        held = piece
        for bit, size in self.upper:
            held = jnp.concatenate(
                [held] + [self.hop(held, k << bit, k << bit) for k in range(1, 1 << size)], axis=0
            )
        held = jnp.concatenate([held, self.hop(held, 1, 2)], axis=0)
        return jnp.concatenate([held, self.hop(held, 2, 1)], axis=0)

    def reduce(self, kept, received):
        rows = kept.shape[0]
        terms = [(kept,), (received,)]

        def total(start, span):
            value = None
            for term in terms:
                parts = [
                    lax.slice_in_dim(part, start, start + span, axis=0).astype(jnp.float32)
                    for part in term
                ]
                if value is None:
                    value = parts[0]
                elif len(parts) == 1:
                    value = low_precision(value + parts[0])
                else:
                    value = low_precision((value + parts[0]) + (parts[1] + parts[2]))
            return value.astype(jnp.bfloat16)

        for mask_even, mask_odd in ((2, 1), (1, 2)):
            rows //= 2
            terms.append((self.hop(total(rows, rows), mask_even, mask_odd),))
        for bit, size in reversed(self.upper):
            rows >>= size
            terms.append(
                tuple(
                    self.hop(total(k * rows, rows), k << bit, k << bit) for k in range(1, 1 << size)
                )
            )
        mine = total(0, rows)
        step = 2
        while step < self.ctx:
            pairs = [(i, i ^ step) for i in range(self.ctx)]
            other = lax.ppermute(mine, "ctx", pairs)
            mine = low_precision(mine.astype(jnp.float32) + other.astype(jnp.float32)).astype(
                jnp.bfloat16
            )
            step *= 2
        return mine


def order_table(links):
    return jnp.concatenate(
        [links.places(links.core), links.places(1 - links.core), links.core[None]]
    ).astype(jnp.int32)


def in_vmem(body, name, scalars, sources, out_shapes):
    return pl.pallas_call(
        body,
        name=name,
        out_shape=out_shapes,
        in_specs=[pl.BlockSpec(memory_space=pltpu.SMEM)]
        + [pl.BlockSpec(memory_space=pltpu.VMEM)] * len(sources),
        out_specs=[pl.BlockSpec(memory_space=pltpu.VMEM)] * len(out_shapes),
        compiler_params=pltpu.CompilerParams(vmem_limit_bytes=48 << 20),
    )(scalars, *sources)


def aligned(row, rows):
    return pl.ds(pl.multiple_of(row, 8), rows)


def assemble(links, name, mine, theirs, parts):
    dp = links.dp
    block = mine.shape[0] // dp

    def body(scalar, mine_ref, theirs_ref, *outs):
        def place(core):
            for side, source in enumerate((mine_ref, theirs_ref)):
                half = core if side == 0 else 1 - core

                def one(position, carry):
                    owner = scalar[side * dp + position]
                    for out, (rows, columns, first) in zip(outs, parts):
                        out[aligned(owner * rows, rows), pl.ds(half * columns, columns)] = source[
                            aligned(position * block, rows), pl.ds(first, columns)
                        ]
                    return carry

                lax.fori_loop(0, dp, one, 0)

        for core in range(2):
            pl.when(scalar[2 * dp] == core)(lambda core=core: place(core))

    shapes = [
        jax.ShapeDtypeStruct((dp * rows, 2 * columns), mine.dtype) for rows, columns, _ in parts
    ]
    return in_vmem(body, name, order_table(links), [mine, theirs], shapes)


def split_up(links, name, wholes, parts):
    dp = links.dp
    block = max(rows for rows, _, _ in parts)
    width = max(first + columns for _, columns, first in parts)

    def body(scalar, *refs):
        sources, outs = refs[: len(wholes)], refs[len(wholes) :]

        def place(core):
            for side, out in enumerate(outs):
                half = core if side == 0 else 1 - core

                def one(position, carry):
                    owner = scalar[side * dp + position]
                    for source, (rows, columns, first) in zip(sources, parts):
                        out[aligned(position * block, rows), pl.ds(first, columns)] = source[
                            aligned(owner * rows, rows), pl.ds(half * columns, columns)
                        ].astype(jnp.bfloat16)
                    return carry

                lax.fori_loop(0, dp, one, 0)

        for core in range(2):
            pl.when(scalar[2 * dp] == core)(lambda core=core: place(core))

    shapes = [jax.ShapeDtypeStruct((dp * block, width), jnp.bfloat16)] * 2
    return in_vmem(body, name, order_table(links), wholes, shapes)


def half_columns(links, value):
    span = value.shape[1] // 2
    return lax.dynamic_slice_in_dim(value, links.core * span, span, 1)


def both_halves(links, mine, theirs):
    even = links.core == 0
    return jnp.concatenate(
        [jnp.where(even, mine, theirs), jnp.where(even, theirs, mine)], axis=1
    ).astype(jnp.float32)


def whole_sequence(links, keys, values):
    if links.ctx != 2:
        return tuple(lax.all_gather(v, "ctx", axis=1, tiled=True) for v in (keys, values))
    mine = jnp.concatenate([keys, values], axis=2)
    theirs = links.swap(mine)
    even = links.core == 0
    both = jnp.concatenate(
        [jnp.where(even, mine, theirs), jnp.where(even, theirs, mine)], axis=1
    )
    width = keys.shape[2]
    return both[:, :, :width], both[:, :, width:]


def own_block(links, grad_keys, grad_values):
    grads = jnp.concatenate([grad_keys, grad_values], axis=1).astype(jnp.bfloat16)
    if links.ctx != 2:
        share = lax.psum_scatter(grads, "ctx", scatter_dimension=0, tiled=True)
    else:
        span = grads.shape[0] // 2
        first, second = grads[:span], grads[span:]
        even = links.core == 0
        theirs = links.swap(jnp.where(even, second, first))
        mine = jnp.where(even, first, second)
        share = (mine.astype(jnp.float32) + theirs.astype(jnp.float32)).astype(jnp.bfloat16)
    width = grad_keys.shape[1]
    return share[:, :width], share[:, width:]


def scatter(links, name, wholes, parts):
    kept, sent = split_up(links, name, wholes, parts)
    mine = links.reduce(kept, links.swap(sent))
    theirs = links.swap(mine)
    return [
        both_halves(
            links, mine[:rows, first : first + columns], theirs[:rows, first : first + columns]
        )
        for rows, columns, first in parts
    ]


def shards(
    tokens,
    lengths,
    qkv_weight,
    query_bias,
    value_bias,
    out_weight,
    out_bias,
    norm1_gain,
    norm1_shift,
    up_weight,
    up_bias,
    down_weight,
    down_bias,
    norm2_gain,
    norm2_shift,
    cotangent,
):
    seq_dev, ctx_tok, model_width = tokens.shape
    head_dim = model_width // HEADS
    score_scale = head_dim ** (-0.5)
    seq_len = ctx_tok * lax.axis_size("ctx")
    key_span = math.gcd(seq_len, 512)
    total_rows = seq_dev * ctx_tok
    positions = lax.axis_index("ctx") * ctx_tok + lax.iota(jnp.int32, ctx_tok)
    valid_rows = (positions[None, :] < lengths[:, None]).reshape(total_rows, 1)
    rows_in = tokens.reshape(total_rows, model_width)
    links = Links()
    shard_rows = qkv_weight.shape[0]
    ff_rows = down_weight.shape[0]
    up_columns = ff_rows // shard_rows
    vectors = jnp.stack(
        [query_bias, value_bias, out_bias, norm1_gain, norm1_shift]
        + [down_bias, norm2_gain, norm2_shift]
        + [up_bias[i * shard_rows : (i + 1) * shard_rows] for i in range(up_columns)],
        axis=1,
    )
    vectors = jnp.pad(vectors, ((0, 0), (0, 128 - vectors.shape[1])))
    attn_piece = jnp.concatenate(
        [half_columns(links, qkv_weight), half_columns(links, out_weight), vectors], axis=1
    )
    qkv_half, out_half, up_half, down_half = (
        weight.shape[1] // 2 for weight in (qkv_weight, out_weight, up_weight, down_weight)
    )
    attn_parts = [(shard_rows, qkv_half, 0), (shard_rows, out_half, qkv_half)]
    up_parts = [(shard_rows, up_half, 0)]
    down_parts = [(ff_rows, down_half, 0)]
    attn_mine = links.gather(attn_piece)
    qkv_full, out_full = assemble(
        links, "attn_weights", attn_mine, links.swap(attn_mine), attn_parts
    )
    up_mine = links.gather(half_columns(links, up_weight))
    (up_full,) = assemble(links, "up_weight", up_mine, links.swap(up_mine), up_parts)
    down_mine = links.gather(half_columns(links, down_weight))
    (down_full,) = assemble(links, "down_weight", down_mine, links.swap(down_mine), down_parts)
    order = jnp.argsort(links.places(links.core))
    vector_blocks = attn_mine[:, qkv_half + out_half :].reshape(links.dp, shard_rows, 128)[order]
    vector_rows = jnp.transpose(vector_blocks, (2, 0, 1)).reshape(128, links.dp * shard_rows)
    up_bias_full = jnp.transpose(
        vector_rows[8 : 8 + up_columns].reshape(up_columns, links.dp, shard_rows), (1, 0, 2)
    ).reshape(-1)
    attn_set = (qkv_full, vector_rows[0], vector_rows[1], out_full) + tuple(
        vector_rows[i] for i in (2, 3, 4)
    )
    ffn_set = (up_full, up_bias_full, down_full) + tuple(vector_rows[i] for i in (5, 6, 7))
    projected = matmul(rows_in, attn_set[0])
    query_rows = (projected[:, :model_width] + attn_set[1].astype(jnp.float32)).astype(jnp.bfloat16)
    key_rows = projected[:, model_width : 2 * model_width].astype(jnp.bfloat16)
    value_rows = (projected[:, 2 * model_width :] + attn_set[2].astype(jnp.float32)).astype(
        jnp.bfloat16
    )
    key_local = key_rows.reshape(seq_dev, ctx_tok, model_width)
    value_local = value_rows.reshape(seq_dev, ctx_tok, model_width)
    key_seq, value_seq = whole_sequence(links, key_local, value_local)
    query_seq = query_rows.reshape(seq_dev, ctx_tok, HEADS, head_dim)
    member = 0
    mixed_heads, log_total = attend_forward(
        query_seq[member],
        key_seq[member],
        value_seq[member],
        lengths[member],
        key_span,
        score_scale,
    )
    head_parts = [mixed_heads]
    mixed_parts = mixed_heads.reshape(ctx_tok, model_width)
    log_parts = [log_total]
    mixed_rows = mixed_parts.astype(jnp.bfloat16)
    attn_branch = matmul(mixed_rows, attn_set[3]) + attn_set[4].astype(jnp.float32)
    input_float = rows_in.astype(jnp.float32)
    resid1 = input_float + attn_branch
    hidden1 = layer_norm(resid1, attn_set[5].astype(jnp.float32), attn_set[6].astype(jnp.float32))
    hidden_low = hidden1.astype(jnp.bfloat16)
    upper_pre = matmul(hidden_low, ffn_set[0]) + ffn_set[1].astype(jnp.float32)
    activated = exact_gelu(upper_pre).astype(jnp.bfloat16)
    ffn_branch = matmul(activated, ffn_set[2]) + ffn_set[3].astype(jnp.float32)
    resid2 = hidden1 + ffn_branch
    output = layer_norm(
        resid2, ffn_set[4].astype(jnp.float32), ffn_set[5].astype(jnp.float32)
    ).astype(jnp.bfloat16)
    totals = (
        jnp.sum(jnp.where(valid_rows, input_float * input_float, 0.0)),
        jnp.sum(jnp.where(valid_rows, attn_branch * attn_branch, 0.0)),
        jnp.sum(jnp.where(valid_rows, ffn_branch * ffn_branch, 0.0)),
        jnp.sum(valid_rows.astype(jnp.float32)),
    )
    back_attn, back_ffn = attn_set, ffn_set
    grad_rows = cotangent.reshape(total_rows, model_width).astype(jnp.float32)
    _, norm2_back = jax.vjp(
        layer_norm, resid2, back_ffn[4].astype(jnp.float32), back_ffn[5].astype(jnp.float32)
    )
    grad_resid2, grad_gain2, grad_shift2 = norm2_back(grad_rows)
    grad_ffn = grad_resid2.astype(jnp.bfloat16)
    grad_down = inner_rows(activated, grad_ffn)
    grad_down_bias = jnp.sum(grad_ffn, axis=0, dtype=jnp.float32)
    _, gelu_back = jax.vjp(exact_gelu, upper_pre)
    grad_upper = gelu_back(outer_rows(grad_ffn, back_ffn[2]))[0].astype(jnp.bfloat16)
    grad_up = inner_rows(hidden_low, grad_upper)
    grad_up_bias = jnp.sum(grad_upper, axis=0, dtype=jnp.float32)
    grad_hidden1 = grad_resid2 + outer_rows(grad_upper, back_ffn[0])
    up_grad = scatter(links, "up_grad", [grad_up.astype(jnp.bfloat16)], up_parts)
    down_grad = scatter(links, "down_grad", [grad_down.astype(jnp.bfloat16)], down_parts)
    _, norm1_back = jax.vjp(
        layer_norm, resid1, back_attn[5].astype(jnp.float32), back_attn[6].astype(jnp.float32)
    )
    grad_resid1, grad_gain1, grad_shift1 = norm1_back(grad_hidden1)
    grad_attn = grad_resid1.astype(jnp.bfloat16)
    grad_out = inner_rows(mixed_rows, grad_attn)
    grad_out_bias = jnp.sum(grad_attn, axis=0, dtype=jnp.float32)
    grad_mixed = (
        outer_rows(grad_attn, back_attn[3])
        .astype(jnp.bfloat16)
        .reshape(seq_dev, ctx_tok, HEADS, head_dim)
    )
    back_keys, back_values = (key_seq, value_seq)
    member = 0
    grad_query, grad_keys, grad_values = attend_backward(
        query_seq[member],
        back_keys[member],
        back_values[member],
        grad_mixed[member],
        head_parts[member],
        log_parts[member],
        lengths[member],
        key_span,
        score_scale,
    )
    key_share, value_share = own_block(links, grad_keys, grad_values)
    query_grads = grad_query.astype(jnp.bfloat16)
    grad_qkv_rows = jnp.concatenate([query_grads, key_share, value_share], axis=1)
    grad_qkv = inner_rows(rows_in, grad_qkv_rows)
    grad_query_bias = jnp.sum(grad_qkv_rows[:, :model_width], axis=0, dtype=jnp.float32)
    grad_value_bias = jnp.sum(grad_qkv_rows[:, 2 * model_width :], axis=0, dtype=jnp.float32)
    input_grad = grad_resid1 + outer_rows(grad_qkv_rows, back_attn[0])
    vector_grads = jnp.stack(
        [grad_query_bias, grad_value_bias, grad_out_bias, grad_gain1, grad_shift1]
        + [grad_down_bias, grad_gain2, grad_shift2]
    )
    up_bias_rows = jnp.transpose(
        grad_up_bias.reshape(links.dp, up_columns, shard_rows), (1, 0, 2)
    ).reshape(up_columns, model_width)
    total_rows_4 = jnp.broadcast_to(jnp.stack(totals)[:, None], (4, model_width))
    vector_grads = jnp.concatenate([vector_grads, up_bias_rows, total_rows_4])
    vector_grads = jnp.pad(vector_grads, ((0, 128 - vector_grads.shape[0]), (0, 0)))
    vector_grads = jnp.transpose(vector_grads).astype(jnp.bfloat16)
    vector_grads = jnp.concatenate([vector_grads, vector_grads], axis=1)
    attn_grad = scatter(
        links,
        "attn_grad",
        [grad_qkv.astype(jnp.bfloat16), grad_out.astype(jnp.bfloat16), vector_grads],
        attn_parts + [(shard_rows, 128, qkv_half + out_half)],
    )
    vector_sums = jnp.transpose(attn_grad[2][:, :128])
    stream_sums = vector_sums[8 + up_columns : 12 + up_columns, 0]
    stream_rms = jnp.sqrt(stream_sums[:3] / (stream_sums[3] * model_width) + 1e-06)
    return (
        output.reshape(seq_dev, ctx_tok, model_width),
        input_grad.reshape(seq_dev, ctx_tok, model_width),
        stream_rms,
        attn_grad[0],
        vector_sums[0],
        vector_sums[1],
        attn_grad[1],
        vector_sums[2],
        vector_sums[3],
        vector_sums[4],
        up_grad[0],
        vector_sums[8 : 8 + up_columns].reshape(-1),
        down_grad[0],
        vector_sums[5],
        vector_sums[6],
        vector_sums[7],
    )


def solution(mesh):
    in_specs = (
        P("dp", "ctx", None),
        P("dp"),
        P("dp", None),
        P("dp"),
        P("dp"),
        P("dp", None),
        P("dp"),
        P("dp"),
        P("dp"),
        P("dp", None),
        P("dp"),
        P("dp", None),
        P("dp"),
        P("dp"),
        P("dp"),
        P("dp", "ctx", None),
    )
    out_specs = (
        P("dp", "ctx", None),
        P("dp", "ctx", None),
        P(),
        P("dp", None),
        P("dp"),
        P("dp"),
        P("dp", None),
        P("dp"),
        P("dp"),
        P("dp"),
        P("dp", None),
        P("dp"),
        P("dp", None),
        P("dp"),
        P("dp"),
        P("dp"),
    )
    return jax.shard_map(shards, mesh=mesh, in_specs=in_specs, out_specs=out_specs, check_vma=False)
```

```python
import math

import jax
import jax.numpy as jnp
from jax import lax
from jax.experimental import pallas as pl
from jax.experimental.pallas import tpu as pltpu
from jax.sharding import PartitionSpec as P

HEADS = 12
LANES = 128
VECTORS = 16

masked_score = -1e30
norm_eps = 1e-05
f32 = jnp.float32
bf16 = jnp.bfloat16


def low_precision(value):
    return lax.reduce_precision(value, exponent_bits=8, mantissa_bits=7)


class Links:
    def __init__(self):
        self.dp = lax.axis_size("dp")
        self.ctx = lax.axis_size("ctx")
        self.bits = self.dp.bit_length() - 1
        assert self.dp == 1 << self.bits and self.bits >= 2 and self.ctx % 2 == 0
        self.core = lax.axis_index("ctx") % 2
        self.me = lax.axis_index("dp")
        self.upper = []
        bit = 2
        while bit < self.bits:
            self.upper.append((bit, min(2, self.bits - bit)))
            bit += 2

    def swap(self, value):
        return lax.ppermute(value, "ctx", [(i, i ^ 1) for i in range(self.ctx)])

    def hop(self, value, mask_even, mask_odd):
        pairs = []
        for block in range(self.ctx):
            mask = mask_odd if block % 2 else mask_even
            pairs += [(block * self.dp + i, block * self.dp + (i ^ mask)) for i in range(self.dp)]
        return lax.ppermute(value, ("ctx", "dp"), pairs)

    def places(self, core):
        position = lax.iota(jnp.int32, self.dp)
        quarter = self.dp // 4
        first = (position // quarter) % 2
        second = position // (2 * quarter)
        mask = (position % quarter) * 4 + first * (1 + core) + second * (2 - core)
        return jnp.bitwise_xor(self.me, mask)

    def spots(self, core):
        mask = jnp.bitwise_xor(self.me, lax.iota(jnp.int32, self.dp))
        low, high = mask % 2, (mask // 2) % 2
        first = jnp.where(core == 0, low, high)
        second = jnp.where(core == 0, high, low)
        quarter = self.dp // 4
        return mask // 4 + first * quarter + second * (2 * quarter)

    def table(self, *more):
        parts = [self.places(self.core), self.places(1 - self.core)]
        parts += [self.spots(self.core), self.spots(1 - self.core)]
        parts += [jnp.reshape(value, (1,)) for value in (self.core,) + more]
        return jnp.concatenate(parts).astype(jnp.int32)

    def gather(self, piece):
        held = piece
        for bit, size in self.upper:
            held = jnp.concatenate(
                [held] + [self.hop(held, k << bit, k << bit) for k in range(1, 1 << size)], axis=0
            )
        held = jnp.concatenate([held, self.hop(held, 1, 2)], axis=0)
        return jnp.concatenate([held, self.hop(held, 2, 1)], axis=0)

    def reduce(self, kept, received):
        rows = kept.shape[0]
        terms = [(kept,), (received,)]

        def total(start, span):
            value = None
            for term in terms:
                parts = [
                    lax.slice_in_dim(part, start, start + span, axis=0).astype(f32)
                    for part in term
                ]
                if value is None:
                    value = parts[0]
                elif len(parts) == 1:
                    value = low_precision(value + parts[0])
                else:
                    value = low_precision((value + parts[0]) + (parts[1] + parts[2]))
            return value.astype(bf16)

        for mask_even, mask_odd in ((2, 1), (1, 2)):
            rows //= 2
            terms.append((self.hop(total(rows, rows), mask_even, mask_odd),))
        for bit, size in reversed(self.upper):
            rows >>= size
            terms.append(
                tuple(
                    self.hop(total(k * rows, rows), k << bit, k << bit) for k in range(1, 1 << size)
                )
            )
        mine = total(0, rows)
        step = 2
        while step < self.ctx:
            pairs = [(i, i ^ step) for i in range(self.ctx)]
            other = lax.ppermute(mine, "ctx", pairs)
            mine = low_precision(mine.astype(f32) + other.astype(f32)).astype(bf16)
            step *= 2
        return mine


def half_columns(links, value):
    span = value.shape[1] // 2
    return lax.dynamic_slice_in_dim(value, links.core * span, span, 1)


def both_halves(links, mine, theirs):
    even = links.core == 0
    return jnp.concatenate(
        [jnp.where(even, mine, theirs), jnp.where(even, theirs, mine)], axis=1
    ).astype(f32)


def dot(left, right):
    return jnp.dot(left, right, preferred_element_type=f32)


def dot_rows(left, right):
    return lax.dot_general(left, right, (((1,), (1,)), ((), ())), preferred_element_type=f32)


def turned(value):
    return jnp.transpose(value)


def aligned(start, size, unit):
    return pl.ds(pl.multiple_of(start, unit), size)


SMEM = pl.BlockSpec(memory_space=pltpu.SMEM)
ANY = pl.BlockSpec(memory_space=pl.ANY)
VMEM = pl.BlockSpec(memory_space=pltpu.VMEM)


def call(body, name, sources, in_specs, outs, scratch=(), cost=None):
    return pl.pallas_call(
        body,
        name=name,
        out_shape=outs,
        in_specs=in_specs,
        out_specs=[VMEM] * len(outs),
        scratch_shapes=list(scratch),
        compiler_params=pltpu.CompilerParams(vmem_limit_bytes=56 << 20),
        cost_estimate=cost,
    )(*sources)


def shape(rows, columns, dtype):
    return jax.ShapeDtypeStruct((rows, columns), dtype)


class Piece:
    def __init__(self, dp, rows, columns, first):
        self.dp, self.rows, self.columns, self.first = dp, rows, columns, first

    def fetch(self, scalar, sides, whole, sem):
        core = scalar[4 * self.dp]
        for side, source in enumerate(sides):
            half = core if side == 0 else 1 - core

            def one(position, carry, side=side, source=source, half=half):
                owner = scalar[side * self.dp + position]
                pltpu.make_async_copy(
                    source.at[
                        aligned(position * self.rows, self.rows, 8),
                        pl.ds(self.first, self.columns),
                    ],
                    whole.at[
                        aligned(owner * self.rows, self.rows, 8),
                        aligned(half * self.columns, self.columns, LANES),
                    ],
                    sem,
                ).start()
                return carry

            lax.fori_loop(0, self.dp, one, 0)

    def ready(self, whole, sem):
        pltpu.make_async_copy(whole, whole, sem).wait()

    def whole(self):
        return pltpu.VMEM((self.dp * self.rows, 2 * self.columns), bf16)


def spread(scalar, dp, side, tile, out, rows, columns, tile_columns, base):
    count = tile.shape[0] // rows

    def one(i, carry):
        spot = scalar[(2 + side) * dp + base + i]
        out[aligned(spot * rows, rows, 8), columns] = tile[
            aligned(i * rows, rows, 8), tile_columns
        ].astype(bf16)
        return carry

    lax.fori_loop(0, count, one, 0)


def project(links, table, rows, mine, theirs, qkv_piece, vector_piece, scale):
    tokens, width = rows.shape

    def body(scalar, rows_ref, mine_ref, theirs_ref, q_ref, kv_ref, vec_ref, weight, vecs, sems):
        qkv_piece.fetch(scalar, (mine_ref, theirs_ref), weight, sems.at[0])
        core = scalar[4 * links.dp]

        def one(position, carry):
            owner = scalar[position]
            pltpu.make_async_copy(
                mine_ref.at[
                    aligned(position * vector_piece.rows, vector_piece.rows, 8),
                    pl.ds(vector_piece.first, LANES),
                ],
                vecs.at[aligned(owner * vector_piece.rows, vector_piece.rows, 8), :],
                sems.at[1],
            ).start()
            return carry

        lax.fori_loop(0, links.dp, one, 0)
        pltpu.make_async_copy(vecs, vecs, sems.at[1]).wait()
        vectors = turned(vecs[...].astype(f32))[:VECTORS]
        vec_ref[...] = vectors
        qkv_piece.ready(weight, sems.at[0])
        x = rows_ref[...]
        query = (dot(x, weight[:, :width]) + vectors[0:1]).astype(bf16)
        q_ref[...] = (query.astype(f32) * scale).astype(bf16)
        kv_ref[:, :width] = dot(x, weight[:, width : 2 * width]).astype(bf16)
        kv_ref[:, width:] = (dot(x, weight[:, 2 * width :]) + vectors[1:2]).astype(bf16)

    return call(
        body,
        "qkv",
        [table, rows, mine, theirs],
        [SMEM, VMEM, ANY, ANY],
        [shape(tokens, width, bf16), shape(tokens, 2 * width, bf16), shape(VECTORS, width, f32)],
        [qkv_piece.whole(), pltpu.VMEM((width, LANES), bf16), pltpu.SemaphoreType.DMA((2,))],
    )


def pair_specs(parts, pairs):
    specs = []
    for part in parts:
        rows = part.shape[0]
        specs.append(pl.BlockSpec((rows, LANES), lambda p, s: (0, p)))
        specs.append(pl.BlockSpec((rows, LANES), lambda p, s, pairs=pairs: (0, pairs + p)))
    return specs


def first_lanes(shape_, count):
    return (lax.broadcasted_iota(jnp.int32, shape_, 1) < count).astype(f32).astype(bf16)


def head_blocks(query):
    lane = lax.broadcasted_iota(jnp.int32, query.shape, 1)
    zero = jnp.zeros_like(query)
    half = LANES // 2
    return jnp.concatenate(
        [jnp.where(lane < half, query, zero), jnp.where(lane >= half, query, zero)], axis=0
    )


def attend(query, parts, starts, length):
    tokens, width = query.shape
    pairs = width // LANES
    span = sum(part.shape[0] for part in parts)
    half = LANES // 2
    chunk = min(256, tokens)
    scalars = jnp.concatenate(
        [jnp.reshape(v, (1,)).astype(jnp.int32) for v in [length, *starts]]
    )

    def body(scalar, q_ref, *refs):
        kv_refs = refs[: 2 * len(parts)]
        mixed_t_ref, mixed_ref, p_ref, inverse_ref, bias = refs[2 * len(parts) :]

        @pl.when(pl.program_id(0) == 0)
        def _():
            at = 0
            for i, part in enumerate(parts):
                rows = part.shape[0]
                position = scalar[1 + i] + lax.broadcasted_iota(jnp.int32, (rows, LANES), 0)
                lane = lax.broadcasted_iota(jnp.int32, (rows, LANES), 1)
                hidden = jnp.where(position < scalar[0], 0.0, masked_score)
                bias[at : at + rows, :] = jnp.where(lane == 0, hidden, 0.0).astype(bf16)
                at += rows

        keys = jnp.concatenate([ref[...] for ref in kv_refs[0::2]], axis=0)
        values = jnp.concatenate([ref[...] for ref in kv_refs[1::2]], axis=0)
        keys = jnp.concatenate([keys, bias[...]], axis=1)
        values_t = jnp.concatenate([turned(values), jnp.ones((16, span), bf16)], axis=0)
        queries = head_blocks(q_ref[...])
        queries = jnp.concatenate([queries, first_lanes(queries.shape, 1)], axis=1)
        for at in range(0, 2 * tokens, chunk):
            scores = dot_rows(keys, queries[at : at + chunk])
            peak = jnp.max(scores, axis=0, keepdims=True)
            weights = jnp.exp(scores - peak).astype(bf16)
            p_ref[:, at : at + chunk] = weights
            sums = dot(values_t, weights)
            inverse = 1.0 / sums[LANES : LANES + 1]
            inverse_ref[:, at : at + chunk] = inverse
            low = 0 if at < tokens else half
            to = at % tokens
            mixed_t_ref[low : low + half, to : to + chunk] = sums[low : low + half] * inverse
        mixed_ref[...] = turned(mixed_t_ref[...]).astype(bf16)

    sources = [query]
    for part in parts:
        sources += [part, part]
    return pl.pallas_call(
        body,
        name="attend",
        out_shape=[
            shape(width, tokens, f32),
            shape(tokens, width, bf16),
            jax.ShapeDtypeStruct((pairs, span, 2 * tokens), bf16),
            jax.ShapeDtypeStruct((pairs, 1, 2 * tokens), f32),
        ],
        grid_spec=pltpu.PrefetchScalarGridSpec(
            num_scalar_prefetch=1,
            grid=(pairs,),
            in_specs=[pl.BlockSpec((tokens, LANES), lambda p, s: (0, p))]
            + pair_specs(parts, pairs),
            out_specs=[
                pl.BlockSpec((LANES, tokens), lambda p, s: (p, 0)),
                pl.BlockSpec((tokens, LANES), lambda p, s: (0, p)),
                pl.BlockSpec((None, span, 2 * tokens), lambda p, s: (p, 0, 0)),
                pl.BlockSpec((None, 1, 2 * tokens), lambda p, s: (p, 0, 0)),
            ],
            scratch_shapes=[pltpu.VMEM((span, LANES), bf16)],
        ),
        compiler_params=pltpu.CompilerParams(vmem_limit_bytes=56 << 20),
    )(scalars, *sources)


def attend_back(query, parts, grad_mixed, mixed_t, weights, inverse, scale):
    tokens, width = query.shape
    pairs = width // LANES
    span = sum(part.shape[0] for part in parts)
    half = LANES // 2
    chunk = min(256, tokens)

    def body(_, q_ref, gm_ref, mt_ref, p_ref, inv_ref, *refs):
        kv_refs = refs[: 2 * len(parts)]
        dq_ref = refs[2 * len(parts)]
        dkv_refs = refs[2 * len(parts) + 1 : -1]
        ds_ref = refs[-1]
        keys = jnp.concatenate([ref[...] for ref in kv_refs[0::2]], axis=0)
        values = jnp.concatenate([ref[...] for ref in kv_refs[1::2]], axis=0)
        grads = turned(gm_ref[...].astype(f32))
        inv = inv_ref[...]
        product = grads * mt_ref[...]
        empty = jnp.zeros((half, tokens), bf16)
        even, odd = inv[:, :tokens], inv[:, tokens:]
        delta = jnp.concatenate(
            [
                jnp.sum(product[:half], axis=0, keepdims=True) * even,
                jnp.sum(product[half:], axis=0, keepdims=True) * odd,
            ],
            axis=1,
        )
        top = jnp.concatenate([(grads[:half] * even).astype(bf16), empty], axis=1)
        bottom = jnp.concatenate([empty, (grads[half:] * odd).astype(bf16)], axis=1)
        scaled = jnp.concatenate([top, bottom], axis=0)
        first = (-delta).astype(bf16).astype(f32)
        second = (-delta - first).astype(bf16).astype(f32)
        third = (-delta - first - second).astype(bf16).astype(f32)
        row = lax.broadcasted_iota(jnp.int32, (LANES, 2 * tokens), 0)
        limbs = jnp.where(
            row == 0, first, jnp.where(row == 1, second, jnp.where(row == 2, third, 0.0))
        ).astype(bf16)
        right = jnp.concatenate([scaled, limbs], axis=0)
        left = jnp.concatenate([values, first_lanes(values.shape, 3)], axis=1)
        for at in range(0, 2 * tokens, chunk):
            grad_probs = dot(left, right[:, at : at + chunk])
            ds_ref[:, at : at + chunk] = (
                p_ref[:, at : at + chunk].astype(f32) * grad_probs
            ).astype(bf16)
        grad_scores = ds_ref[...]
        turned_grad = dot(turned(keys), grad_scores)
        dq_ref[...] = (
            turned(
                jnp.concatenate([turned_grad[:half, :tokens], turned_grad[half:, tokens:]], axis=0)
            )
            * scale
        ).astype(bf16)
        grad_keys = dot(grad_scores, head_blocks(q_ref[...])).astype(bf16)
        grad_values = dot_rows(p_ref[...], scaled).astype(bf16)
        at = 0
        for i, part in enumerate(parts):
            rows = part.shape[0]
            dkv_refs[2 * i][...] = grad_keys[at : at + rows]
            dkv_refs[2 * i + 1][...] = grad_values[at : at + rows]
            at += rows

    sources = [query, grad_mixed, mixed_t, weights, inverse]
    out_shapes = [shape(tokens, width, bf16)]
    columns = lambda p, s: (0, p)
    out_specs = [pl.BlockSpec((tokens, LANES), columns)]
    for part in parts:
        sources += [part, part]
        rows = part.shape[0]
        out_shapes += [shape(rows, width, bf16)] * 2
        out_specs += [pl.BlockSpec((rows, LANES), columns)] * 2
    return pl.pallas_call(
        body,
        name="attend_back",
        out_shape=out_shapes,
        grid_spec=pltpu.PrefetchScalarGridSpec(
            num_scalar_prefetch=1,
            grid=(pairs,),
            in_specs=[
                pl.BlockSpec((tokens, LANES), columns),
                pl.BlockSpec((tokens, LANES), columns),
                pl.BlockSpec((LANES, tokens), lambda p, s: (p, 0)),
                pl.BlockSpec((None, span, 2 * tokens), lambda p, s: (p, 0, 0)),
                pl.BlockSpec((None, 1, 2 * tokens), lambda p, s: (p, 0, 0)),
            ]
            + pair_specs(parts, pairs),
            out_specs=out_specs,
            scratch_shapes=[pltpu.VMEM((span, 2 * tokens), bf16)],
        ),
        compiler_params=pltpu.CompilerParams(vmem_limit_bytes=56 << 20),
    )(jnp.zeros((1,), jnp.int32), *sources)


def normalize(resid):
    center = resid - jnp.mean(resid, axis=1, keepdims=True)
    inverse = lax.rsqrt(jnp.mean(center * center, axis=1, keepdims=True) + norm_eps)
    return center * inverse, inverse


def norm_back(grads, normal, inverse, gain):
    scaled = grads * gain
    return inverse * (
        scaled
        - jnp.mean(scaled, axis=1, keepdims=True)
        - normal * jnp.mean(scaled * normal, axis=1, keepdims=True)
    )


def column_sums(value):
    return jnp.sum(value, axis=0, keepdims=True)


def masked_total(value, valid, width):
    lanes = column_sums(jnp.where(valid, value * value, 0.0))
    return jnp.broadcast_to(jnp.sum(lanes, axis=1, keepdims=True), (1, width))


def valid_rows(scalar, at, tokens):
    position = scalar[at + 1] + lax.broadcasted_iota(jnp.int32, (tokens, 1), 0)
    return position < scalar[at]


def after_attention(links, table, rows, mixed, vectors, mine, theirs, out_piece):
    tokens, width = rows.shape
    extra = 4 * links.dp + 1

    def body(scalar, rows_ref, mixed_ref, vec_ref, mine_ref, theirs_ref, *refs):
        hidden_ref, low_ref, normal_ref, inverse_ref, sums_ref, weight, sem = refs
        out_piece.fetch(scalar, (mine_ref, theirs_ref), weight, sem.at[0])
        x = rows_ref[...].astype(f32)
        valid = valid_rows(scalar, extra, tokens)
        sums_ref[0:1, :] = masked_total(x, valid, width)
        count = jnp.sum(valid.astype(f32), axis=0, keepdims=True)
        sums_ref[2:3, :] = jnp.broadcast_to(count, (1, width))
        out_piece.ready(weight, sem.at[0])
        branch = dot(mixed_ref[...], weight[...]) + vec_ref[2:3]
        sums_ref[1:2, :] = masked_total(branch, valid, width)
        normal, inverse = normalize(x + branch)
        hidden = normal * vec_ref[3:4] + vec_ref[4:5]
        normal_ref[...] = normal
        inverse_ref[...] = inverse
        hidden_ref[...] = hidden
        low_ref[...] = hidden.astype(bf16)

    return call(
        body,
        "after_attention",
        [table, rows, mixed, vectors, mine, theirs],
        [SMEM, VMEM, VMEM, VMEM, ANY, ANY],
        [
            shape(tokens, width, f32),
            shape(tokens, width, bf16),
            shape(tokens, width, f32),
            shape(tokens, 1, f32),
            shape(3, width, f32),
        ],
        [out_piece.whole(), pltpu.SemaphoreType.DMA((1,))],
    )


def gelu_and_slope(u):
    size = jnp.abs(u)
    t = 1.0 / (1.0 + (0.3275911 * math.sqrt(0.5)) * size)
    bell = jnp.exp(-0.5 * (u * u))
    series = 0.5 * 1.061405429 * t - 0.5 * 1.453152027
    series = series * t + 0.5 * 1.421413741
    series = series * t - 0.5 * 0.284496736
    series = series * t + 0.5 * 0.254829592
    tail = series * t * bell
    phi = jnp.where(u < 0.0, tail, 1.0 - tail)
    return u * phi, phi + u * bell * (1.0 / math.sqrt(2.0 * math.pi))


def feed_forward(links, table, hidden, low, vectors, up_bias, cotangent, up, down, pieces):
    tokens, width = hidden.shape
    up_piece, down_piece = pieces
    inner = up_bias.shape[1]
    block = width
    extra = 4 * links.dp + 1
    dp = links.dp

    def body(scalar, hidden_ref, low_ref, vec_ref, bias_ref, cot_ref, um, ut, dm, dt, *refs):
        out_ref, slope_ref, resid_ref, grad_ref, keep_ref, send_ref, sums_ref = refs[:7]
        up_w, down_w, act, total, tile, sems = refs[7:]
        up_piece.fetch(scalar, (um, ut), up_w, sems.at[0])
        down_piece.fetch(scalar, (dm, dt), down_w, sems.at[1])
        up_piece.ready(up_w, sems.at[0])
        down_piece.ready(down_w, sems.at[1])
        total[...] = jnp.zeros_like(total)

        def forward(j, carry):
            at = aligned(j * block, block, LANES)
            u = dot(low_ref[...], up_w[:, at]) + bias_ref[:, at]
            value, slope = gelu_and_slope(u)
            value = value.astype(bf16)
            act[:, at] = value
            slope_ref[:, at] = slope.astype(bf16)
            total[...] += dot(value, down_w[at, :])
            return carry

        lax.fori_loop(0, inner // block, forward, 0)
        branch = total[...] + vec_ref[5:6]
        sums_ref[3:4, :] = masked_total(branch, valid_rows(scalar, extra, tokens), width)
        normal, inverse = normalize(hidden_ref[...] + branch)
        out_ref[...] = (normal * vec_ref[6:7] + vec_ref[7:8]).astype(bf16)
        grads = cot_ref[...].astype(f32)
        sums_ref[1:2, :] = column_sums(grads * normal)
        sums_ref[2:3, :] = column_sums(grads)
        resid = norm_back(grads, normal, inverse, vec_ref[6:7])
        resid_ref[...] = resid
        grad_ffn = resid.astype(bf16)
        grad_ref[...] = grad_ffn
        sums_ref[0:1, :] = column_sums(grad_ffn.astype(f32))
        core = scalar[4 * dp]

        def backward(j, carry):
            at = aligned(j * block, block, LANES)
            tile[...] = dot(turned(act[:, at]), grad_ref[...])
            for side, out in enumerate((keep_ref, send_ref)):
                half = core if side == 0 else 1 - core
                spread(
                    scalar,
                    dp,
                    side,
                    tile,
                    out,
                    down_piece.rows,
                    slice(None),
                    aligned(half * down_piece.columns, down_piece.columns, LANES),
                    j * (block // down_piece.rows),
                )
            return carry

        lax.fori_loop(0, inner // block, backward, 0)

    return call(
        body,
        "feed_forward",
        [table, hidden, low, vectors, up_bias, cotangent, *up, *down],
        [SMEM] + [VMEM] * 5 + [ANY] * 4,
        [
            shape(tokens, width, bf16),
            shape(tokens, inner, bf16),
            shape(tokens, width, f32),
            shape(tokens, width, bf16),
            shape(inner, width // 2, bf16),
            shape(inner, width // 2, bf16),
            shape(4, width, f32),
        ],
        [
            up_piece.whole(),
            down_piece.whole(),
            pltpu.VMEM((tokens, inner), bf16),
            pltpu.VMEM((tokens, width), f32),
            pltpu.VMEM((block, width), f32),
            pltpu.SemaphoreType.DMA((2,)),
        ],
    )


def feed_back(links, table, low, slope, resid, grad_ffn, up, down, pieces):
    tokens, width = resid.shape
    up_piece, down_piece = pieces
    inner = slope.shape[1]
    span = inner // 2
    block = width if span % width == 0 else span
    dp = links.dp

    def body(scalar, low_ref, slope_ref, resid_ref, grad_ref, um, ut, dm, dt, *refs):
        hidden_ref, keep_ref, send_ref, bias_ref, up_w, down_w, low_t, tile, sems = refs
        up_piece.fetch(scalar, (um, ut), up_w, sems.at[0])
        down_piece.fetch(scalar, (dm, dt), down_w, sems.at[1])
        low_t[...] = turned(low_ref[...])
        hidden_ref[...] = resid_ref[...]
        up_piece.ready(up_w, sems.at[0])
        down_piece.ready(down_w, sems.at[1])
        core = scalar[4 * dp]
        for side, out in enumerate((keep_ref, send_ref)):
            half = core if side == 0 else 1 - core

            def backward(j, carry, side=side, out=out, half=half):
                at = aligned(half * span + j * block, block, LANES)
                grads = dot_rows(grad_ref[...], down_w[at, :]) * slope_ref[:, at].astype(f32)
                grads = grads.astype(bf16)
                bias_ref[:, at] = column_sums(grads.astype(f32))
                hidden_ref[...] += dot_rows(grads, up_w[:, at])
                tile[...] = dot(low_t[...], grads)
                spread(
                    scalar,
                    dp,
                    side,
                    tile,
                    out,
                    up_piece.rows,
                    aligned(j * block, block, LANES),
                    slice(None),
                    0,
                )
                return carry

            lax.fori_loop(0, span // block, backward, 0)

    return call(
        body,
        "feed_back",
        [table, low, slope, resid, grad_ffn, *up, *down],
        [SMEM] + [VMEM] * 4 + [ANY] * 4,
        [
            shape(tokens, width, f32),
            shape(width, span, bf16),
            shape(width, span, bf16),
            shape(1, inner, f32),
        ],
        [
            up_piece.whole(),
            down_piece.whole(),
            pltpu.VMEM((width, tokens), bf16),
            pltpu.VMEM((width, block), f32),
            pltpu.SemaphoreType.DMA((2,)),
        ],
    )


def before_attention(links, table, grad_hidden, normal, inverse, mixed, vectors, attn, piece):
    tokens, width = normal.shape

    def body(scalar, grad_ref, normal_ref, inverse_ref, mixed_ref, vec_ref, mine, theirs, *refs):
        resid_ref, gm_ref, out_ref, sums_ref, weight, sem = refs
        piece.fetch(scalar, (mine, theirs), weight, sem.at[0])
        grads = grad_ref[...]
        normal_ = normal_ref[...]
        sums_ref[1:2, :] = column_sums(grads * normal_)
        sums_ref[2:3, :] = column_sums(grads)
        resid = norm_back(grads, normal_, inverse_ref[...], vec_ref[3:4])
        resid_ref[...] = resid
        grad_attn = resid.astype(bf16)
        sums_ref[0:1, :] = column_sums(grad_attn.astype(f32))
        piece.ready(weight, sem.at[0])
        gm_ref[...] = dot_rows(grad_attn, weight[...]).astype(bf16)
        out_ref[...] = dot(turned(mixed_ref[...]), grad_attn).astype(bf16)

    return call(
        body,
        "before_attention",
        [table, grad_hidden, normal, inverse, mixed, vectors, *attn],
        [SMEM] + [VMEM] * 5 + [ANY] * 2,
        [
            shape(tokens, width, f32),
            shape(tokens, width, bf16),
            shape(width, width, bf16),
            shape(3, width, f32),
        ],
        [piece.whole(), pltpu.SemaphoreType.DMA((1,))],
    )


def qkv_gradient(links, table, rows, query_grad, mine, theirs, out_grad, vectors, pieces):
    tokens, width = rows.shape
    qkv_piece, out_piece, vector_piece = pieces
    dp = links.dp
    count = 2 if theirs else 1
    total = qkv_piece.columns + out_piece.columns + LANES

    def body(scalar, rows_ref, dq_ref, *refs):
        share_refs = refs[: 2 * count]
        out_ref, vec_ref, grads_ref, keep_ref, send_ref, tile, vec_tile = refs[2 * count :]
        grads_ref[:, :width] = dq_ref[...]
        for i in range(2):
            share = share_refs[i][...]
            if count == 2:
                share = (share.astype(f32) + share_refs[2 + i][...].astype(f32)).astype(bf16)
            grads_ref[:, (1 + i) * width : (2 + i) * width] = share
        rows_t = turned(rows_ref[...])
        for i in range(3):
            at = slice(i * width, (i + 1) * width)
            tile[:, at] = dot(rows_t, grads_ref[:, at]).astype(bf16)
        sums = vec_ref[...]
        query_sum = column_sums(grads_ref[:, :width].astype(f32))
        value_sum = column_sums(grads_ref[:, 2 * width :].astype(f32))
        row = lax.broadcasted_iota(jnp.int32, (LANES, width), 0)
        padded = jnp.concatenate([sums, jnp.zeros((LANES - VECTORS, width), f32)], axis=0)
        padded = jnp.where(row == 0, query_sum, jnp.where(row == 1, value_sum, padded))
        vec_tile[...] = turned(padded).astype(bf16)
        core = scalar[4 * dp]
        for side, out in enumerate((keep_ref, send_ref)):
            half = core if side == 0 else 1 - core
            for source, piece in ((tile, qkv_piece), (out_ref, out_piece), (vec_tile, vector_piece)):
                columns = (
                    slice(None)
                    if piece is vector_piece
                    else aligned(half * piece.columns, piece.columns, LANES)
                )
                spread(
                    scalar,
                    dp,
                    side,
                    source,
                    out,
                    piece.rows,
                    slice(piece.first, piece.first + piece.columns),
                    columns,
                    0,
                )

    return call(
        body,
        "qkv_gradient",
        [table, rows, query_grad, *mine, *theirs, out_grad, vectors],
        [SMEM] + [VMEM] * (4 + 2 * count),
        [
            shape(tokens, 3 * width, bf16),
            shape(width, total, bf16),
            shape(width, total, bf16),
        ],
        [pltpu.VMEM((width, 3 * width), bf16), pltpu.VMEM((width, LANES), bf16)],
    )


def input_gradient(links, table, grads, resid, attn, qkv_piece):
    tokens, width = resid.shape

    def body(scalar, grads_ref, resid_ref, mine, theirs, out_ref, weight, sem):
        qkv_piece.fetch(scalar, (mine, theirs), weight, sem.at[0])
        qkv_piece.ready(weight, sem.at[0])
        out_ref[...] = resid_ref[...] + dot_rows(grads_ref[...], weight[...])

    return call(
        body,
        "input_gradient",
        [table, grads, resid, *attn],
        [SMEM, VMEM, VMEM, ANY, ANY],
        [shape(tokens, width, f32)],
        [qkv_piece.whole(), pltpu.SemaphoreType.DMA((1,))],
    )[0]


def settle(links, kept, sent, pieces):
    mine = links.reduce(kept, links.swap(sent))
    theirs = links.swap(mine)
    return [
        both_halves(
            links,
            mine[:, piece.first : piece.first + piece.columns],
            theirs[:, piece.first : piece.first + piece.columns],
        )
        for piece in pieces
    ]


def shards(
    tokens,
    lengths,
    qkv_weight,
    query_bias,
    value_bias,
    out_weight,
    out_bias,
    norm1_gain,
    norm1_shift,
    up_weight,
    up_bias,
    down_weight,
    down_bias,
    norm2_gain,
    norm2_shift,
    cotangent,
):
    seq_dev, ctx_tok, width = tokens.shape
    assert seq_dev == 1 and width // HEADS == LANES // 2
    scale = (width // HEADS) ** (-0.5)
    links = Links()
    dp = links.dp
    rows = tokens.reshape(ctx_tok, width)
    cot = cotangent.reshape(ctx_tok, width)
    block = lax.axis_index("ctx")
    start = block * ctx_tok
    table = links.table(lengths[0], start)

    shard = qkv_weight.shape[0]
    inner = down_weight.shape[0] * dp
    folds = down_weight.shape[0] // shard
    half = [w.shape[1] // 2 for w in (qkv_weight, out_weight, up_weight, down_weight)]
    qkv_piece = Piece(dp, shard, half[0], 0)
    out_piece = Piece(dp, shard, half[1], half[0])
    vector_piece = Piece(dp, shard, LANES, half[0] + half[1])
    up_piece = Piece(dp, shard, half[2], 0)
    down_piece = Piece(dp, down_weight.shape[0], half[3], 0)

    columns = [query_bias, value_bias, out_bias, norm1_gain, norm1_shift]
    columns += [down_bias, norm2_gain, norm2_shift]
    base = len(columns)
    columns += [up_bias[i * shard : (i + 1) * shard] for i in range(folds)]
    packed = jnp.stack(columns, axis=1)
    packed = jnp.pad(packed, ((0, 0), (0, LANES - packed.shape[1])))
    attn_piece = jnp.concatenate(
        [half_columns(links, qkv_weight), half_columns(links, out_weight), packed], axis=1
    )
    attn_mine = links.gather(attn_piece)
    attn = (attn_mine, links.swap(attn_mine))
    up_mine = links.gather(half_columns(links, up_weight))
    up = (up_mine, links.swap(up_mine))
    down_mine = links.gather(half_columns(links, down_weight))
    down = (down_mine, links.swap(down_mine))

    query, kv, vectors = project(
        links, table, rows, *attn, qkv_piece, vector_piece, scale
    )
    up_bias_row = (
        vectors[base : base + folds].reshape(folds, dp, shard).transpose(1, 0, 2).reshape(1, inner)
    )
    if links.ctx == 2:
        parts = [kv, links.swap(kv)]
        starts = [start, (1 - block) * ctx_tok]
    else:
        parts = [lax.all_gather(kv, "ctx", axis=0, tiled=True)]
        starts = [jnp.int32(0)]
    mixed_t, mixed, weights, inverse = attend(query, parts, starts, lengths[0])
    hidden, low, normal, deviation, sums1 = after_attention(
        links, table, rows, mixed, vectors, *attn, out_piece
    )
    output, slope, resid2, grad_ffn, down_keep, down_send, sums2 = feed_forward(
        links, table, hidden, low, vectors, up_bias_row, cot, up, down, (up_piece, down_piece)
    )
    (down_grad,) = settle(links, down_keep, down_send, [down_piece])
    grad_hidden, up_keep, up_send, up_bias_grad = feed_back(
        links, table, low, slope, resid2, grad_ffn, up, down, (up_piece, down_piece)
    )
    (up_grad,) = settle(links, up_keep, up_send, [up_piece])
    resid1, grad_mixed, out_grad, sums3 = before_attention(
        links, table, grad_hidden, normal, deviation, mixed, vectors, attn, out_piece
    )
    back = attend_back(query, parts, grad_mixed, mixed_t, weights, inverse, scale)
    if links.ctx == 2:
        received = links.swap(jnp.concatenate([back[3], back[4]], axis=1))
        mine, theirs = back[1:3], [received[:, :width], received[:, width:]]
    else:
        both = lax.psum_scatter(
            jnp.concatenate(back[1:3], axis=1), "ctx", scatter_dimension=0, tiled=True
        )
        mine, theirs = [both[:, :width], both[:, width:]], []
    up_bias_rows = (
        up_bias_grad.reshape(dp, folds, shard).transpose(1, 0, 2).reshape(folds, width)
    )
    blank = jnp.zeros((2, width), f32)
    sent = jnp.concatenate([blank, sums3, sums2[0:3], up_bias_rows, sums1, sums2[3:4]], axis=0)
    sent = jnp.pad(sent, ((0, VECTORS - sent.shape[0]), (0, 0)))
    grads, attn_keep, attn_send = qkv_gradient(
        links,
        table,
        rows,
        back[0],
        list(mine),
        list(theirs),
        out_grad,
        sent,
        (qkv_piece, out_piece, vector_piece),
    )
    qkv_grad, out_grad, vector_grad = settle(
        links, attn_keep, attn_send, [qkv_piece, out_piece, vector_piece]
    )
    input_grad = input_gradient(links, table, grads, resid1, attn, qkv_piece)
    sums = jnp.transpose(vector_grad[:, :LANES])
    at = base + folds
    stream = sums[at : at + 4, 0]
    stream_rms = jnp.sqrt(
        jnp.stack([stream[0], stream[1], stream[3]]) / (stream[2] * width) + 1e-06
    )
    return (
        output.reshape(seq_dev, ctx_tok, width),
        input_grad.reshape(seq_dev, ctx_tok, width),
        stream_rms,
        qkv_grad,
        sums[0],
        sums[1],
        out_grad,
        sums[2],
        sums[3],
        sums[4],
        up_grad,
        sums[base : base + folds].reshape(-1),
        down_grad,
        sums[5],
        sums[6],
        sums[7],
    )


def solution(mesh):
    in_specs = (
        P("dp", "ctx", None),
        P("dp"),
        P("dp", None),
        P("dp"),
        P("dp"),
        P("dp", None),
        P("dp"),
        P("dp"),
        P("dp"),
        P("dp", None),
        P("dp"),
        P("dp", None),
        P("dp"),
        P("dp"),
        P("dp"),
        P("dp", "ctx", None),
    )
    out_specs = (
        P("dp", "ctx", None),
        P("dp", "ctx", None),
        P(),
        P("dp", None),
        P("dp"),
        P("dp"),
        P("dp", None),
        P("dp"),
        P("dp"),
        P("dp"),
        P("dp", None),
        P("dp"),
        P("dp", None),
        P("dp"),
        P("dp"),
        P("dp"),
    )
    return jax.shard_map(shards, mesh=mesh, in_specs=in_specs, out_specs=out_specs, check_vma=False)
```

```python
import math

import jax
import jax.numpy as jnp
from jax import lax
from jax.experimental import pallas as pl
from jax.experimental.pallas import tpu as pltpu
from jax.sharding import PartitionSpec as P

HEADS = 12
LANES = 128
VECTORS = 16
VMEM_BYTES = 24 << 20

masked_score = -1e30
norm_eps = 1e-05
f32 = jnp.float32
bf16 = jnp.bfloat16


def low_precision(value):
    return lax.reduce_precision(value, exponent_bits=8, mantissa_bits=7)


class Links:
    def __init__(self):
        self.dp = lax.axis_size("dp")
        self.ctx = lax.axis_size("ctx")
        self.bits = self.dp.bit_length() - 1
        assert self.dp == 1 << self.bits and self.bits >= 2 and self.ctx % 2 == 0
        self.core = lax.axis_index("ctx") % 2
        self.me = lax.axis_index("dp")
        self.upper = []
        bit = 2
        while bit < self.bits:
            self.upper.append((bit, min(2, self.bits - bit)))
            bit += 2

    def swap(self, value):
        return lax.ppermute(value, "ctx", [(i, i ^ 1) for i in range(self.ctx)])

    def hop(self, value, mask_even, mask_odd):
        pairs = []
        for block in range(self.ctx):
            mask = mask_odd if block % 2 else mask_even
            pairs += [(block * self.dp + i, block * self.dp + (i ^ mask)) for i in range(self.dp)]
        return lax.ppermute(value, ("ctx", "dp"), pairs)

    def places(self, core):
        position = lax.iota(jnp.int32, self.dp)
        quarter = self.dp // 4
        first = (position // quarter) % 2
        second = position // (2 * quarter)
        mask = (position % quarter) * 4 + first * (1 + core) + second * (2 - core)
        return jnp.bitwise_xor(self.me, mask)

    def spots(self, core):
        mask = jnp.bitwise_xor(self.me, lax.iota(jnp.int32, self.dp))
        low, high = mask % 2, (mask // 2) % 2
        first = jnp.where(core == 0, low, high)
        second = jnp.where(core == 0, high, low)
        quarter = self.dp // 4
        return mask // 4 + first * quarter + second * (2 * quarter)

    def table(self, *more):
        parts = [self.places(self.core), self.places(1 - self.core)]
        parts += [self.spots(self.core), self.spots(1 - self.core)]
        parts += [jnp.reshape(value, (1,)) for value in (self.core,) + more]
        return jnp.concatenate(parts).astype(jnp.int32)

    def cross(self, piece):
        held = [piece]
        for bit, size in self.upper:
            here = jnp.concatenate(held, axis=0) if len(held) > 1 else held[0]
            held = [here] + [self.hop(here, k << bit, k << bit) for k in range(1, 1 << size)]
        return held

    def first(self, held, *waits):
        more = self.hop(held, 1, 2)
        return jnp.concatenate([held, after(more, *waits) if waits else more], axis=0)

    def second(self, held, *waits):
        early = self.swap(held)
        more = self.hop(held, 2, 1)
        if waits:
            early, more = after((early, more), *waits)
        return [held, more], [early, self.swap(more)]


def joined(held, *waits):
    return jnp.concatenate(after(tuple(held), *waits) if waits else held, axis=0)


class Sum:
    def __init__(self, links, kept, received):
        self.links = links
        self.rows = kept.shape[0]
        self.terms = [(kept,), (received,)]
        self.steps = [[(2, 1)], [(1, 2)]]
        for bit, size in reversed(links.upper):
            self.steps.append([(k << bit, k << bit) for k in range(1, 1 << size)])
        self.ready = None

    def total(self, start, span):
        value = None
        for term in self.terms:
            parts = [
                lax.slice_in_dim(part, start, start + span, axis=0).astype(f32) for part in term
            ]
            if value is None:
                value = parts[0]
            elif len(parts) == 1:
                value = low_precision(value + parts[0])
            else:
                value = low_precision((value + parts[0]) + (parts[1] + parts[2]))
        return value.astype(bf16)

    def prepare(self):
        masks = self.steps[0]
        self.rows //= len(masks) + 1
        self.ready = [self.total((i + 1) * self.rows, self.rows) for i in range(len(masks))]
        return self.ready

    def send(self):
        if self.ready is None:
            self.prepare()
        masks = self.steps.pop(0)
        self.terms.append(
            tuple(self.links.hop(value, *mask) for value, mask in zip(self.ready, masks))
        )
        self.ready = None

    def hold(self, other):
        self.terms[-1] = tuple(after(value, other) for value in self.terms[-1])

    def finish(self):
        while self.steps:
            self.send()
        mine = self.total(0, self.rows)
        step = 2
        while step < self.links.ctx:
            pairs = [(i, i ^ step) for i in range(self.links.ctx)]
            other = lax.ppermute(mine, "ctx", pairs)
            mine = low_precision(mine.astype(f32) + other.astype(f32)).astype(bf16)
            step *= 2
        return mine


def after(value, *others):
    return lax.optimization_barrier((value, others))[0]


def half_columns(links, value):
    span = value.shape[1] // 2
    return lax.dynamic_slice_in_dim(value, links.core * span, span, 1)


def both_halves(links, mine, theirs):
    even = links.core == 0
    return jnp.concatenate(
        [jnp.where(even, mine, theirs), jnp.where(even, theirs, mine)], axis=1
    ).astype(f32)


def dot(left, right):
    return jnp.dot(left, right, preferred_element_type=f32)


def dot_rows(left, right):
    return lax.dot_general(left, right, (((1,), (1,)), ((), ())), preferred_element_type=f32)


def turned(value):
    return jnp.transpose(value)


def aligned(start, size, unit):
    return pl.ds(pl.multiple_of(start, unit), size)


SMEM = pl.BlockSpec(memory_space=pltpu.SMEM)
ANY = pl.BlockSpec(memory_space=pl.ANY)
VMEM = pl.BlockSpec(memory_space=pltpu.VMEM)


def call(body, name, sources, in_specs, outs, scratch=(), cost=None):
    return pl.pallas_call(
        body,
        name=name,
        out_shape=outs,
        in_specs=in_specs,
        out_specs=[VMEM] * len(outs),
        scratch_shapes=list(scratch),
        compiler_params=pltpu.CompilerParams(vmem_limit_bytes=VMEM_BYTES),
        cost_estimate=cost,
    )(*sources)


def shape(rows, columns, dtype):
    return jax.ShapeDtypeStruct((rows, columns), dtype)


class Piece:
    def __init__(self, dp, rows, columns, first):
        self.dp, self.rows, self.columns, self.first = dp, rows, columns, first

    def fetch(self, scalar, sides, whole, sem):
        core = scalar[4 * self.dp]
        for side, sources in enumerate(sides):
            half = core if side == 0 else 1 - core
            count = self.dp // len(sources)
            for i, source in enumerate(sources):

                def one(position, carry, side=side, source=source, half=half, base=i * count):
                    owner = scalar[side * self.dp + base + position]
                    pltpu.make_async_copy(
                        source.at[
                            aligned(position * self.rows, self.rows, 8),
                            pl.ds(self.first, self.columns),
                        ],
                        whole.at[
                            aligned(owner * self.rows, self.rows, 8),
                            aligned(half * self.columns, self.columns, LANES),
                        ],
                        sem,
                    ).start()
                    return carry

                lax.fori_loop(0, count, one, 0)

    def fetch_side(self, scalar, side, sources, whole, sem):
        count = self.dp // len(sources)
        for i, source in enumerate(sources):

            def one(position, carry, source=source, base=i * count):
                owner = scalar[side * self.dp + base + position]
                pltpu.make_async_copy(
                    source.at[
                        aligned(position * self.rows, self.rows, 8),
                        pl.ds(self.first, self.columns),
                    ],
                    whole.at[aligned(owner * self.rows, self.rows, 8), :],
                    sem,
                ).start()
                return carry

            lax.fori_loop(0, count, one, 0)

    def fetch_rows(self, scalar, part, sides, whole, sem):
        core = scalar[4 * self.dp]
        for side, sources in enumerate(sides):
            half = core if side == 0 else 1 - core
            count = self.dp // len(sources)

            def one(i, carry, side=side, sources=sources, half=half, count=count):
                spot = scalar[(2 + side) * self.dp + part * (self.dp // 2) + i]
                for j, source in enumerate(sources):

                    @pl.when(spot // count == j)
                    def _(source=source, j=j):
                        pltpu.make_async_copy(
                            source.at[
                                aligned((spot - j * count) * self.rows, self.rows, 8),
                                pl.ds(self.first, self.columns),
                            ],
                            whole.at[
                                aligned(i * self.rows, self.rows, 8),
                                aligned(half * self.columns, self.columns, LANES),
                            ],
                            sem,
                        ).start()

                return carry

            lax.fori_loop(0, self.dp // 2, one, 0)

    def ready(self, whole, sem):
        pltpu.make_async_copy(whole, whole, sem).wait()

    def whole(self):
        return pltpu.VMEM((self.dp * self.rows, 2 * self.columns), bf16)


def spread(scalar, dp, side, tile, out, rows, columns, tile_columns, base):
    count = tile.shape[0] // rows

    def one(i, carry):
        spot = scalar[(2 + side) * dp + base + i]
        out[aligned(spot * rows, rows, 8), columns] = tile[
            aligned(i * rows, rows, 8), tile_columns
        ].astype(bf16)
        return carry

    lax.fori_loop(0, count, one, 0)


def sides(refs):
    return (refs[:2], refs[2:4])


def flat(gathered):
    return [*gathered[0], *gathered[1]]


def project(links, table, rows, gathered, qkv_piece, vector_piece, scale):
    tokens, width = rows.shape

    def body(scalar, rows_ref, *refs):
        q_ref, kv_ref, vec_ref, weight, vecs, sems = refs[4:]
        pieces = sides(refs)
        vector_piece.fetch_side(scalar, 0, pieces[0], vecs, sems.at[1])
        qkv_piece.fetch(scalar, pieces, weight, sems.at[0])
        vector_piece.ready(vecs, sems.at[1])
        vectors = turned(vecs[...].astype(f32))[:VECTORS]
        vec_ref[...] = vectors
        qkv_piece.ready(weight, sems.at[0])
        x = rows_ref[...]
        query = (dot(x, weight[:, :width]) + vectors[0:1]).astype(bf16)
        q_ref[...] = (query.astype(f32) * scale).astype(bf16)
        kv_ref[:, :width] = dot(x, weight[:, width : 2 * width]).astype(bf16)
        kv_ref[:, width:] = (dot(x, weight[:, 2 * width :]) + vectors[1:2]).astype(bf16)

    return call(
        body,
        "qkv",
        [table, rows, *flat(gathered)],
        [SMEM, VMEM] + [ANY] * 4,
        [shape(tokens, width, bf16), shape(tokens, 2 * width, bf16), shape(VECTORS, width, f32)],
        [qkv_piece.whole(), pltpu.VMEM((width, LANES), bf16), pltpu.SemaphoreType.DMA((2,))],
    )


def pair_specs(parts, pairs, base):
    specs = []
    for part in parts:
        rows = part.shape[0]
        specs.append(pl.BlockSpec((rows, LANES), lambda p, s: (0, base + p)))
        specs.append(pl.BlockSpec((rows, LANES), lambda p, s: (0, pairs + base + p)))
    return specs


def first_lanes(shape_, count):
    return (lax.broadcasted_iota(jnp.int32, shape_, 1) < count).astype(f32).astype(bf16)


def head_blocks(query):
    lane = lax.broadcasted_iota(jnp.int32, query.shape, 1)
    zero = jnp.zeros_like(query)
    half = LANES // 2
    return jnp.concatenate(
        [jnp.where(lane < half, query, zero), jnp.where(lane >= half, query, zero)], axis=0
    )


def attend(query, parts, starts, length, base, count):
    tokens, width = query.shape
    pairs = width // LANES
    span = sum(part.shape[0] for part in parts)
    half = LANES // 2
    chunk = min(256, tokens)
    scalars = jnp.concatenate(
        [jnp.reshape(v, (1,)).astype(jnp.int32) for v in [length, *starts]]
    )

    def body(scalar, q_ref, *refs):
        kv_refs = refs[: 2 * len(parts)]
        mixed_t_ref, mixed_ref, p_ref, inverse_ref, bias = refs[2 * len(parts) :]

        @pl.when(pl.program_id(0) == 0)
        def _():
            at = 0
            for i, part in enumerate(parts):
                rows = part.shape[0]
                position = scalar[1 + i] + lax.broadcasted_iota(jnp.int32, (rows, LANES), 0)
                lane = lax.broadcasted_iota(jnp.int32, (rows, LANES), 1)
                hidden = jnp.where(position < scalar[0], 0.0, masked_score)
                bias[at : at + rows, :] = jnp.where(lane == 0, hidden, 0.0).astype(bf16)
                at += rows

        keys = jnp.concatenate([ref[...] for ref in kv_refs[0::2]], axis=0)
        values = jnp.concatenate([ref[...] for ref in kv_refs[1::2]], axis=0)
        keys = jnp.concatenate([keys, bias[...]], axis=1)
        values_t = jnp.concatenate([turned(values), jnp.ones((16, span), bf16)], axis=0)
        queries = head_blocks(q_ref[...])
        queries = jnp.concatenate([queries, first_lanes(queries.shape, 1)], axis=1)
        for at in range(0, 2 * tokens, chunk):
            scores = dot_rows(keys, queries[at : at + chunk])
            peak = jnp.max(scores, axis=0, keepdims=True)
            weights = jnp.exp(scores - peak).astype(bf16)
            p_ref[:, at : at + chunk] = weights
            sums = dot(values_t, weights)
            inverse = 1.0 / sums[LANES : LANES + 1]
            inverse_ref[:, at : at + chunk] = inverse
            low = 0 if at < tokens else half
            to = at % tokens
            mixed_t_ref[low : low + half, to : to + chunk] = sums[low : low + half] * inverse
        mixed_ref[...] = turned(mixed_t_ref[...]).astype(bf16)

    sources = [query]
    for part in parts:
        sources += [part, part]
    return pl.pallas_call(
        body,
        name="attend",
        out_shape=[
            shape(count * LANES, tokens, f32),
            shape(tokens, count * LANES, bf16),
            jax.ShapeDtypeStruct((count, span, 2 * tokens), bf16),
            jax.ShapeDtypeStruct((count, 1, 2 * tokens), f32),
        ],
        grid_spec=pltpu.PrefetchScalarGridSpec(
            num_scalar_prefetch=1,
            grid=(count,),
            in_specs=[pl.BlockSpec((tokens, LANES), lambda p, s: (0, base + p))]
            + pair_specs(parts, pairs, base),
            out_specs=[
                pl.BlockSpec((LANES, tokens), lambda p, s: (p, 0)),
                pl.BlockSpec((tokens, LANES), lambda p, s: (0, p)),
                pl.BlockSpec((None, span, 2 * tokens), lambda p, s: (p, 0, 0)),
                pl.BlockSpec((None, 1, 2 * tokens), lambda p, s: (p, 0, 0)),
            ],
            scratch_shapes=[pltpu.VMEM((span, LANES), bf16)],
        ),
        compiler_params=pltpu.CompilerParams(vmem_limit_bytes=min(56 << 20, VMEM_BYTES * max(1, span // 1024))),
    )(scalars, *sources)


def attend_back(query, parts, grad_mixed, mixed_t, weights, inverse, scale, base, count):
    tokens, width = query.shape
    pairs = width // LANES
    span = sum(part.shape[0] for part in parts)
    half = LANES // 2
    chunk = min(256, tokens)

    def body(_, q_ref, gm_ref, mt_ref, p_ref, inv_ref, *refs):
        kv_refs = refs[: 2 * len(parts)]
        dq_ref = refs[2 * len(parts)]
        dkv_refs = refs[2 * len(parts) + 1 : -1]
        ds_ref = refs[-1]
        keys = jnp.concatenate([ref[...] for ref in kv_refs[0::2]], axis=0)
        values = jnp.concatenate([ref[...] for ref in kv_refs[1::2]], axis=0)
        grads = turned(gm_ref[...].astype(f32))
        inv = inv_ref[...]
        product = grads * mt_ref[...]
        empty = jnp.zeros((half, tokens), bf16)
        even, odd = inv[:, :tokens], inv[:, tokens:]
        delta = jnp.concatenate(
            [
                jnp.sum(product[:half], axis=0, keepdims=True) * even,
                jnp.sum(product[half:], axis=0, keepdims=True) * odd,
            ],
            axis=1,
        )
        top = jnp.concatenate([(grads[:half] * even).astype(bf16), empty], axis=1)
        bottom = jnp.concatenate([empty, (grads[half:] * odd).astype(bf16)], axis=1)
        scaled = jnp.concatenate([top, bottom], axis=0)
        first = (-delta).astype(bf16).astype(f32)
        second = (-delta - first).astype(bf16).astype(f32)
        third = (-delta - first - second).astype(bf16).astype(f32)
        row = lax.broadcasted_iota(jnp.int32, (LANES, 2 * tokens), 0)
        limbs = jnp.where(
            row == 0, first, jnp.where(row == 1, second, jnp.where(row == 2, third, 0.0))
        ).astype(bf16)
        right = jnp.concatenate([scaled, limbs], axis=0)
        left = jnp.concatenate([values, first_lanes(values.shape, 3)], axis=1)
        for at in range(0, 2 * tokens, chunk):
            grad_probs = dot(left, right[:, at : at + chunk])
            ds_ref[:, at : at + chunk] = (
                p_ref[:, at : at + chunk].astype(f32) * grad_probs
            ).astype(bf16)
        grad_scores = ds_ref[...]
        turned_grad = dot(turned(keys), grad_scores)
        dq_ref[...] = (
            turned(
                jnp.concatenate([turned_grad[:half, :tokens], turned_grad[half:, tokens:]], axis=0)
            )
            * scale
        ).astype(bf16)
        grad_keys = dot(grad_scores, head_blocks(q_ref[...])).astype(bf16)
        grad_values = dot_rows(p_ref[...], scaled).astype(bf16)
        at = 0
        for i, part in enumerate(parts):
            rows = part.shape[0]
            dkv_refs[2 * i][...] = grad_keys[at : at + rows]
            dkv_refs[2 * i + 1][...] = grad_values[at : at + rows]
            at += rows

    sources = [query, grad_mixed, mixed_t, weights, inverse]
    out_shapes = [shape(tokens, count * LANES, bf16)]
    columns = lambda p, s: (0, p)
    offset = lambda p, s: (0, base + p)
    out_specs = [pl.BlockSpec((tokens, LANES), columns)]
    for part in parts:
        sources += [part, part]
        rows = part.shape[0]
        out_shapes += [shape(rows, count * LANES, bf16)] * 2
        out_specs += [pl.BlockSpec((rows, LANES), columns)] * 2
    return pl.pallas_call(
        body,
        name="attend_back",
        out_shape=out_shapes,
        grid_spec=pltpu.PrefetchScalarGridSpec(
            num_scalar_prefetch=1,
            grid=(count,),
            in_specs=[
                pl.BlockSpec((tokens, LANES), offset),
                pl.BlockSpec((tokens, LANES), offset),
                pl.BlockSpec((LANES, tokens), lambda p, s: (p, 0)),
                pl.BlockSpec((None, span, 2 * tokens), lambda p, s: (p, 0, 0)),
                pl.BlockSpec((None, 1, 2 * tokens), lambda p, s: (p, 0, 0)),
            ]
            + pair_specs(parts, pairs, base),
            out_specs=out_specs,
            scratch_shapes=[pltpu.VMEM((span, 2 * tokens), bf16)],
        ),
        compiler_params=pltpu.CompilerParams(vmem_limit_bytes=min(56 << 20, VMEM_BYTES * max(1, span // 1024))),
    )(jnp.zeros((1,), jnp.int32), *sources)


def normalize(resid):
    center = resid - jnp.mean(resid, axis=1, keepdims=True)
    inverse = lax.rsqrt(jnp.mean(center * center, axis=1, keepdims=True) + norm_eps)
    return center * inverse, inverse


def norm_back(grads, normal, inverse, gain):
    scaled = grads * gain
    return inverse * (
        scaled
        - jnp.mean(scaled, axis=1, keepdims=True)
        - normal * jnp.mean(scaled * normal, axis=1, keepdims=True)
    )


def column_sums(value):
    return jnp.sum(value, axis=0, keepdims=True)


def masked_total(value, valid, width):
    lanes = column_sums(jnp.where(valid, value * value, 0.0))
    return jnp.broadcast_to(jnp.sum(lanes, axis=1, keepdims=True), (1, width))


def valid_rows(scalar, at, tokens):
    position = scalar[at + 1] + lax.broadcasted_iota(jnp.int32, (tokens, 1), 0)
    return position < scalar[at]


def after_attention(links, table, rows, mixed, vectors, gathered, out_piece):
    tokens, width = rows.shape
    extra = 4 * links.dp + 1
    count = len(mixed)
    part = width // count

    def body(scalar, rows_ref, vec_ref, *refs):
        mixed_refs = refs[:count]
        pieces = sides(refs[count:])
        hidden_ref, low_ref, normal_ref, inverse_ref, sums_ref, weight, sem = refs[count + 4 :]
        out_piece.fetch(scalar, pieces, weight, sem.at[0])
        x = rows_ref[...].astype(f32)
        valid = valid_rows(scalar, extra, tokens)
        sums_ref[0:1, :] = masked_total(x, valid, width)
        rows_there = jnp.sum(valid.astype(f32), axis=0, keepdims=True)
        sums_ref[2:3, :] = jnp.broadcast_to(rows_there, (1, width))
        out_piece.ready(weight, sem.at[0])
        branch = vec_ref[2:3]
        for i, ref in enumerate(mixed_refs):
            branch = branch + dot(ref[...], weight[i * part : (i + 1) * part, :])
        sums_ref[1:2, :] = masked_total(branch, valid, width)
        normal, inverse = normalize(x + branch)
        hidden = normal * vec_ref[3:4] + vec_ref[4:5]
        normal_ref[...] = normal
        inverse_ref[...] = inverse
        hidden_ref[...] = hidden
        low_ref[...] = hidden.astype(bf16)

    return call(
        body,
        "after_attention",
        [table, rows, vectors, *mixed, *flat(gathered)],
        [SMEM] + [VMEM] * (2 + count) + [ANY] * 4,
        [
            shape(tokens, width, f32),
            shape(tokens, width, bf16),
            shape(tokens, width, f32),
            shape(tokens, 1, f32),
            shape(3, width, f32),
        ],
        [out_piece.whole(), pltpu.SemaphoreType.DMA((1,))],
    )


def gelu_and_slope(u):
    phi = 0.5 * lax.erf(u * math.sqrt(0.5)) + 0.5
    bell = jnp.exp(-0.5 * (u * u)) * (1.0 / math.sqrt(2.0 * math.pi))
    return u * phi, phi + u * bell


def feed_up(links, table, low, up_bias, gathered, up_piece):
    tokens, width = low.shape
    inner = up_bias.shape[1]

    def body(scalar, low_ref, bias_ref, *refs):
        act_ref, slope_ref, weight, sem = refs[4:]
        up_piece.fetch(scalar, sides(refs), weight, sem.at[0])
        up_piece.ready(weight, sem.at[0])

        def forward(j, carry):
            at = aligned(j * width, width, LANES)
            value, slope = gelu_and_slope(dot(low_ref[...], weight[:, at]) + bias_ref[:, at])
            act_ref[:, at] = value.astype(bf16)
            slope_ref[:, at] = slope.astype(bf16)
            return carry

        lax.fori_loop(0, inner // width, forward, 0)

    return call(
        body,
        "feed_up",
        [table, low, up_bias, *flat(gathered)],
        [SMEM] + [VMEM] * 2 + [ANY] * 4,
        [shape(tokens, inner, bf16), shape(tokens, inner, bf16)],
        [up_piece.whole(), pltpu.SemaphoreType.DMA((1,))],
    )


def feed_down(links, table, act, hidden, vectors, cotangent, gathered, down_piece):
    tokens, width = hidden.shape
    inner = act.shape[1]
    extra = 4 * links.dp + 1
    dp = links.dp

    def body(scalar, act_ref, hidden_ref, vec_ref, cot_ref, *refs):
        out_ref, resid_ref, grad_ref, keep_ref, send_ref, sums_ref, weight, tile, sem = refs[4:]
        down_piece.fetch(scalar, sides(refs), weight, sem.at[0])
        down_piece.ready(weight, sem.at[0])
        branch = dot(act_ref[...], weight[...]) + vec_ref[5:6]
        sums_ref[3:4, :] = masked_total(branch, valid_rows(scalar, extra, tokens), width)
        normal, inverse = normalize(hidden_ref[...] + branch)
        out_ref[...] = (normal * vec_ref[6:7] + vec_ref[7:8]).astype(bf16)
        grads = cot_ref[...].astype(f32)
        sums_ref[1:2, :] = column_sums(grads * normal)
        sums_ref[2:3, :] = column_sums(grads)
        resid = norm_back(grads, normal, inverse, vec_ref[6:7])
        resid_ref[...] = resid
        grad_ffn = resid.astype(bf16)
        grad_ref[...] = grad_ffn
        sums_ref[0:1, :] = column_sums(grad_ffn.astype(f32))
        core = scalar[4 * dp]

        def backward(j, carry):
            at = aligned(j * width, width, LANES)
            tile[...] = dot(turned(act_ref[:, at]), grad_ref[...])
            for side, out in enumerate((keep_ref, send_ref)):
                half = core if side == 0 else 1 - core
                spread(
                    scalar,
                    dp,
                    side,
                    tile,
                    out,
                    down_piece.rows,
                    slice(None),
                    aligned(half * down_piece.columns, down_piece.columns, LANES),
                    j * (width // down_piece.rows),
                )
            return carry

        lax.fori_loop(0, inner // width, backward, 0)

    return call(
        body,
        "feed_down",
        [table, act, hidden, vectors, cotangent, *flat(gathered)],
        [SMEM] + [VMEM] * 4 + [ANY] * 4,
        [
            shape(tokens, width, bf16),
            shape(tokens, width, f32),
            shape(tokens, width, bf16),
            shape(inner, width // 2, bf16),
            shape(inner, width // 2, bf16),
            shape(4, width, f32),
        ],
        [
            down_piece.whole(),
            pltpu.VMEM((width, width), f32),
            pltpu.SemaphoreType.DMA((1,)),
        ],
    )


def feed_back(links, table, side, low, slope, so_far, grad_ffn, up, down, pieces):
    tokens, width = so_far.shape
    up_piece, down_piece = pieces
    span = up_piece.columns
    block = width if span % width == 0 else span
    dp = links.dp

    def body(scalar, low_ref, slope_ref, so_far_ref, grad_ref, um, ul, *refs):
        hidden_ref, out_ref, bias_ref, up_w, down_w, low_t, tile, sems = refs[4:]
        core = scalar[4 * dp]
        half = core if side == 0 else 1 - core
        down_piece.fetch_rows(scalar, half, sides(refs), down_w, sems.at[1])
        up_piece.fetch_side(scalar, side, (um, ul), up_w, sems.at[0])
        low_t[...] = turned(low_ref[...])
        hidden_ref[...] = so_far_ref[...]
        down_piece.ready(down_w, sems.at[1])
        up_piece.ready(up_w, sems.at[0])

        def backward(j, carry):
            here = aligned(j * block, block, LANES)
            at = aligned(half * span + j * block, block, LANES)
            grads = dot_rows(grad_ref[...], down_w[here, :]) * slope_ref[:, at].astype(f32)
            grads = grads.astype(bf16)
            bias_ref[:, here] = column_sums(grads.astype(f32))
            hidden_ref[...] += dot_rows(grads, up_w[:, here])
            tile[...] = dot(low_t[...], grads)
            spread(scalar, dp, side, tile, out_ref, up_piece.rows, here, slice(None), 0)
            return carry

        lax.fori_loop(0, span // block, backward, 0)

    return call(
        body,
        "feed_back",
        [table, low, slope, so_far, grad_ffn, *up[side], *flat(down)],
        [SMEM] + [VMEM] * 4 + [ANY] * 6,
        [shape(tokens, width, f32), shape(width, span, bf16), shape(1, span, f32)],
        [
            pltpu.VMEM((width, span), bf16),
            pltpu.VMEM((span, width), bf16),
            pltpu.VMEM((width, tokens), bf16),
            pltpu.VMEM((width, block), f32),
            pltpu.SemaphoreType.DMA((2,)),
        ],
    )


def before_attention(links, table, grad_hidden, normal, inverse, mixed, vectors, gathered, piece):
    tokens, width = normal.shape
    count = len(mixed)
    part = width // count

    def body(scalar, grad_ref, normal_ref, inverse_ref, vec_ref, *refs):
        mixed_refs = refs[:count]
        pieces = sides(refs[count:])
        resid_ref, gm_ref, out_ref, sums_ref, weight, sem = refs[count + 4 :]
        piece.fetch(scalar, pieces, weight, sem.at[0])
        grads = grad_ref[...]
        normal_ = normal_ref[...]
        sums_ref[1:2, :] = column_sums(grads * normal_)
        sums_ref[2:3, :] = column_sums(grads)
        resid = norm_back(grads, normal_, inverse_ref[...], vec_ref[3:4])
        resid_ref[...] = resid
        grad_attn = resid.astype(bf16)
        sums_ref[0:1, :] = column_sums(grad_attn.astype(f32))
        piece.ready(weight, sem.at[0])
        gm_ref[...] = dot_rows(grad_attn, weight[...]).astype(bf16)
        for i, ref in enumerate(mixed_refs):
            out_ref[i * part : (i + 1) * part, :] = dot(turned(ref[...]), grad_attn).astype(bf16)

    return call(
        body,
        "before_attention",
        [table, grad_hidden, normal, inverse, vectors, *mixed, *flat(gathered)],
        [SMEM] + [VMEM] * (4 + count) + [ANY] * 4,
        [
            shape(tokens, width, f32),
            shape(tokens, width, bf16),
            shape(width, width, bf16),
            shape(3, width, f32),
        ],
        [piece.whole(), pltpu.SemaphoreType.DMA((1,))],
    )


def qkv_gradient(links, table, rows, shares, out_grad, vectors, pieces):
    tokens, width = rows.shape
    qkv_piece, out_piece, vector_piece = pieces
    dp = links.dp
    total = qkv_piece.columns + out_piece.columns + LANES
    sizes = [len(share) for share in shares]
    given = [value for share in shares for value in share]

    def body(scalar, rows_ref, *refs):
        share_refs = list(refs[: len(given)])
        out_ref, vec_ref, grads_ref, keep_ref, send_ref, tile, vec_tile = refs[len(given) :]
        at = 0
        for size in sizes:
            group, share_refs = share_refs[:size], share_refs[size:]
            span = group[0].shape[1]
            grads_ref[:, at : at + span] = group[0][...]
            for i in range(2):
                if size == 3:
                    share = group[1 + i][...]
                else:
                    both = group[3][:, i * span : (i + 1) * span]
                    share = (group[1 + i][...].astype(f32) + both.astype(f32)).astype(bf16)
                grads_ref[:, (1 + i) * width + at : (1 + i) * width + at + span] = share
            at += span
        rows_t = turned(rows_ref[...])
        for i in range(3):
            at = slice(i * width, (i + 1) * width)
            tile[:, at] = dot(rows_t, grads_ref[:, at]).astype(bf16)
        sums = vec_ref[...]
        query_sum = column_sums(grads_ref[:, :width].astype(f32))
        value_sum = column_sums(grads_ref[:, 2 * width :].astype(f32))
        row = lax.broadcasted_iota(jnp.int32, (LANES, width), 0)
        padded = jnp.concatenate([sums, jnp.zeros((LANES - VECTORS, width), f32)], axis=0)
        padded = jnp.where(row == 0, query_sum, jnp.where(row == 1, value_sum, padded))
        vec_tile[...] = turned(padded).astype(bf16)
        core = scalar[4 * dp]
        for side, out in enumerate((keep_ref, send_ref)):
            half = core if side == 0 else 1 - core
            for source, piece in ((tile, qkv_piece), (out_ref, out_piece), (vec_tile, vector_piece)):
                columns = (
                    slice(None)
                    if piece is vector_piece
                    else aligned(half * piece.columns, piece.columns, LANES)
                )
                spread(
                    scalar,
                    dp,
                    side,
                    source,
                    out,
                    piece.rows,
                    slice(piece.first, piece.first + piece.columns),
                    columns,
                    0,
                )

    return call(
        body,
        "qkv_gradient",
        [table, rows, *given, out_grad, vectors],
        [SMEM] + [VMEM] * (3 + len(given)),
        [
            shape(tokens, 3 * width, bf16),
            shape(width, total, bf16),
            shape(width, total, bf16),
        ],
        [pltpu.VMEM((width, 3 * width), bf16), pltpu.VMEM((width, LANES), bf16)],
    )


def input_gradient(links, table, grads, resid, gathered, qkv_piece):
    tokens, width = resid.shape

    def body(scalar, grads_ref, resid_ref, *refs):
        out_ref, weight, sem = refs[4:]
        qkv_piece.fetch(scalar, sides(refs), weight, sem.at[0])
        qkv_piece.ready(weight, sem.at[0])
        out_ref[...] = resid_ref[...] + dot_rows(grads_ref[...], weight[...])

    return call(
        body,
        "input_gradient",
        [table, grads, resid, *flat(gathered)],
        [SMEM, VMEM, VMEM] + [ANY] * 4,
        [shape(tokens, width, f32)],
        [qkv_piece.whole(), pltpu.SemaphoreType.DMA((1,))],
    )[0]


def settle(links, reduction, pieces):
    mine = reduction.finish()
    theirs = links.swap(mine)
    return [
        both_halves(
            links,
            mine[:, piece.first : piece.first + piece.columns],
            theirs[:, piece.first : piece.first + piece.columns],
        )
        for piece in pieces
    ]


def shards(
    tokens,
    lengths,
    qkv_weight,
    query_bias,
    value_bias,
    out_weight,
    out_bias,
    norm1_gain,
    norm1_shift,
    up_weight,
    up_bias,
    down_weight,
    down_bias,
    norm2_gain,
    norm2_shift,
    cotangent,
):
    seq_dev, ctx_tok, width = tokens.shape
    assert seq_dev == 1 and width // HEADS == LANES // 2
    scale = (width // HEADS) ** (-0.5)
    links = Links()
    dp = links.dp
    rows = tokens.reshape(ctx_tok, width)
    cot = cotangent.reshape(ctx_tok, width)
    block = lax.axis_index("ctx")
    start = block * ctx_tok
    table = links.table(lengths[0], start)

    shard = qkv_weight.shape[0]
    inner = down_weight.shape[0] * dp
    folds = down_weight.shape[0] // shard
    half = [w.shape[1] // 2 for w in (qkv_weight, out_weight, up_weight, down_weight)]
    qkv_piece = Piece(dp, shard, half[0], 0)
    vector_piece = Piece(dp, shard, LANES, half[0])
    up_piece = Piece(dp, shard, half[2], 0)
    out_piece = Piece(dp, shard, half[1], half[2])
    down_piece = Piece(dp, down_weight.shape[0], half[3], 0)
    out_grad_piece = Piece(dp, shard, half[1], half[0])
    vector_grad_piece = Piece(dp, shard, LANES, half[0] + half[1])
    ffn_pieces = (up_piece, down_piece)

    columns = [query_bias, value_bias, out_bias, norm1_gain, norm1_shift]
    columns += [down_bias, norm2_gain, norm2_shift]
    base = len(columns)
    columns += [up_bias[i * shard : (i + 1) * shard] for i in range(folds)]
    packed = jnp.stack(columns, axis=1)
    packed = jnp.pad(packed, ((0, 0), (0, LANES - packed.shape[1])))
    qkv_sent = jnp.concatenate([half_columns(links, qkv_weight), packed], axis=1)
    up_sent = jnp.concatenate(
        [half_columns(links, up_weight), half_columns(links, out_weight)], axis=1
    )
    down_sent = half_columns(links, down_weight)

    qkv_held = joined(links.cross(qkv_sent))
    up_held = links.cross(after(up_sent, qkv_held))
    down_sent = after(down_sent, up_held)
    qkv_held = links.first(qkv_held)
    qkv = links.second(after(qkv_held, up_held[1]), *up_held)
    up_held = after(joined(up_held), qkv[0][1])
    query, kv, vectors = project(
        links, table, after(rows, up_held), qkv, qkv_piece, vector_piece, scale
    )
    up_held = links.first(up_held, query)
    up_bias_row = (
        vectors[base : base + folds].reshape(folds, dp, shard).transpose(1, 0, 2).reshape(1, inner)
    )
    if links.ctx == 2:
        parts = [kv, links.swap(kv)]
        starts = [start, (1 - block) * ctx_tok]
    else:
        parts = [lax.all_gather(kv, "ctx", axis=0, tiled=True)]
        starts = [jnp.int32(0)]
    groups = 3
    count = width // LANES // groups
    forward = []
    waits = [up_held, query, query]
    for i in range(groups):
        given = after(query, waits[i], *(forward[-1][1:2] if forward else ()))
        forward.append(attend(given, parts, starts, lengths[0], i * count, count))
    up = links.second(up_held, forward[1][1])
    down_held = joined(links.cross(after(down_sent, up_held)), forward[0][1])
    down_held = links.first(down_held, forward[1][1])
    mixed = [f[1] for f in forward]
    hidden, low, normal, deviation, sums1 = after_attention(
        links, table, after(rows, down_held), mixed, vectors, up, out_piece
    )
    down = links.second(down_held, hidden)
    act, slope = feed_up(links, table, low, up_bias_row, up, up_piece)
    output, resid2, grad_ffn, down_keep, down_send, sums2 = feed_down(
        links, table, act, hidden, vectors, cot, down, down_piece
    )
    down_sum = Sum(links, down_keep, links.swap(down_send))
    grad_hidden, up_sent, bias_sent = feed_back(
        links, table, 1, low, slope, resid2, grad_ffn, up, down, ffn_pieces
    )
    grad_hidden, up_kept, bias_kept = feed_back(
        links,
        table,
        0,
        low,
        slope,
        after(grad_hidden, down_sum.prepare()),
        grad_ffn,
        up,
        down,
        ffn_pieces,
    )
    down_sum.send()
    up_sum = Sum(links, up_kept, links.swap(up_sent))
    resid1, grad_mixed, out_grad, sums3 = before_attention(
        links,
        table,
        after(grad_hidden, up_sum.prepare()),
        normal,
        deviation,
        mixed,
        vectors,
        up,
        out_piece,
    )
    up_sum.send()
    back = None
    shares = []
    for i in range(groups):
        sum_ = (down_sum, up_sum, down_sum)[i]
        if back is not None:
            sum_.hold(back[0])
        given = after(query, sum_.prepare(), *(shares[-1][0:1] if shares else ()))
        sum_.send()
        mixed_t, _, weights, inverse = forward[i]
        back = attend_back(
            given, parts, grad_mixed, mixed_t, weights, inverse, scale, i * count, count
        )
        if links.ctx == 2:
            received = links.swap(jnp.concatenate([back[3], back[4]], axis=1))
            shares.append([back[0], back[1], back[2], received])
        else:
            both = lax.psum_scatter(
                jnp.concatenate(back[1:3], axis=1), "ctx", scatter_dimension=0, tiled=True
            )
            shares.append([back[0], both[:, : count * LANES], both[:, count * LANES :]])
    bias = jnp.where(
        links.core == 0,
        jnp.concatenate([bias_kept, bias_sent], axis=1),
        jnp.concatenate([bias_sent, bias_kept], axis=1),
    )
    up_bias_rows = bias.reshape(dp, folds, shard).transpose(1, 0, 2).reshape(folds, width)
    blank = jnp.zeros((2, width), f32)
    sent = jnp.concatenate([blank, sums3, sums2[0:3], up_bias_rows, sums1, sums2[3:4]], axis=0)
    sent = jnp.pad(sent, ((0, VECTORS - sent.shape[0]), (0, 0)))
    up_sum.hold(back[0])
    grads, attn_keep, attn_send = qkv_gradient(
        links,
        table,
        after(rows, up_sum.prepare()),
        shares,
        out_grad,
        sent,
        (qkv_piece, out_grad_piece, vector_grad_piece),
    )
    up_sum.send()
    attn_sum = Sum(links, attn_keep, links.swap(attn_send))
    given = after(grads, attn_sum.prepare())
    attn_sum.send()
    input_grad = input_gradient(links, table, given, resid1, qkv, qkv_piece)
    attn_sum.hold(input_grad)
    (down_grad,) = settle(links, down_sum, [down_piece])
    (up_grad,) = settle(links, up_sum, [up_piece])
    qkv_grad, out_grad, vector_grad = settle(
        links, attn_sum, [qkv_piece, out_grad_piece, vector_grad_piece]
    )
    sums = jnp.transpose(vector_grad[:, :LANES])
    at = base + folds
    stream = sums[at : at + 4, 0]
    stream_rms = jnp.sqrt(
        jnp.stack([stream[0], stream[1], stream[3]]) / (stream[2] * width) + 1e-06
    )
    return (
        output.reshape(seq_dev, ctx_tok, width),
        input_grad.reshape(seq_dev, ctx_tok, width),
        stream_rms,
        qkv_grad,
        sums[0],
        sums[1],
        out_grad,
        sums[2],
        sums[3],
        sums[4],
        up_grad,
        sums[base : base + folds].reshape(-1),
        down_grad,
        sums[5],
        sums[6],
        sums[7],
    )


def solution(mesh):
    in_specs = (
        P("dp", "ctx", None),
        P("dp"),
        P("dp", None),
        P("dp"),
        P("dp"),
        P("dp", None),
        P("dp"),
        P("dp"),
        P("dp"),
        P("dp", None),
        P("dp"),
        P("dp", None),
        P("dp"),
        P("dp"),
        P("dp"),
        P("dp", "ctx", None),
    )
    out_specs = (
        P("dp", "ctx", None),
        P("dp", "ctx", None),
        P(),
        P("dp", None),
        P("dp"),
        P("dp"),
        P("dp", None),
        P("dp"),
        P("dp"),
        P("dp"),
        P("dp", None),
        P("dp"),
        P("dp", None),
        P("dp"),
        P("dp"),
        P("dp"),
    )
    return jax.shard_map(shards, mesh=mesh, in_specs=in_specs, out_specs=out_specs, check_vma=False)
```

```python
import math

import jax
import jax.numpy as jnp
from jax import lax
from jax.experimental import pallas as pl
from jax.experimental.pallas import tpu as pltpu
from jax.sharding import PartitionSpec as P

HEADS = 12
LANES = 128
VECTORS = 16
VMEM_BYTES = 24 << 20
FLOPS = 400_000_000
BYTES = 1_200_000

masked_score = -1e30
norm_eps = 1e-05
f32 = jnp.float32
bf16 = jnp.bfloat16


def low_precision(value):
    return lax.reduce_precision(value, exponent_bits=8, mantissa_bits=7)


class Links:
    def __init__(self):
        self.dp = lax.axis_size("dp")
        self.ctx = lax.axis_size("ctx")
        self.bits = self.dp.bit_length() - 1
        assert self.dp == 1 << self.bits and self.bits >= 2 and self.ctx % 2 == 0
        self.core = lax.axis_index("ctx") % 2
        self.me = lax.axis_index("dp")
        self.upper = []
        bit = 2
        while bit < self.bits:
            self.upper.append((bit, min(2, self.bits - bit)))
            bit += 2

    def swap(self, value):
        return lax.ppermute(value, "ctx", [(i, i ^ 1) for i in range(self.ctx)])

    def hop(self, value, mask_even, mask_odd):
        pairs = []
        for block in range(self.ctx):
            mask = mask_odd if block % 2 else mask_even
            pairs += [(block * self.dp + i, block * self.dp + (i ^ mask)) for i in range(self.dp)]
        return lax.ppermute(value, ("ctx", "dp"), pairs)

    def places(self, core):
        position = lax.iota(jnp.int32, self.dp)
        quarter = self.dp // 4
        first = (position // quarter) % 2
        second = position // (2 * quarter)
        mask = (position % quarter) * 4 + first * (1 + core) + second * (2 - core)
        return jnp.bitwise_xor(self.me, mask)

    def spots(self, core):
        mask = jnp.bitwise_xor(self.me, lax.iota(jnp.int32, self.dp))
        low, high = mask % 2, (mask // 2) % 2
        first = jnp.where(core == 0, low, high)
        second = jnp.where(core == 0, high, low)
        quarter = self.dp // 4
        return mask // 4 + first * quarter + second * (2 * quarter)

    def table(self, *more):
        parts = [self.places(self.core), self.places(1 - self.core)]
        parts += [self.spots(self.core), self.spots(1 - self.core)]
        parts += [jnp.reshape(value, (1,)) for value in (self.core,) + more]
        return jnp.concatenate(parts).astype(jnp.int32)

    def cross(self, piece):
        held = [piece]
        for bit, size in self.upper:
            here = jnp.concatenate(held, axis=0) if len(held) > 1 else held[0]
            held = [here] + [self.hop(here, k << bit, k << bit) for k in range(1, 1 << size)]
        return held

    def first(self, held, *waits):
        more = self.hop(held, 1, 2)
        return jnp.concatenate([held, after(more, *waits) if waits else more], axis=0)

    def second(self, held, *waits):
        early = self.swap(held)
        more = self.hop(held, 2, 1)
        if waits:
            early, more = after((early, more), *waits)
        return [held, more], [early, self.swap(more)]


def joined(held, *waits):
    return jnp.concatenate(after(tuple(held), *waits) if waits else held, axis=0)


class Sum:
    def __init__(self, links, kept):
        self.links = links
        self.kept = kept
        self.quarter = kept[0].shape[0]
        self.rows = 4 * self.quarter
        self.terms = []
        self.steps = [[(2, 1)], [(1, 2)]]
        for bit, size in reversed(links.upper):
            self.steps.append([(k << bit, k << bit) for k in range(1, 1 << size)])
        self.ready = None

    def total(self, start, span):
        index = min(2, start // self.quarter)
        first = start - index * self.quarter
        value = self.kept[index]
        if span != value.shape[0]:
            value = lax.slice_in_dim(value, first, first + span, axis=0)
        if not self.terms:
            return value
        value = value.astype(f32)
        for term in self.terms:
            parts = [
                lax.slice_in_dim(part, start, start + span, axis=0).astype(f32) for part in term
            ]
            if len(parts) == 1:
                value = low_precision(value + parts[0])
            else:
                value = low_precision((value + parts[0]) + (parts[1] + parts[2]))
        return value.astype(bf16)

    def prepare(self):
        masks = self.steps[0]
        self.rows //= len(masks) + 1
        self.ready = [self.total((i + 1) * self.rows, self.rows) for i in range(len(masks))]
        return self.ready

    def send(self):
        if self.ready is None:
            self.prepare()
        masks = self.steps.pop(0)
        self.terms.append(
            tuple(self.links.hop(value, *mask) for value, mask in zip(self.ready, masks))
        )
        self.ready = None

    def hold(self, other):
        self.terms[-1] = tuple(after(value, other) for value in self.terms[-1])

    def finish(self):
        while self.steps:
            self.send()
        mine = self.total(0, self.rows)
        step = 2
        while step < self.links.ctx:
            pairs = [(i, i ^ step) for i in range(self.links.ctx)]
            other = lax.ppermute(mine, "ctx", pairs)
            mine = low_precision(mine.astype(f32) + other.astype(f32)).astype(bf16)
            step *= 2
        return mine


def after(value, *others):
    return lax.optimization_barrier((value, others))[0]


def half_columns(links, value):
    span = value.shape[1] // 2
    return lax.dynamic_slice_in_dim(value, links.core * span, span, 1)


def both_halves(links, mine, theirs):
    even = links.core == 0
    return jnp.concatenate(
        [jnp.where(even, mine, theirs), jnp.where(even, theirs, mine)], axis=1
    ).astype(f32)


def dot(left, right):
    return jnp.dot(left, right, preferred_element_type=f32)


def dot_rows(left, right):
    return lax.dot_general(left, right, (((1,), (1,)), ((), ())), preferred_element_type=f32)


def turned(value):
    return jnp.transpose(value)


def aligned(start, size, unit):
    return pl.ds(pl.multiple_of(start, unit), size)


SMEM = pl.BlockSpec(memory_space=pltpu.SMEM)
ANY = pl.BlockSpec(memory_space=pl.ANY)
VMEM = pl.BlockSpec(memory_space=pltpu.VMEM)


def cost(microseconds):
    return pl.CostEstimate(
        flops=int(microseconds * FLOPS), transcendentals=0, bytes_accessed=int(microseconds * BYTES)
    )


def call(body, name, sources, in_specs, outs, scratch=(), time=5):
    return pl.pallas_call(
        body,
        name=name,
        out_shape=outs,
        in_specs=in_specs,
        out_specs=[VMEM] * len(outs),
        scratch_shapes=list(scratch),
        compiler_params=pltpu.CompilerParams(vmem_limit_bytes=VMEM_BYTES),
        cost_estimate=cost(time),
    )(*sources)


def shape(rows, columns, dtype):
    return jax.ShapeDtypeStruct((rows, columns), dtype)


class Piece:
    def __init__(self, dp, rows, columns, first):
        self.dp, self.rows, self.columns, self.first = dp, rows, columns, first

    def fetch(self, scalar, sides, whole, sem):
        core = scalar[4 * self.dp]
        for side, sources in enumerate(sides):
            half = core if side == 0 else 1 - core
            count = self.dp // len(sources)
            for i, source in enumerate(sources):

                def one(position, carry, side=side, source=source, half=half, base=i * count):
                    owner = scalar[side * self.dp + base + position]
                    pltpu.make_async_copy(
                        source.at[
                            aligned(position * self.rows, self.rows, 8),
                            pl.ds(self.first, self.columns),
                        ],
                        whole.at[
                            aligned(owner * self.rows, self.rows, 8),
                            aligned(half * self.columns, self.columns, LANES),
                        ],
                        sem,
                    ).start()
                    return carry

                lax.fori_loop(0, count, one, 0)

    def fetch_side(self, scalar, side, sources, whole, sem):
        count = self.dp // len(sources)
        for i, source in enumerate(sources):

            def one(position, carry, source=source, base=i * count):
                owner = scalar[side * self.dp + base + position]
                pltpu.make_async_copy(
                    source.at[
                        aligned(position * self.rows, self.rows, 8),
                        pl.ds(self.first, self.columns),
                    ],
                    whole.at[aligned(owner * self.rows, self.rows, 8), :],
                    sem,
                ).start()
                return carry

            lax.fori_loop(0, count, one, 0)

    def fetch_rows(self, scalar, part, sides, whole, sem):
        core = scalar[4 * self.dp]
        for side, sources in enumerate(sides):
            half = core if side == 0 else 1 - core
            count = self.dp // len(sources)

            def one(i, carry, side=side, sources=sources, half=half, count=count):
                spot = scalar[(2 + side) * self.dp + part * (self.dp // 2) + i]
                for j, source in enumerate(sources):

                    @pl.when(spot // count == j)
                    def _(source=source, j=j):
                        pltpu.make_async_copy(
                            source.at[
                                aligned((spot - j * count) * self.rows, self.rows, 8),
                                pl.ds(self.first, self.columns),
                            ],
                            whole.at[
                                aligned(i * self.rows, self.rows, 8),
                                aligned(half * self.columns, self.columns, LANES),
                            ],
                            sem,
                        ).start()

                return carry

            lax.fori_loop(0, self.dp // 2, one, 0)

    def ready(self, whole, sem):
        pltpu.make_async_copy(whole, whole, sem).wait()

    def whole(self):
        return pltpu.VMEM((self.dp * self.rows, 2 * self.columns), bf16)


def place(scalar, dp, tile, outs, rows, columns):
    base = 0
    for out in outs:
        count = out.shape[0] // rows

        def one(i, carry, out=out, base=base):
            owner = scalar[base + i]
            out[aligned(i * rows, rows, 8), columns] = tile[aligned(owner * rows, rows, 8), :].astype(
                bf16
            )
            return carry

        lax.fori_loop(0, count, one, 0)
        base += count


def placed(dp, rows, columns):
    return [
        shape(rows * dp // 4, columns, bf16),
        shape(rows * dp // 4, columns, bf16),
        shape(rows * dp // 2, columns, bf16),
    ]


def in_hbm(*dims):
    *dims, dtype = dims
    return pltpu.HBM(tuple(dims), dtype)


def sides(refs):
    return (refs[:2], refs[2:4])


def far(value):
    return pltpu.with_memory_space_constraint(value, pltpu.HBM)


def flat(gathered):
    return [far(value) for value in (*gathered[0], *gathered[1])]


def project(links, table, rows, gathered, qkv_piece, vector_piece, scale, base, folds):
    tokens, width = rows.shape
    shard = width // links.dp

    def body(scalar, rows_ref, *refs):
        q_ref, kv_ref, vec_ref, bias_ref, rows_t_ref, weight, vecs, sems = refs[4:]
        pieces = sides(refs)
        vector_piece.fetch_side(scalar, 0, pieces[0], vecs, sems.at[1])
        qkv_piece.fetch(scalar, pieces, weight, sems.at[0])
        vector_piece.ready(vecs, sems.at[1])
        vectors = turned(vecs[...].astype(f32))[:VECTORS]
        vec_ref[...] = vectors
        bias_ref[...] = jnp.concatenate(
            [
                vectors[base + j : base + j + 1, i * shard : (i + 1) * shard]
                for i in range(links.dp)
                for j in range(folds)
            ],
            axis=1,
        )
        rows_t_ref[...] = turned(rows_ref[...])
        qkv_piece.ready(weight, sems.at[0])
        x = rows_ref[...]
        query = (dot(x, weight[:, :width]) + vectors[0:1]).astype(bf16)
        q_ref[...] = (query.astype(f32) * scale).astype(bf16)
        kv_ref[:, :width] = dot(x, weight[:, width : 2 * width]).astype(bf16)
        kv_ref[:, width:] = (dot(x, weight[:, 2 * width :]) + vectors[1:2]).astype(bf16)

    return call(
        body,
        "qkv",
        [table, rows, *flat(gathered)],
        [SMEM, VMEM] + [ANY] * 4,
        [
            shape(tokens, width, bf16),
            shape(tokens, 2 * width, bf16),
            shape(VECTORS, width, f32),
            shape(1, folds * width, f32),
            shape(width, tokens, bf16),
        ],
        [qkv_piece.whole(), pltpu.VMEM((width, LANES), bf16), pltpu.SemaphoreType.DMA((2,))],
        time=5,
    )


def pair_specs(parts, pairs, base):
    specs = []
    for part in parts:
        rows = part.shape[0]
        specs.append(pl.BlockSpec((rows, LANES), lambda p, s: (0, base + p)))
        specs.append(pl.BlockSpec((rows, LANES), lambda p, s: (0, pairs + base + p)))
    return specs


def first_lanes(shape_, count):
    return (lax.broadcasted_iota(jnp.int32, shape_, 1) < count).astype(f32).astype(bf16)


def head_blocks(query):
    lane = lax.broadcasted_iota(jnp.int32, query.shape, 1)
    zero = jnp.zeros_like(query)
    half = LANES // 2
    return jnp.concatenate(
        [jnp.where(lane < half, query, zero), jnp.where(lane >= half, query, zero)], axis=0
    )


def attend(query, parts, starts, length, base, count):
    tokens, width = query.shape
    pairs = width // LANES
    span = sum(part.shape[0] for part in parts)
    half = LANES // 2
    chunk = min(256, tokens)
    scalars = jnp.concatenate(
        [jnp.reshape(v, (1,)).astype(jnp.int32) for v in [length, *starts]]
    )

    def body(scalar, q_ref, *refs):
        kv_refs = refs[: 2 * len(parts)]
        mixed_t_ref, mixed_ref, p_ref, inverse_ref, bias = refs[2 * len(parts) :]

        @pl.when(pl.program_id(0) == 0)
        def _():
            at = 0
            for i, part in enumerate(parts):
                rows = part.shape[0]
                position = scalar[1 + i] + lax.broadcasted_iota(jnp.int32, (rows, LANES), 0)
                lane = lax.broadcasted_iota(jnp.int32, (rows, LANES), 1)
                hidden = jnp.where(position < scalar[0], 0.0, masked_score)
                bias[at : at + rows, :] = jnp.where(lane == 0, hidden, 0.0).astype(bf16)
                at += rows

        keys = jnp.concatenate([ref[...] for ref in kv_refs[0::2]], axis=0)
        values = jnp.concatenate([ref[...] for ref in kv_refs[1::2]], axis=0)
        keys = jnp.concatenate([keys, bias[...]], axis=1)
        values_t = jnp.concatenate([turned(values), jnp.ones((16, span), bf16)], axis=0)
        queries = head_blocks(q_ref[...])
        queries = jnp.concatenate([queries, first_lanes(queries.shape, 1)], axis=1)
        for at in range(0, 2 * tokens, chunk):
            scores = dot_rows(keys, queries[at : at + chunk])
            peak = jnp.max(scores, axis=0, keepdims=True)
            weights = jnp.exp(scores - peak).astype(bf16)
            p_ref[:, at : at + chunk] = weights
            sums = dot(values_t, weights)
            inverse = 1.0 / sums[LANES : LANES + 1]
            inverse_ref[:, at : at + chunk] = inverse
            low = 0 if at < tokens else half
            to = at % tokens
            mixed_t_ref[low : low + half, to : to + chunk] = sums[low : low + half] * inverse
        mixed_ref[...] = turned(mixed_t_ref[...]).astype(bf16)

    sources = [query]
    for part in parts:
        sources += [part, part]
    return pl.pallas_call(
        body,
        name="attend",
        cost_estimate=cost(8),
        out_shape=[
            in_hbm(count * LANES, tokens, f32),
            shape(tokens, count * LANES, bf16),
            in_hbm(count, span, 2 * tokens, bf16),
            in_hbm(count, 1, 2 * tokens, f32),
        ],
        grid_spec=pltpu.PrefetchScalarGridSpec(
            num_scalar_prefetch=1,
            grid=(count,),
            in_specs=[pl.BlockSpec((tokens, LANES), lambda p, s: (0, base + p))]
            + pair_specs(parts, pairs, base),
            out_specs=[
                pl.BlockSpec((LANES, tokens), lambda p, s: (p, 0)),
                pl.BlockSpec((tokens, LANES), lambda p, s: (0, p)),
                pl.BlockSpec((None, span, 2 * tokens), lambda p, s: (p, 0, 0)),
                pl.BlockSpec((None, 1, 2 * tokens), lambda p, s: (p, 0, 0)),
            ],
            scratch_shapes=[pltpu.VMEM((span, LANES), bf16)],
        ),
        compiler_params=pltpu.CompilerParams(vmem_limit_bytes=min(56 << 20, VMEM_BYTES * max(1, span // 1024))),
    )(scalars, *sources)


def attend_back(query, parts, grad_mixed, mixed_t, weights, inverse, scale, base, core):
    tokens, width = query.shape
    pairs = width // LANES
    span = sum(part.shape[0] for part in parts)
    half = LANES // 2
    chunk = min(256, tokens)

    def body(_, q_ref, gm_ref, mt_ref, p_ref, inv_ref, *refs):
        kv_refs = refs[: 2 * len(parts)]
        send_ref, keep_ref, ds_ref = refs[2 * len(parts) :]
        keys = jnp.concatenate([ref[...] for ref in kv_refs[0::2]], axis=0)
        values = jnp.concatenate([ref[...] for ref in kv_refs[1::2]], axis=0)
        grads = turned(gm_ref[...].astype(f32))
        inv = inv_ref[...]
        product = grads * mt_ref[...]
        empty = jnp.zeros((half, tokens), bf16)
        even, odd = inv[:, :tokens], inv[:, tokens:]
        delta = jnp.concatenate(
            [
                jnp.sum(product[:half], axis=0, keepdims=True) * even,
                jnp.sum(product[half:], axis=0, keepdims=True) * odd,
            ],
            axis=1,
        )
        top = jnp.concatenate([(grads[:half] * even).astype(bf16), empty], axis=1)
        bottom = jnp.concatenate([empty, (grads[half:] * odd).astype(bf16)], axis=1)
        scaled = jnp.concatenate([top, bottom], axis=0)
        first = (-delta).astype(bf16).astype(f32)
        second = (-delta - first).astype(bf16).astype(f32)
        third = (-delta - first - second).astype(bf16).astype(f32)
        row = lax.broadcasted_iota(jnp.int32, (LANES, 2 * tokens), 0)
        limbs = jnp.where(
            row == 0, first, jnp.where(row == 1, second, jnp.where(row == 2, third, 0.0))
        ).astype(bf16)
        right = jnp.concatenate([scaled, limbs], axis=0)
        left = jnp.concatenate([values, first_lanes(values.shape, 3)], axis=1)
        for at in range(0, 2 * tokens, chunk):
            grad_probs = dot(left, right[:, at : at + chunk])
            ds_ref[:, at : at + chunk] = (
                p_ref[:, at : at + chunk].astype(f32) * grad_probs
            ).astype(bf16)
        grad_scores = ds_ref[...]
        turned_grad = dot(turned(keys), grad_scores)
        grad_query = (
            turned(
                jnp.concatenate([turned_grad[:half, :tokens], turned_grad[half:, tokens:]], axis=0)
            )
            * scale
        ).astype(bf16)
        grad_keys = dot(grad_scores, head_blocks(q_ref[...])).astype(bf16)
        grad_values = dot_rows(p_ref[...], scaled).astype(bf16)
        pieces = [grad_query]
        at = 0
        for part in parts:
            rows = part.shape[0]
            pieces += [grad_keys[at : at + rows], grad_values[at : at + rows]]
            at += rows

        def write(ref, values_, start):
            for value in values_:
                ref[start : start + value.shape[0], :] = value
                start += value.shape[0]

        @pl.when(pl.program_id(0) == 0)
        def _():
            write(send_ref, pieces, 0)

        @pl.when(pl.program_id(0) == 1)
        def _():
            write(keep_ref, pieces[:3], 0)
            write(send_ref, pieces[3:], 5 * tokens)

    local = lambda p, s: (1 - p) * (1 - s[0]) + p * s[0]
    offset = lambda p, s: (0, base + local(p, s))
    sources = [query, grad_mixed, far(mixed_t), far(weights), far(inverse)]
    in_specs = [
        pl.BlockSpec((tokens, LANES), offset),
        pl.BlockSpec((tokens, LANES), offset),
        pl.BlockSpec((LANES, tokens), lambda p, s: (local(p, s), 0)),
        pl.BlockSpec((None, span, 2 * tokens), lambda p, s: (local(p, s), 0, 0)),
        pl.BlockSpec((None, 1, 2 * tokens), lambda p, s: (local(p, s), 0, 0)),
    ]
    for part in parts:
        sources += [part, part]
        rows = part.shape[0]
        in_specs.append(pl.BlockSpec((rows, LANES), offset))
        in_specs.append(pl.BlockSpec((rows, LANES), lambda p, s: (0, pairs + base + local(p, s))))
    kept = tokens + 2 * parts[0].shape[0]
    sent = 7 * tokens if len(parts) == 2 else kept
    return pl.pallas_call(
        body,
        name="attend_back",
        cost_estimate=cost(5),
        out_shape=[shape(sent, LANES, bf16), shape(kept, LANES, bf16)],
        grid_spec=pltpu.PrefetchScalarGridSpec(
            num_scalar_prefetch=1,
            grid=(2,),
            in_specs=in_specs,
            out_specs=[
                pl.BlockSpec((sent, LANES), lambda p, s: (0, 0)),
                pl.BlockSpec((kept, LANES), lambda p, s: (0, 0)),
            ],
            scratch_shapes=[pltpu.VMEM((span, 2 * tokens), bf16)],
        ),
        compiler_params=pltpu.CompilerParams(
            vmem_limit_bytes=min(56 << 20, VMEM_BYTES * max(1, span // 1024))
        ),
    )(jnp.reshape(core, (1,)).astype(jnp.int32), *sources)


def normalize(resid):
    center = resid - jnp.mean(resid, axis=1, keepdims=True)
    inverse = lax.rsqrt(jnp.mean(center * center, axis=1, keepdims=True) + norm_eps)
    return center * inverse, inverse


def norm_back(grads, normal, inverse, gain):
    scaled = grads * gain
    return inverse * (
        scaled
        - jnp.mean(scaled, axis=1, keepdims=True)
        - normal * jnp.mean(scaled * normal, axis=1, keepdims=True)
    )


def column_sums(value):
    return jnp.sum(value, axis=0, keepdims=True)


def masked_total(value, valid, width):
    lanes = column_sums(jnp.where(valid, value * value, 0.0))
    return jnp.broadcast_to(jnp.sum(lanes, axis=1, keepdims=True), (1, width))


def valid_rows(scalar, at, tokens):
    position = scalar[at + 1] + lax.broadcasted_iota(jnp.int32, (tokens, 1), 0)
    return position < scalar[at]


def after_attention(links, table, rows, mixed, vectors, gathered, out_piece):
    tokens, width = rows.shape
    extra = 4 * links.dp + 1
    count = len(mixed)
    part = width // count

    def body(scalar, rows_ref, vec_ref, *refs):
        mixed_refs = refs[:count]
        pieces = sides(refs[count:])
        hidden_ref, low_ref, low_t_ref, mixed_t_ref = refs[count + 4 : count + 8]
        normal_ref, inverse_ref, sums_ref, weight, sem = refs[count + 8 :]
        out_piece.fetch(scalar, pieces, weight, sem.at[0])
        x = rows_ref[...].astype(f32)
        valid = valid_rows(scalar, extra, tokens)
        sums_ref[0:1, :] = masked_total(x, valid, width)
        rows_there = jnp.sum(valid.astype(f32), axis=0, keepdims=True)
        sums_ref[2:3, :] = jnp.broadcast_to(rows_there, (1, width))
        out_piece.ready(weight, sem.at[0])
        branch = vec_ref[2:3]
        for i, ref in enumerate(mixed_refs):
            branch = branch + dot(ref[...], weight[i * part : (i + 1) * part, :])
        sums_ref[1:2, :] = masked_total(branch, valid, width)
        normal, inverse = normalize(x + branch)
        hidden = normal * vec_ref[3:4] + vec_ref[4:5]
        normal_ref[...] = normal
        inverse_ref[...] = inverse
        hidden_ref[...] = hidden
        low = hidden.astype(bf16)
        low_ref[...] = low
        low_t_ref[...] = turned(low)
        for i, ref in enumerate(mixed_refs):
            mixed_t_ref[i * part : (i + 1) * part, :] = turned(ref[...])

    return call(
        body,
        "after_attention",
        [table, rows, vectors, *mixed, *flat(gathered)],
        [SMEM] + [VMEM] * (2 + count) + [ANY] * 4,
        [
            shape(tokens, width, f32),
            shape(tokens, width, bf16),
            shape(width, tokens, bf16),
            shape(width, tokens, bf16),
            shape(tokens, width, f32),
            shape(tokens, 1, f32),
            shape(3, width, f32),
        ],
        [out_piece.whole(), pltpu.SemaphoreType.DMA((1,))],
        time=3.5,
    )


def gelu_and_slope(u):
    phi = 0.5 * lax.erf(u * math.sqrt(0.5)) + 0.5
    bell = jnp.exp(-0.5 * (u * u)) * (1.0 / math.sqrt(2.0 * math.pi))
    return u * phi, phi + u * bell


def feed_up(links, table, low, up_bias, gathered, up_piece):
    tokens, width = low.shape
    inner = up_bias.shape[1]

    def body(scalar, low_ref, bias_ref, *refs):
        act_ref, act_t_ref, slope_ref, weight, sem = refs[4:]
        up_piece.fetch(scalar, sides(refs), weight, sem.at[0])
        up_piece.ready(weight, sem.at[0])

        def forward(j, carry):
            at = aligned(j * width, width, LANES)
            value, slope = gelu_and_slope(dot(low_ref[...], weight[:, at]) + bias_ref[:, at])
            value = value.astype(bf16)
            act_ref[:, at] = value
            act_t_ref[at, :] = turned(value)
            slope_ref[:, at] = slope.astype(bf16)
            return carry

        lax.fori_loop(0, inner // width, forward, 0)

    return call(
        body,
        "feed_up",
        [table, low, up_bias, *flat(gathered)],
        [SMEM] + [VMEM] * 2 + [ANY] * 4,
        [
            shape(tokens, inner, bf16),
            shape(inner, tokens, bf16),
            shape(tokens, inner, bf16),
        ],
        [up_piece.whole(), pltpu.SemaphoreType.DMA((1,))],
        time=8,
    )


def share(core, value, keep_ref, send_ref):
    span = value.shape[1] // 2
    low, high = value[:, :span], value[:, span:]
    even = core == 0
    keep_ref[...] = jnp.where(even, low, high)
    send_ref[...] = jnp.where(even, high, low)


def feed_down(links, table, act, hidden, vectors, cotangent, gathered, down_piece):
    tokens, width = hidden.shape
    inner = act.shape[1]
    extra = 4 * links.dp + 1
    dp = links.dp

    def body(scalar, act_ref, hidden_ref, vec_ref, cot_ref, *refs):
        out_ref, resid_ref, grad_ref, keep_ref, send_ref, sums_ref, weight, sem = refs[4:]
        down_piece.fetch(scalar, sides(refs), weight, sem.at[0])
        down_piece.ready(weight, sem.at[0])
        branch = dot(act_ref[...], weight[...]) + vec_ref[5:6]
        sums_ref[3:4, :] = masked_total(branch, valid_rows(scalar, extra, tokens), width)
        normal, inverse = normalize(hidden_ref[...] + branch)
        out_ref[...] = (normal * vec_ref[6:7] + vec_ref[7:8]).astype(bf16)
        grads = cot_ref[...].astype(f32)
        sums_ref[1:2, :] = column_sums(grads * normal)
        sums_ref[2:3, :] = column_sums(grads)
        resid = norm_back(grads, normal, inverse, vec_ref[6:7])
        resid_ref[...] = resid
        grad_ffn = resid.astype(bf16)
        grad_ref[...] = grad_ffn
        sums_ref[0:1, :] = column_sums(grad_ffn.astype(f32))
        share(scalar[4 * dp], grad_ffn, keep_ref, send_ref)

    return call(
        body,
        "feed_down",
        [table, act, hidden, vectors, cotangent, *flat(gathered)],
        [SMEM] + [VMEM] * 4 + [ANY] * 4,
        [
            shape(tokens, width, bf16),
            shape(tokens, width, f32),
            shape(tokens, width, bf16),
            shape(tokens, width // 2, bf16),
            shape(tokens, width // 2, bf16),
            shape(4, width, f32),
        ],
        [down_piece.whole(), pltpu.SemaphoreType.DMA((1,))],
        time=6,
    )


def feed_back(links, table, side, slope, so_far, grad_ffn, up, down, pieces):
    tokens, width = so_far.shape
    up_piece, down_piece = pieces
    span = up_piece.columns
    block = width if span % width == 0 else span
    dp = links.dp

    def body(scalar, slope_ref, so_far_ref, grad_ref, um, ul, *refs):
        hidden_ref, out_ref, bias_ref, up_w, down_w, sems = refs[4:]
        core = scalar[4 * dp]
        half = core if side == 0 else 1 - core
        down_piece.fetch_rows(scalar, half, sides(refs), down_w, sems.at[1])
        up_piece.fetch_side(scalar, side, (um, ul), up_w, sems.at[0])
        hidden_ref[...] = so_far_ref[...]
        down_piece.ready(down_w, sems.at[1])
        up_piece.ready(up_w, sems.at[0])

        def backward(j, carry):
            here = aligned(j * block, block, LANES)
            at = aligned(half * span + j * block, block, LANES)
            grads = dot_rows(grad_ref[...], down_w[here, :]) * slope_ref[:, at].astype(f32)
            grads = grads.astype(bf16)
            bias_ref[:, here] = column_sums(grads.astype(f32))
            hidden_ref[...] += dot_rows(grads, up_w[:, here])
            out_ref[:, here] = grads
            return carry

        lax.fori_loop(0, span // block, backward, 0)

    return call(
        body,
        "feed_back",
        [table, slope, so_far, grad_ffn, *map(far, up[side]), *flat(down)],
        [SMEM] + [VMEM] * 3 + [ANY] * 6,
        [shape(tokens, width, f32), shape(tokens, span, bf16), shape(1, span, f32)],
        [
            pltpu.VMEM((width, span), bf16),
            pltpu.VMEM((span, width), bf16),
            pltpu.SemaphoreType.DMA((2,)),
        ],
        time=6,
    )


def before_attention(links, table, grad_hidden, normal, inverse, vectors, gathered, piece):
    tokens, width = normal.shape

    def body(scalar, grad_ref, normal_ref, inverse_ref, vec_ref, *refs):
        resid_ref, gm_ref, keep_ref, send_ref, sums_ref, weight, sem = refs[4:]
        piece.fetch(scalar, sides(refs), weight, sem.at[0])
        grads = grad_ref[...]
        normal_ = normal_ref[...]
        sums_ref[1:2, :] = column_sums(grads * normal_)
        sums_ref[2:3, :] = column_sums(grads)
        resid = norm_back(grads, normal_, inverse_ref[...], vec_ref[3:4])
        resid_ref[...] = resid
        grad_attn = resid.astype(bf16)
        sums_ref[0:1, :] = column_sums(grad_attn.astype(f32))
        piece.ready(weight, sem.at[0])
        gm_ref[...] = dot_rows(grad_attn, weight[...]).astype(bf16)
        share(scalar[4 * links.dp], grad_attn, keep_ref, send_ref)

    return call(
        body,
        "before_attention",
        [table, grad_hidden, normal, inverse, vectors, *flat(gathered)],
        [SMEM] + [VMEM] * 4 + [ANY] * 4,
        [
            shape(tokens, width, f32),
            shape(tokens, width, bf16),
            shape(tokens, width // 2, bf16),
            shape(tokens, width // 2, bf16),
            shape(3, width, f32),
        ],
        [piece.whole(), pltpu.SemaphoreType.DMA((1,))],
        time=0.01,
    )


def weight_gradient(name, links, table, left, right, rows):
    outer, tokens = left[0].shape
    columns = right[0].shape[1]
    block = min(outer, 768)

    def body(scalar, lm, lt, rm, rt, *refs):
        tile = refs[-1]

        def one(j, carry):
            at = aligned(j * block, block, 8)
            tile[at, :] = dot(lm[at, :], rm[...]) + dot(lt[at, :], rt[...])
            return carry

        lax.fori_loop(0, outer // block, one, 0)
        place(scalar, links.dp, tile, refs[:3], rows, slice(None))

    return call(
        body,
        name,
        [table, *left, *right],
        [SMEM] + [VMEM] * 4,
        placed(links.dp, rows, columns),
        [pltpu.VMEM((outer, columns), f32)],
    )


class Shares:
    def __init__(self, refs, tokens):
        self.sent, self.kept, self.came = refs
        self.tokens = tokens

    def rows(self, ref, i):
        return ref[i * self.tokens : (i + 1) * self.tokens, :]

    def add(self, one, other):
        return (one.astype(f32) + other.astype(f32)).astype(bf16)

    def own(self):
        return [self.rows(self.kept, 0)] + [
            self.add(self.rows(self.kept, i), self.rows(self.came, 2 + i)) for i in (1, 2)
        ]

    def others(self):
        return [self.rows(self.came, 0)] + [
            self.add(self.rows(self.sent, 4 + i), self.rows(self.came, i)) for i in (1, 2)
        ]

    def partners(self):
        return [self.rows(self.sent, 0)] + [
            self.add(self.rows(self.sent, i), self.rows(self.came, 4 + i)) for i in (1, 2)
        ]


def attention_gradient(name, links, table, rows_t, groups, rows, out=None, vectors=None, folds=0, sums=()):
    width, tokens = rows_t[0].shape
    dp = links.dp
    wide = 3 * LANES
    half = width // 2
    total = wide * len(groups) + (half if out else 0) + (LANES if vectors is not None else 0)
    given = [value for group in groups for value in group]
    more = list(out or []) + ([*vectors, *sums] if vectors is not None else [])

    def body(scalar, xm, xt, *refs):
        group_refs = refs[: len(given)]
        more_refs = list(refs[len(given) : len(given) + len(more)])
        outs = refs[len(given) + len(more) :]
        sum_ref, tile = outs[3], outs[4]
        for g in range(len(groups)):
            shares = Shares(group_refs[3 * g : 3 * g + 3], tokens)
            mine = jnp.concatenate(shares.own(), axis=1)
            theirs = jnp.concatenate(shares.others(), axis=1)
            tile[:, g * wide : (g + 1) * wide] = dot(xm[...], mine) + dot(xt[...], theirs)
            sums_ = column_sums(mine.astype(f32)) + column_sums(theirs.astype(f32))
            sum_ref[g : g + 1, :] = sums_
        at = wide * len(groups)
        if out:
            mm, mt, gm, gt = more_refs[:4]
            tile[:, at : at + half] = dot(mm[...], gm[...]) + dot(mt[...], gt[...])
            at += half
        if vectors is not None:
            sums3, sums2, kept, sent, sums1, *sum_refs = more_refs
            even = scalar[4 * dp] == 0
            bias = jnp.concatenate(
                [
                    jnp.where(even, kept[...], sent[...]),
                    jnp.where(even, sent[...], kept[...]),
                ],
                axis=1,
            )
            biases = [
                jnp.concatenate(
                    [
                        bias[:, (i * folds + j) * rows : (i * folds + j + 1) * rows]
                        for i in range(dp)
                    ],
                    axis=1,
                )
                for j in range(folds)
            ]
            head = jnp.concatenate(
                [jnp.zeros((2, width), f32), sums3[...], sums2[0:3]]
                + biases
                + [sums1[...], sums2[3:4]],
                axis=0,
            )
            every = [ref[i : i + 1, :] for ref in sum_refs for i in range(ref.shape[0])]
            every += [sum_ref[g : g + 1, :] for g in range(len(groups))]
            lane = lax.broadcasted_iota(jnp.int32, (1, width), 1)
            owned = (lane // LANES) % 2 == scalar[4 * dp]
            lines = []
            for j in (0, 2):
                parts = [s[:, j * LANES : (j + 1) * LANES] for s in every for _ in range(2)]
                lines.append(jnp.where(owned, jnp.concatenate(parts, axis=1), 0.0))
            row = lax.broadcasted_iota(jnp.int32, (LANES, width), 0)
            padded = jnp.concatenate(
                [head, jnp.zeros((LANES - head.shape[0], width), f32)], axis=0
            )
            padded = jnp.where(row == 0, lines[0], jnp.where(row == 1, lines[1], padded))
            tile[:, at : at + LANES] = turned(padded)
        place(scalar, dp, tile, outs[:3], rows, slice(None))

    return call(
        body,
        name,
        [table, *rows_t, *given, *more],
        [SMEM] + [VMEM] * (2 + len(given) + len(more)),
        placed(dp, rows, total) + [shape(len(groups), wide, f32)],
        [pltpu.VMEM((width, total), f32)],
    )


def input_gradient(links, table, groups, resid, gathered, qkv_piece):
    tokens, width = resid.shape
    given = [value for group in groups for value in group]

    def body(scalar, resid_ref, *refs):
        group_refs = refs[: len(given)]
        out_ref, weight, grads, sem = refs[len(given) + 4 :]
        qkv_piece.fetch(scalar, sides(refs[len(given) :]), weight, sem.at[0])
        core = scalar[4 * links.dp]
        for g in range(len(groups)):
            shares = Shares(group_refs[3 * g : 3 * g + 3], tokens)
            for owner, values in ((core, shares.own()), (1 - core, shares.partners())):
                for j, value in enumerate(values):
                    at = j * width + (2 * g + owner) * LANES
                    grads[:, aligned(at, LANES, LANES)] = value
        qkv_piece.ready(weight, sem.at[0])
        out_ref[...] = resid_ref[...] + dot_rows(grads[...], weight[...])

    return call(
        body,
        "input_gradient",
        [table, resid, *given, *flat(gathered)],
        [SMEM] + [VMEM] * (1 + len(given)) + [ANY] * 4,
        [shape(tokens, width, f32)],
        [qkv_piece.whole(), pltpu.VMEM((tokens, 3 * width), bf16), pltpu.SemaphoreType.DMA((1,))],
        time=20,
    )[0]


def closing(links, table, early, late, folds, width):
    rows = early[0].shape[0]
    wide = 3 * LANES
    half = width // 2
    base = 8

    def body(scalar, em, et, lm, lt, *outs):
        qkv_ref, out_ref, *vec_refs, up_ref, rms_ref = outs

        def write(core):
            for owner, early_ref, late_ref in ((core, em, lm), (1 - core, et, lt)):
                groups = [(early_ref, 0), (early_ref, wide), (late_ref, 0)]
                for g, (ref, first) in enumerate(groups):
                    for j in range(3):
                        at = j * width + (2 * g + owner) * LANES
                        qkv_ref[:, at : at + LANES] = ref[
                            :, first + j * LANES : first + (j + 1) * LANES
                        ].astype(f32)
                out_ref[:, owner * half : (owner + 1) * half] = early_ref[
                    :, 2 * wide : 2 * wide + half
                ].astype(f32)

        for core in range(2):
            pl.when(scalar[4 * links.dp] == core)(lambda core=core: write(core))
        last = slice(wide, wide + LANES)
        vectors = turned(lm[:, last].astype(f32) + lt[:, last].astype(f32))
        for i, ref in enumerate(vec_refs):
            ref[...] = vectors[i : i + 1]
        for i in range(folds):
            up_ref[:, i * rows : (i + 1) * rows] = vectors[base + i : base + i + 1]
        at = base + folds
        count = vectors[at + 2 : at + 3] * width
        for i, line in enumerate((at, at + 1, at + 3)):
            value = jnp.sqrt(vectors[line : line + 1] / count + 1e-06)
            rms_ref[:, i : i + 1] = value[:, 0:1]

    return call(
        body,
        "closing",
        [table, *early, *late],
        [SMEM] + [VMEM] * 4,
        [shape(rows, 3 * width, f32), shape(rows, width, f32)]
        + [shape(1, rows, f32)] * base
        + [shape(1, folds * rows, f32), shape(1, 3, f32)],
    )


def settle(links, reduction):
    mine = reduction.finish()
    return mine, links.swap(mine)


def shards(
    tokens,
    lengths,
    qkv_weight,
    query_bias,
    value_bias,
    out_weight,
    out_bias,
    norm1_gain,
    norm1_shift,
    up_weight,
    up_bias,
    down_weight,
    down_bias,
    norm2_gain,
    norm2_shift,
    cotangent,
):
    seq_dev, ctx_tok, width = tokens.shape
    assert seq_dev == 1 and width // HEADS == LANES // 2
    scale = (width // HEADS) ** (-0.5)
    links = Links()
    dp = links.dp
    rows = tokens.reshape(ctx_tok, width)
    cot = cotangent.reshape(ctx_tok, width)
    block = lax.axis_index("ctx")
    start = block * ctx_tok
    table = links.table(lengths[0], start)

    shard = qkv_weight.shape[0]
    inner = down_weight.shape[0] * dp
    folds = down_weight.shape[0] // shard
    half = [w.shape[1] // 2 for w in (qkv_weight, out_weight, up_weight, down_weight)]
    qkv_piece = Piece(dp, shard, half[0], 0)
    vector_piece = Piece(dp, shard, LANES, half[0])
    up_piece = Piece(dp, shard, half[2], 0)
    out_piece = Piece(dp, shard, half[1], half[2])
    down_piece = Piece(dp, down_weight.shape[0], half[3], 0)
    ffn_pieces = (up_piece, down_piece)

    columns = [query_bias, value_bias, out_bias, norm1_gain, norm1_shift]
    columns += [down_bias, norm2_gain, norm2_shift]
    base = len(columns)
    columns += [up_bias[i * shard : (i + 1) * shard] for i in range(folds)]
    packed = jnp.stack(columns, axis=1)
    packed = jnp.pad(packed, ((0, 0), (0, LANES - packed.shape[1])))
    qkv_sent = jnp.concatenate([half_columns(links, qkv_weight), packed], axis=1)
    up_sent = jnp.concatenate(
        [half_columns(links, up_weight), half_columns(links, out_weight)], axis=1
    )
    down_sent = half_columns(links, down_weight)

    qkv_held = joined(links.cross(qkv_sent))
    up_held = links.cross(after(up_sent, qkv_held))
    down_sent = after(down_sent, up_held)
    qkv_held = links.first(qkv_held)
    qkv = links.second(after(qkv_held, up_held[1]), *up_held)
    up_held = after(joined(up_held), qkv[0][1])
    query, kv, vectors, up_bias_row, rows_t = project(
        links, table, after(rows, up_held), qkv, qkv_piece, vector_piece, scale, base, folds
    )
    down_held = joined(links.cross(after(down_sent, up_held)), query)
    kv = after(kv, down_held)
    rows_t = [rows_t, links.swap(rows_t)]
    if links.ctx == 2:
        parts = [kv, links.swap(kv)]
        starts = [start, (1 - block) * ctx_tok]
    else:
        parts = [lax.all_gather(kv, "ctx", axis=0, tiled=True)]
        starts = [jnp.int32(0)]
    groups = 3
    count = width // LANES // groups
    forward = []
    waits = [(), (), ()]
    for i in range(groups):
        given = after(query, *waits[i], *(forward[-1][1:2] if forward else ()))
        forward.append(attend(given, parts, starts, lengths[0], i * count, count))
        if i == 0:
            up_held = links.first(up_held, forward[0][1])
            waits[1] = (up_held,)
    up = links.second(up_held, forward[1][1])
    down_held = links.first(after(down_held, forward[1][1]), forward[2][1])
    mixed = [f[1] for f in forward]
    hidden, low, low_t, mixed_t, normal, deviation, sums1 = after_attention(
        links, table, after(rows, down_held), mixed, vectors, up, out_piece
    )
    down = links.second(after(down_held, forward[2][1]), hidden)
    low_t = [low_t, links.swap(low_t)]
    mixed_t = [mixed_t, links.swap(mixed_t)]
    act, act_t, slope = feed_up(links, table, low, up_bias_row, up, up_piece)
    act_t = [act_t, links.swap(act_t)]
    output, resid2, grad_ffn, ffn_keep, ffn_send, sums2 = feed_down(
        links, table, act, hidden, vectors, cot, down, down_piece
    )
    ffn_came = links.swap(ffn_send)
    grad_hidden, upper_send, bias_sent = feed_back(
        links, table, 1, slope, resid2, grad_ffn, up, down, ffn_pieces
    )
    upper_came = links.swap(upper_send)
    down_sum = Sum(
        links,
        weight_gradient(
            "down_gradient",
            links,
            table,
            [after(act_t[0], grad_hidden), act_t[1]],
            [ffn_keep, ffn_came],
            down_piece.rows,
        ),
    )
    given = after(grad_hidden, down_sum.prepare())
    down_sum.send()
    grad_hidden, upper_keep, bias_kept = feed_back(
        links, table, 0, slope, given, grad_ffn, up, down, ffn_pieces
    )
    up_sum = Sum(
        links,
        weight_gradient(
            "up_gradient", links, table, low_t, [upper_keep, upper_came], up_piece.rows
        ),
    )
    given = after(grad_hidden, up_sum.prepare())
    up_sum.send()
    resid1, grad_mixed, attn_keep, attn_send, sums3 = before_attention(
        links, table, given, normal, deviation, vectors, up, out_piece
    )
    out_parts = [*mixed_t, attn_keep, links.swap(attn_send)]

    def back_through(i, given):
        turned_mixed, _, weights, inverse = forward[i]
        sent, kept = attend_back(
            given,
            parts,
            grad_mixed,
            turned_mixed,
            weights,
            inverse,
            scale,
            i * count,
            links.core,
        )
        if links.ctx == 2:
            return [sent, kept, links.swap(sent)]
        whole = []
        for value in (sent, kept):
            keys, values = jnp.split(value[ctx_tok:], 2, axis=0)
            both = lax.psum_scatter(
                jnp.concatenate([keys, values], axis=1), "ctx", scatter_dimension=0, tiled=True
            )
            whole.append([value[:ctx_tok], both[:, :LANES], both[:, LANES:]])
        blank = jnp.zeros((4 * ctx_tok, LANES), bf16)
        sent = jnp.concatenate(whole[0] + [blank], axis=0)
        return [sent, jnp.concatenate(whole[1], axis=0), links.swap(sent)]

    down_sum.hold(grad_mixed)
    given = after(query, down_sum.prepare(), grad_mixed)
    down_sum.send()
    back = [back_through(0, given)]
    back.append(back_through(1, after(query, back[0][1])))
    down_sum.hold(back[1][1])
    given = after(rows_t[0], down_sum.prepare())
    down_sum.send()
    *early, early_sums = attention_gradient(
        "early_gradient", links, table, [given, rows_t[1]], back[:2], shard, out=out_parts
    )
    early_sum = Sum(links, early)
    up_sum.hold(early[2])
    given = after(query, early_sum.prepare(), up_sum.prepare())
    up_sum.send()
    early_sum.send()
    back.append(back_through(2, given))
    up_sum.hold(back[2][1])
    early_sum.hold(back[2][1])
    given = after(rows_t[0], up_sum.prepare(), early_sum.prepare())
    up_sum.send()
    early_sum.send()
    *late, _ = attention_gradient(
        "late_gradient",
        links,
        table,
        [given, rows_t[1]],
        back[2:],
        shard,
        vectors=[sums3, sums2, bias_kept, bias_sent, sums1],
        folds=folds,
        sums=[early_sums],
    )
    late_sum = Sum(links, late)
    down_sum.hold(late[2])
    down_mine = down_sum.finish()
    early_sum.hold(late[2])
    given = after(resid1, late_sum.prepare(), down_mine, early_sum.prepare())
    late_sum.send()
    early_sum.send()
    input_grad = input_gradient(links, table, back, given, qkv, qkv_piece)
    late_sum.hold(input_grad)
    up_sum.hold(input_grad)
    early_sum.hold(input_grad)
    down_grad = both_halves(links, down_mine, links.swap(down_mine))
    up_mine, up_theirs = settle(links, up_sum)
    up_grad = both_halves(links, up_mine, up_theirs)
    early = settle(links, early_sum)
    late = settle(links, late_sum)
    qkv_grad, out_grad, *sums, up_bias_grad, stream_rms = closing(
        links, table, early, late, folds, width
    )
    sums = [value.reshape(shard) for value in sums]
    return (
        output.reshape(seq_dev, ctx_tok, width),
        input_grad.reshape(seq_dev, ctx_tok, width),
        stream_rms.reshape(3),
        qkv_grad,
        sums[0],
        sums[1],
        out_grad,
        sums[2],
        sums[3],
        sums[4],
        up_grad,
        up_bias_grad.reshape(-1),
        down_grad,
        sums[5],
        sums[6],
        sums[7],
    )


def solution(mesh):
    in_specs = (
        P("dp", "ctx", None),
        P("dp"),
        P("dp", None),
        P("dp"),
        P("dp"),
        P("dp", None),
        P("dp"),
        P("dp"),
        P("dp"),
        P("dp", None),
        P("dp"),
        P("dp", None),
        P("dp"),
        P("dp"),
        P("dp"),
        P("dp", "ctx", None),
    )
    out_specs = (
        P("dp", "ctx", None),
        P("dp", "ctx", None),
        P(),
        P("dp", None),
        P("dp"),
        P("dp"),
        P("dp", None),
        P("dp"),
        P("dp"),
        P("dp"),
        P("dp", None),
        P("dp"),
        P("dp", None),
        P("dp"),
        P("dp"),
        P("dp"),
    )
    return jax.shard_map(shards, mesh=mesh, in_specs=in_specs, out_specs=out_specs, check_vma=False)
```

```python
import math

import jax
import jax.numpy as jnp
from jax import lax
from jax.experimental import pallas as pl
from jax.experimental.pallas import tpu as pltpu
from jax.sharding import PartitionSpec as P

HEADS = 12
LANES = 128
VECTORS = 16
VMEM_BYTES = 24 << 20
FLOPS = 400_000_000
BYTES = 1_200_000

masked_score = -1e30
norm_eps = 1e-05
f32 = jnp.float32
bf16 = jnp.bfloat16


def low_precision(value):
    return lax.reduce_precision(value, exponent_bits=8, mantissa_bits=7)


class Links:
    def __init__(self):
        self.dp = lax.axis_size("dp")
        self.ctx = lax.axis_size("ctx")
        self.bits = self.dp.bit_length() - 1
        assert self.dp == 1 << self.bits and self.bits >= 2 and self.ctx % 2 == 0
        self.core = lax.axis_index("ctx") % 2
        self.me = lax.axis_index("dp")
        self.upper = []
        bit = self.bits - 1
        while bit >= 2:
            size = 2 if (bit - 1) % 2 == 0 else 1
            self.upper.append(tuple(range(bit, bit - size, -1)))
            bit -= size

    def swap(self, value):
        return lax.ppermute(value, "ctx", [(i, i ^ 1) for i in range(self.ctx)])

    def hop(self, value, mask_even, mask_odd):
        pairs = []
        for block in range(self.ctx):
            mask = mask_odd if block % 2 else mask_even
            pairs += [(block * self.dp + i, block * self.dp + (i ^ mask)) for i in range(self.dp)]
        return lax.ppermute(value, ("ctx", "dp"), pairs)

    def places(self, core):
        position = lax.iota(jnp.int32, self.dp)
        quarter = self.dp // 4
        first = (position // quarter) % 2
        second = position // (2 * quarter)
        mask = first * (1 + core) + second * (2 - core)
        for i in range(self.bits - 2):
            mask = mask + ((position >> i) % 2) * (1 << (self.bits - 1 - i))
        return jnp.bitwise_xor(self.me, mask)

    def spots(self, core):
        mask = jnp.bitwise_xor(self.me, lax.iota(jnp.int32, self.dp))
        low, high = mask % 2, (mask // 2) % 2
        first = jnp.where(core == 0, low, high)
        second = jnp.where(core == 0, high, low)
        quarter = self.dp // 4
        spot = first * quarter + second * (2 * quarter)
        for i in range(self.bits - 2):
            spot = spot + ((mask >> (self.bits - 1 - i)) % 2) * (1 << i)
        return spot

    def table(self, *more):
        parts = [self.places(self.core), self.places(1 - self.core)]
        parts += [self.spots(self.core), self.spots(1 - self.core)]
        parts += [jnp.reshape(value, (1,)) for value in (self.core,) + more]
        return jnp.concatenate(parts).astype(jnp.int32)

    def masks(self, bits):
        return [
            sum(((i >> j) & 1) << bit for j, bit in enumerate(bits)) for i in range(1 << len(bits))
        ]

    def cross(self, piece):
        held = [piece]
        for bits in self.upper:
            here = jnp.concatenate(held, axis=0) if len(held) > 1 else held[0]
            held = [here] + [self.hop(here, mask, mask) for mask in self.masks(bits)[1:]]
        return held

    def first(self, held, *waits):
        more = self.hop(held, 1, 2)
        return jnp.concatenate([held, after(more, *waits) if waits else more], axis=0)

    def second(self, held, *waits):
        early = self.swap(held)
        more = self.hop(held, 2, 1)
        if waits:
            early, more = after((early, more), *waits)
        return [held, more], [early, self.swap(more)]


def joined(held, *waits):
    return jnp.concatenate(after(tuple(held), *waits) if waits else held, axis=0)


class Sum:
    def __init__(self, links, kept, direct=False):
        self.links = links
        self.kept = kept
        self.quarter = kept[0].shape[0]
        self.rows = 4 * self.quarter
        self.terms = []
        self.steps = [[(2, 1)], [(1, 2)]]
        for bits in reversed(links.upper):
            if direct:
                self.steps.append([(mask, mask) for mask in links.masks(bits)[1:]])
            else:
                self.steps += [[(1 << bit, 1 << bit)] for bit in reversed(bits)]
        self.ready = None

    def total(self, start, span):
        index = min(2, start // self.quarter)
        first = start - index * self.quarter
        value = self.kept[index]
        if span != value.shape[0]:
            value = lax.slice_in_dim(value, first, first + span, axis=0)
        if not self.terms:
            return value
        value = value.astype(f32)
        for term in self.terms:
            parts = [
                lax.slice_in_dim(part, start, start + span, axis=0).astype(f32) for part in term
            ]
            if len(parts) == 1:
                value = low_precision(value + parts[0])
            else:
                value = low_precision((value + parts[0]) + (parts[1] + parts[2]))
        return value.astype(bf16)

    def prepare(self):
        masks = self.steps[0]
        self.rows //= len(masks) + 1
        self.ready = [self.total((i + 1) * self.rows, self.rows) for i in range(len(masks))]
        return self.ready

    def send(self):
        if self.ready is None:
            self.prepare()
        masks = self.steps.pop(0)
        self.terms.append(
            tuple(self.links.hop(value, *mask) for value, mask in zip(self.ready, masks))
        )
        self.ready = None

    def hold(self, other):
        self.terms[-1] = tuple(after(value, other) for value in self.terms[-1])

    def finish(self):
        while self.steps:
            self.send()
        mine = self.total(0, self.rows)
        step = 2
        while step < self.links.ctx:
            pairs = [(i, i ^ step) for i in range(self.links.ctx)]
            other = lax.ppermute(mine, "ctx", pairs)
            mine = low_precision(mine.astype(f32) + other.astype(f32)).astype(bf16)
            step *= 2
        return mine


def after(value, *others):
    return lax.optimization_barrier((value, others))[0]


def half_columns(links, value):
    span = value.shape[1] // 2
    return lax.dynamic_slice_in_dim(value, links.core * span, span, 1)


def both_halves(links, mine, theirs):
    even = links.core == 0
    return jnp.concatenate(
        [jnp.where(even, mine, theirs), jnp.where(even, theirs, mine)], axis=1
    ).astype(f32)


def dot(left, right):
    return jnp.dot(left, right, preferred_element_type=f32)


def dot_rows(left, right):
    return lax.dot_general(left, right, (((1,), (1,)), ((), ())), preferred_element_type=f32)


def turned(value):
    return jnp.transpose(value)


def aligned(start, size, unit):
    return pl.ds(pl.multiple_of(start, unit), size)


SMEM = pl.BlockSpec(memory_space=pltpu.SMEM)
ANY = pl.BlockSpec(memory_space=pl.ANY)
VMEM = pl.BlockSpec(memory_space=pltpu.VMEM)


def cost(microseconds):
    return pl.CostEstimate(
        flops=int(microseconds * FLOPS), transcendentals=0, bytes_accessed=int(microseconds * BYTES)
    )


def call(body, name, sources, in_specs, outs, scratch=(), time=5):
    return pl.pallas_call(
        body,
        name=name,
        out_shape=outs,
        in_specs=in_specs,
        out_specs=[VMEM] * len(outs),
        scratch_shapes=list(scratch),
        compiler_params=pltpu.CompilerParams(vmem_limit_bytes=VMEM_BYTES),
        cost_estimate=cost(time),
    )(*sources)


def shape(rows, columns, dtype):
    return jax.ShapeDtypeStruct((rows, columns), dtype)


class Piece:
    def __init__(self, dp, rows, columns, first):
        self.dp, self.rows, self.columns, self.first = dp, rows, columns, first

    def fetch(self, scalar, sides, whole, sem):
        core = scalar[4 * self.dp]
        for side, sources in enumerate(sides):
            half = core if side == 0 else 1 - core
            count = self.dp // len(sources)
            for i, source in enumerate(sources):

                def one(position, carry, side=side, source=source, half=half, base=i * count):
                    owner = scalar[side * self.dp + base + position]
                    pltpu.make_async_copy(
                        source.at[
                            aligned(position * self.rows, self.rows, 8),
                            pl.ds(self.first, self.columns),
                        ],
                        whole.at[
                            aligned(owner * self.rows, self.rows, 8),
                            aligned(half * self.columns, self.columns, LANES),
                        ],
                        sem,
                    ).start()
                    return carry

                lax.fori_loop(0, count, one, 0)

    def fetch_side(self, scalar, side, sources, whole, sem):
        count = self.dp // len(sources)
        for i, source in enumerate(sources):

            def one(position, carry, source=source, base=i * count):
                owner = scalar[side * self.dp + base + position]
                pltpu.make_async_copy(
                    source.at[
                        aligned(position * self.rows, self.rows, 8),
                        pl.ds(self.first, self.columns),
                    ],
                    whole.at[aligned(owner * self.rows, self.rows, 8), :],
                    sem,
                ).start()
                return carry

            lax.fori_loop(0, count, one, 0)

    def fetch_rows(self, scalar, part, sides, whole, sem):
        core = scalar[4 * self.dp]
        for side, sources in enumerate(sides):
            half = core if side == 0 else 1 - core
            count = self.dp // len(sources)

            def one(i, carry, side=side, sources=sources, half=half, count=count):
                spot = scalar[(2 + side) * self.dp + part * (self.dp // 2) + i]
                for j, source in enumerate(sources):

                    @pl.when(spot // count == j)
                    def _(source=source, j=j):
                        pltpu.make_async_copy(
                            source.at[
                                aligned((spot - j * count) * self.rows, self.rows, 8),
                                pl.ds(self.first, self.columns),
                            ],
                            whole.at[
                                aligned(i * self.rows, self.rows, 8),
                                aligned(half * self.columns, self.columns, LANES),
                            ],
                            sem,
                        ).start()

                return carry

            lax.fori_loop(0, self.dp // 2, one, 0)

    def ready(self, whole, sem):
        pltpu.make_async_copy(whole, whole, sem).wait()

    def whole(self):
        return pltpu.VMEM((self.dp * self.rows, 2 * self.columns), bf16)


def place(scalar, dp, tile, outs, rows, columns):
    base = 0
    for out in outs:
        count = out.shape[0] // rows

        def one(i, carry, out=out, base=base):
            owner = scalar[base + i]
            out[aligned(i * rows, rows, 8), columns] = tile[aligned(owner * rows, rows, 8), :].astype(
                bf16
            )
            return carry

        lax.fori_loop(0, count, one, 0)
        base += count


def placed(dp, rows, columns):
    return [
        shape(rows * dp // 4, columns, bf16),
        shape(rows * dp // 4, columns, bf16),
        shape(rows * dp // 2, columns, bf16),
    ]


def in_hbm(*dims):
    *dims, dtype = dims
    return pltpu.HBM(tuple(dims), dtype)


def sides(refs):
    return (refs[:2], refs[2:4])


def far(value):
    return pltpu.with_memory_space_constraint(value, pltpu.HBM)


def flat(gathered):
    return [far(value) for value in (*gathered[0], *gathered[1])]


def project(links, table, rows, gathered, qkv_piece, vector_piece, scale, base, folds):
    tokens, width = rows.shape
    shard = width // links.dp

    def body(scalar, rows_ref, *refs):
        q_ref, kv_ref, vec_ref, bias_ref, rows_t_ref, weight, vecs, sems = refs[4:]
        pieces = sides(refs)
        vector_piece.fetch_side(scalar, 0, pieces[0], vecs, sems.at[1])
        qkv_piece.fetch(scalar, pieces, weight, sems.at[0])
        vector_piece.ready(vecs, sems.at[1])
        vectors = turned(vecs[...].astype(f32))[:VECTORS]
        vec_ref[...] = vectors
        bias_ref[...] = jnp.concatenate(
            [
                vectors[base + j : base + j + 1, i * shard : (i + 1) * shard]
                for i in range(links.dp)
                for j in range(folds)
            ],
            axis=1,
        )
        rows_t_ref[...] = turned(rows_ref[...])
        qkv_piece.ready(weight, sems.at[0])
        x = rows_ref[...]
        query = (dot(x, weight[:, :width]) + vectors[0:1]).astype(bf16)
        q_ref[...] = (query.astype(f32) * scale).astype(bf16)
        kv_ref[:, :width] = dot(x, weight[:, width : 2 * width]).astype(bf16)
        kv_ref[:, width:] = (dot(x, weight[:, 2 * width :]) + vectors[1:2]).astype(bf16)

    return call(
        body,
        "qkv",
        [table, rows, *flat(gathered)],
        [SMEM, VMEM] + [ANY] * 4,
        [
            shape(tokens, width, bf16),
            shape(tokens, 2 * width, bf16),
            shape(VECTORS, width, f32),
            shape(1, folds * width, f32),
            shape(width, tokens, bf16),
        ],
        [qkv_piece.whole(), pltpu.VMEM((width, LANES), bf16), pltpu.SemaphoreType.DMA((2,))],
        time=5,
    )


def pair_specs(parts, pairs, base):
    specs = []
    for part in parts:
        rows = part.shape[0]
        specs.append(pl.BlockSpec((rows, LANES), lambda p, s: (0, base + p)))
        specs.append(pl.BlockSpec((rows, LANES), lambda p, s: (0, pairs + base + p)))
    return specs


def first_lanes(shape_, count):
    return (lax.broadcasted_iota(jnp.int32, shape_, 1) < count).astype(f32).astype(bf16)


def head_blocks(query):
    lane = lax.broadcasted_iota(jnp.int32, query.shape, 1)
    zero = jnp.zeros_like(query)
    half = LANES // 2
    return jnp.concatenate(
        [jnp.where(lane < half, query, zero), jnp.where(lane >= half, query, zero)], axis=0
    )


def attend(query, parts, starts, length, base, count):
    tokens, width = query.shape
    pairs = width // LANES
    span = sum(part.shape[0] for part in parts)
    half = LANES // 2
    chunk = min(256, tokens)
    scalars = jnp.concatenate(
        [jnp.reshape(v, (1,)).astype(jnp.int32) for v in [length, *starts]]
    )

    def body(scalar, q_ref, *refs):
        kv_refs = refs[: 2 * len(parts)]
        mixed_t_ref, mixed_ref, p_ref, inverse_ref, bias = refs[2 * len(parts) :]

        @pl.when(pl.program_id(0) == 0)
        def _():
            at = 0
            for i, part in enumerate(parts):
                rows = part.shape[0]
                position = scalar[1 + i] + lax.broadcasted_iota(jnp.int32, (rows, LANES), 0)
                lane = lax.broadcasted_iota(jnp.int32, (rows, LANES), 1)
                hidden = jnp.where(position < scalar[0], 0.0, masked_score)
                bias[at : at + rows, :] = jnp.where(lane == 0, hidden, 0.0).astype(bf16)
                at += rows

        keys = jnp.concatenate([ref[...] for ref in kv_refs[0::2]], axis=0)
        values = jnp.concatenate([ref[...] for ref in kv_refs[1::2]], axis=0)
        keys = jnp.concatenate([keys, bias[...]], axis=1)
        values_t = jnp.concatenate([turned(values), jnp.ones((16, span), bf16)], axis=0)
        queries = head_blocks(q_ref[...])
        queries = jnp.concatenate([queries, first_lanes(queries.shape, 1)], axis=1)
        for at in range(0, 2 * tokens, chunk):
            scores = dot_rows(keys, queries[at : at + chunk])
            peak = jnp.max(scores, axis=0, keepdims=True)
            weights = jnp.exp(scores - peak).astype(bf16)
            p_ref[:, at : at + chunk] = weights
        sums = dot(values_t, p_ref[...])
        inverse = 1.0 / sums[LANES : LANES + 1]
        inverse_ref[...] = inverse
        mixed_t_ref[:half, :] = sums[:half, :tokens] * inverse[:, :tokens]
        mixed_t_ref[half:, :] = sums[half:LANES, tokens:] * inverse[:, tokens:]
        mixed_ref[...] = turned(mixed_t_ref[...]).astype(bf16)

    sources = [query]
    for part in parts:
        sources += [part, part]
    return pl.pallas_call(
        body,
        name="attend",
        cost_estimate=cost(8),
        out_shape=[
            in_hbm(count * LANES, tokens, f32),
            shape(tokens, count * LANES, bf16),
            in_hbm(count, span, 2 * tokens, bf16),
            in_hbm(count, 1, 2 * tokens, f32),
        ],
        grid_spec=pltpu.PrefetchScalarGridSpec(
            num_scalar_prefetch=1,
            grid=(count,),
            in_specs=[pl.BlockSpec((tokens, LANES), lambda p, s: (0, base + p))]
            + pair_specs(parts, pairs, base),
            out_specs=[
                pl.BlockSpec((LANES, tokens), lambda p, s: (p, 0)),
                pl.BlockSpec((tokens, LANES), lambda p, s: (0, p)),
                pl.BlockSpec((None, span, 2 * tokens), lambda p, s: (p, 0, 0)),
                pl.BlockSpec((None, 1, 2 * tokens), lambda p, s: (p, 0, 0)),
            ],
            scratch_shapes=[pltpu.VMEM((span, LANES), bf16)],
        ),
        compiler_params=pltpu.CompilerParams(vmem_limit_bytes=min(56 << 20, VMEM_BYTES * max(1, span // 1024))),
    )(scalars, *sources)


def attend_back(query, parts, grad_mixed, mixed_t, weights, inverse, scale, base, core):
    tokens, width = query.shape
    pairs = width // LANES
    span = sum(part.shape[0] for part in parts)
    half = LANES // 2
    chunk = min(256, tokens)

    def body(_, q_ref, gm_ref, mt_ref, p_ref, inv_ref, *refs):
        kv_refs = refs[: 2 * len(parts)]
        send_ref, keep_ref, ds_ref = refs[2 * len(parts) :]
        keys = jnp.concatenate([ref[...] for ref in kv_refs[0::2]], axis=0)
        values = jnp.concatenate([ref[...] for ref in kv_refs[1::2]], axis=0)
        grads = turned(gm_ref[...].astype(f32))
        inv = inv_ref[...]
        product = grads * mt_ref[...]
        empty = jnp.zeros((half, tokens), bf16)
        even, odd = inv[:, :tokens], inv[:, tokens:]
        delta = jnp.concatenate(
            [
                jnp.sum(product[:half], axis=0, keepdims=True) * even,
                jnp.sum(product[half:], axis=0, keepdims=True) * odd,
            ],
            axis=1,
        )
        top = jnp.concatenate([(grads[:half] * even).astype(bf16), empty], axis=1)
        bottom = jnp.concatenate([empty, (grads[half:] * odd).astype(bf16)], axis=1)
        scaled = jnp.concatenate([top, bottom], axis=0)
        first = (-delta).astype(bf16).astype(f32)
        second = (-delta - first).astype(bf16).astype(f32)
        third = (-delta - first - second).astype(bf16).astype(f32)
        row = lax.broadcasted_iota(jnp.int32, (LANES, 2 * tokens), 0)
        limbs = jnp.where(
            row == 0, first, jnp.where(row == 1, second, jnp.where(row == 2, third, 0.0))
        ).astype(bf16)
        right = jnp.concatenate([scaled, limbs], axis=0)
        left = jnp.concatenate([values, first_lanes(values.shape, 3)], axis=1)
        for at in range(0, 2 * tokens, chunk):
            grad_probs = dot(left, right[:, at : at + chunk])
            ds_ref[:, at : at + chunk] = (
                p_ref[:, at : at + chunk].astype(f32) * grad_probs
            ).astype(bf16)
        grad_scores = ds_ref[...]
        turned_grad = dot(turned(keys), grad_scores)
        grad_query = (
            turned(
                jnp.concatenate([turned_grad[:half, :tokens], turned_grad[half:, tokens:]], axis=0)
            )
            * scale
        ).astype(bf16)
        grad_keys = dot(grad_scores, head_blocks(q_ref[...])).astype(bf16)
        grad_values = dot_rows(p_ref[...], scaled).astype(bf16)
        pieces = [grad_query]
        at = 0
        for part in parts:
            rows = part.shape[0]
            pieces += [grad_keys[at : at + rows], grad_values[at : at + rows]]
            at += rows

        def write(ref, values_, start):
            for value in values_:
                ref[start : start + value.shape[0], :] = value
                start += value.shape[0]

        @pl.when(pl.program_id(0) == 0)
        def _():
            write(send_ref, pieces, 0)

        @pl.when(pl.program_id(0) == 1)
        def _():
            write(keep_ref, pieces[:3], 0)
            write(send_ref, pieces[3:], 5 * tokens)

    local = lambda p, s: (1 - p) * (1 - s[0]) + p * s[0]
    offset = lambda p, s: (0, base + local(p, s))
    sources = [query, grad_mixed, far(mixed_t), far(weights), far(inverse)]
    in_specs = [
        pl.BlockSpec((tokens, LANES), offset),
        pl.BlockSpec((tokens, LANES), offset),
        pl.BlockSpec((LANES, tokens), lambda p, s: (local(p, s), 0)),
        pl.BlockSpec((None, span, 2 * tokens), lambda p, s: (local(p, s), 0, 0)),
        pl.BlockSpec((None, 1, 2 * tokens), lambda p, s: (local(p, s), 0, 0)),
    ]
    for part in parts:
        sources += [part, part]
        rows = part.shape[0]
        in_specs.append(pl.BlockSpec((rows, LANES), offset))
        in_specs.append(pl.BlockSpec((rows, LANES), lambda p, s: (0, pairs + base + local(p, s))))
    kept = tokens + 2 * parts[0].shape[0]
    sent = 7 * tokens if len(parts) == 2 else kept
    return pl.pallas_call(
        body,
        name="attend_back",
        cost_estimate=cost(5),
        out_shape=[shape(sent, LANES, bf16), shape(kept, LANES, bf16)],
        grid_spec=pltpu.PrefetchScalarGridSpec(
            num_scalar_prefetch=1,
            grid=(2,),
            in_specs=in_specs,
            out_specs=[
                pl.BlockSpec((sent, LANES), lambda p, s: (0, 0)),
                pl.BlockSpec((kept, LANES), lambda p, s: (0, 0)),
            ],
            scratch_shapes=[pltpu.VMEM((span, 2 * tokens), bf16)],
        ),
        compiler_params=pltpu.CompilerParams(
            vmem_limit_bytes=min(56 << 20, VMEM_BYTES * max(1, span // 1024))
        ),
    )(jnp.reshape(core, (1,)).astype(jnp.int32), *sources)


def normalize(resid):
    center = resid - jnp.mean(resid, axis=1, keepdims=True)
    inverse = lax.rsqrt(jnp.mean(center * center, axis=1, keepdims=True) + norm_eps)
    return center * inverse, inverse


def norm_back(grads, normal, inverse, gain):
    scaled = grads * gain
    return inverse * (
        scaled
        - jnp.mean(scaled, axis=1, keepdims=True)
        - normal * jnp.mean(scaled * normal, axis=1, keepdims=True)
    )


def column_sums(value):
    return jnp.sum(value, axis=0, keepdims=True)


def by_rows(tokens, body):
    rows = min(tokens, 128)

    def one(i, carry):
        body(aligned(i * rows, rows, 8), i * rows, rows)
        return carry

    lax.fori_loop(0, tokens // rows, one, 0)


def add_row(ref, row, value):
    ref[row : row + 1, :] += value


def spread_total(ref, row):
    lanes = ref[row : row + 1, :]
    ref[row : row + 1, :] = jnp.broadcast_to(jnp.sum(lanes, axis=1, keepdims=True), lanes.shape)


def masked_squares(value, valid):
    return column_sums(jnp.where(valid, value * value, 0.0))


def valid_rows(scalar, at, first, rows):
    position = scalar[at + 1] + first + lax.broadcasted_iota(jnp.int32, (rows, 1), 0)
    return position < scalar[at]


def after_attention(links, table, rows, mixed, vectors, gathered, out_piece):
    tokens, width = rows.shape
    extra = 4 * links.dp + 1
    count = len(mixed)
    part = width // count

    def body(scalar, rows_ref, vec_ref, *refs):
        mixed_refs = refs[:count]
        pieces = sides(refs[count:])
        hidden_ref, low_ref, low_t_ref, mixed_t_ref = refs[count + 4 : count + 8]
        normal_ref, inverse_ref, sums_ref, weight, sem = refs[count + 8 :]
        out_piece.fetch(scalar, pieces, weight, sem.at[0])
        out_piece.ready(weight, sem.at[0])
        for i, ref in enumerate(mixed_refs):
            product = dot(ref[...], weight[i * part : (i + 1) * part, :])
            hidden_ref[...] = product if i == 0 else hidden_ref[...] + product
        sums_ref[...] = jnp.zeros_like(sums_ref)

        def block(at, first, span):
            x = rows_ref[at, :].astype(f32)
            valid = valid_rows(scalar, extra, first, span)
            branch = hidden_ref[at, :] + vec_ref[2:3]
            add_row(sums_ref, 0, masked_squares(x, valid))
            add_row(sums_ref, 1, masked_squares(branch, valid))
            count = jnp.sum(valid.astype(f32), axis=0, keepdims=True)
            add_row(sums_ref, 2, jnp.broadcast_to(count, (1, width)))
            normal, inverse = normalize(x + branch)
            hidden = normal * vec_ref[3:4] + vec_ref[4:5]
            normal_ref[at, :] = normal
            inverse_ref[at, :] = inverse
            hidden_ref[at, :] = hidden
            low_ref[at, :] = hidden.astype(bf16)

        by_rows(tokens, block)
        spread_total(sums_ref, 0)
        spread_total(sums_ref, 1)
        low_t_ref[...] = turned(low_ref[...])
        for i, ref in enumerate(mixed_refs):
            mixed_t_ref[i * part : (i + 1) * part, :] = turned(ref[...])

    return call(
        body,
        "after_attention",
        [table, rows, vectors, *mixed, *flat(gathered)],
        [SMEM] + [VMEM] * (2 + count) + [ANY] * 4,
        [
            shape(tokens, width, f32),
            shape(tokens, width, bf16),
            shape(width, tokens, bf16),
            shape(width, tokens, bf16),
            shape(tokens, width, f32),
            shape(tokens, 1, f32),
            shape(3, width, f32),
        ],
        [out_piece.whole(), pltpu.SemaphoreType.DMA((1,))],
        time=3.5,
    )


def gelu_and_slope(u):
    phi = 0.5 * lax.erf(u * math.sqrt(0.5)) + 0.5
    bell = jnp.exp(-0.5 * (u * u)) * (1.0 / math.sqrt(2.0 * math.pi))
    return u * phi, phi + u * bell


def feed_up(links, table, low, up_bias, gathered, up_piece):
    tokens, width = low.shape
    inner = up_bias.shape[1]

    def body(scalar, low_ref, bias_ref, *refs):
        act_ref, act_t_ref, slope_ref, weight, sem = refs[4:]
        up_piece.fetch(scalar, sides(refs), weight, sem.at[0])
        up_piece.ready(weight, sem.at[0])

        def forward(j, carry):
            at = aligned(j * width, width, LANES)
            value, slope = gelu_and_slope(dot(low_ref[...], weight[:, at]) + bias_ref[:, at])
            value = value.astype(bf16)
            act_ref[:, at] = value
            act_t_ref[at, :] = turned(value)
            slope_ref[:, at] = slope.astype(bf16)
            return carry

        lax.fori_loop(0, inner // width, forward, 0)

    return call(
        body,
        "feed_up",
        [table, low, up_bias, *flat(gathered)],
        [SMEM] + [VMEM] * 2 + [ANY] * 4,
        [
            shape(tokens, inner, bf16),
            shape(inner, tokens, bf16),
            shape(tokens, inner, bf16),
        ],
        [up_piece.whole(), pltpu.SemaphoreType.DMA((1,))],
        time=8,
    )


def share(core, value, at, keep_ref, send_ref):
    span = value.shape[1] // 2
    low, high = value[:, :span], value[:, span:]
    even = core == 0
    keep_ref[at, :] = jnp.where(even, low, high)
    send_ref[at, :] = jnp.where(even, high, low)


def feed_down(links, table, act, hidden, vectors, cotangent, gathered, down_piece):
    tokens, width = hidden.shape
    inner = act.shape[1]
    extra = 4 * links.dp + 1
    dp = links.dp

    def body(scalar, act_ref, hidden_ref, vec_ref, cot_ref, *refs):
        out_ref, resid_ref, grad_ref, keep_ref, send_ref, sums_ref, weight, sem = refs[4:]
        down_piece.fetch(scalar, sides(refs), weight, sem.at[0])
        down_piece.ready(weight, sem.at[0])
        resid_ref[...] = dot(act_ref[...], weight[...])
        sums_ref[...] = jnp.zeros_like(sums_ref)

        def block(at, first, span):
            branch = resid_ref[at, :] + vec_ref[5:6]
            valid = valid_rows(scalar, extra, first, span)
            add_row(sums_ref, 3, masked_squares(branch, valid))
            normal, inverse = normalize(hidden_ref[at, :] + branch)
            out_ref[at, :] = (normal * vec_ref[6:7] + vec_ref[7:8]).astype(bf16)
            grads = cot_ref[at, :].astype(f32)
            add_row(sums_ref, 1, column_sums(grads * normal))
            add_row(sums_ref, 2, column_sums(grads))
            resid = norm_back(grads, normal, inverse, vec_ref[6:7])
            resid_ref[at, :] = resid
            grad_ffn = resid.astype(bf16)
            grad_ref[at, :] = grad_ffn
            add_row(sums_ref, 0, column_sums(grad_ffn.astype(f32)))
            share(scalar[4 * dp], grad_ffn, at, keep_ref, send_ref)

        by_rows(tokens, block)
        spread_total(sums_ref, 3)

    return call(
        body,
        "feed_down",
        [table, act, hidden, vectors, cotangent, *flat(gathered)],
        [SMEM] + [VMEM] * 4 + [ANY] * 4,
        [
            shape(tokens, width, bf16),
            shape(tokens, width, f32),
            shape(tokens, width, bf16),
            shape(tokens, width // 2, bf16),
            shape(tokens, width // 2, bf16),
            shape(4, width, f32),
        ],
        [down_piece.whole(), pltpu.SemaphoreType.DMA((1,))],
        time=6,
    )


def feed_back(links, table, side, slope, so_far, grad_ffn, up, down, pieces):
    tokens, width = so_far.shape
    up_piece, down_piece = pieces
    span = up_piece.columns
    block = width if span % width == 0 else span
    dp = links.dp

    def body(scalar, slope_ref, so_far_ref, grad_ref, um, ul, *refs):
        hidden_ref, out_ref, bias_ref, up_w, down_w, sems = refs[4:]
        core = scalar[4 * dp]
        half = core if side == 0 else 1 - core
        down_piece.fetch_rows(scalar, half, sides(refs), down_w, sems.at[1])
        up_piece.fetch_side(scalar, side, (um, ul), up_w, sems.at[0])
        hidden_ref[...] = so_far_ref[...]
        down_piece.ready(down_w, sems.at[1])
        up_piece.ready(up_w, sems.at[0])

        def backward(j, carry):
            here = aligned(j * block, block, LANES)
            at = aligned(half * span + j * block, block, LANES)
            grads = dot_rows(grad_ref[...], down_w[here, :]) * slope_ref[:, at].astype(f32)
            grads = grads.astype(bf16)
            bias_ref[:, here] = column_sums(grads.astype(f32))
            hidden_ref[...] += dot_rows(grads, up_w[:, here])
            out_ref[:, here] = grads
            return carry

        lax.fori_loop(0, span // block, backward, 0)

    return call(
        body,
        "feed_back",
        [table, slope, so_far, grad_ffn, *map(far, up[side]), *flat(down)],
        [SMEM] + [VMEM] * 3 + [ANY] * 6,
        [shape(tokens, width, f32), shape(tokens, span, bf16), shape(1, span, f32)],
        [
            pltpu.VMEM((width, span), bf16),
            pltpu.VMEM((span, width), bf16),
            pltpu.SemaphoreType.DMA((2,)),
        ],
        time=6,
    )


def before_attention(links, table, grad_hidden, normal, inverse, vectors, gathered, piece):
    tokens, width = normal.shape

    def body(scalar, grad_ref, normal_ref, inverse_ref, vec_ref, *refs):
        resid_ref, gm_ref, keep_ref, send_ref, sums_ref, weight, whole, sem = refs[4:]
        piece.fetch(scalar, sides(refs), weight, sem.at[0])
        sums_ref[...] = jnp.zeros_like(sums_ref)

        def block(at, first, span):
            grads = grad_ref[at, :]
            normal_ = normal_ref[at, :]
            add_row(sums_ref, 1, column_sums(grads * normal_))
            add_row(sums_ref, 2, column_sums(grads))
            resid = norm_back(grads, normal_, inverse_ref[at, :], vec_ref[3:4])
            resid_ref[at, :] = resid
            grad_attn = resid.astype(bf16)
            whole[at, :] = grad_attn
            add_row(sums_ref, 0, column_sums(grad_attn.astype(f32)))
            share(scalar[4 * links.dp], grad_attn, at, keep_ref, send_ref)

        by_rows(tokens, block)
        piece.ready(weight, sem.at[0])
        gm_ref[...] = dot_rows(whole[...], weight[...]).astype(bf16)

    return call(
        body,
        "before_attention",
        [table, grad_hidden, normal, inverse, vectors, *flat(gathered)],
        [SMEM] + [VMEM] * 4 + [ANY] * 4,
        [
            shape(tokens, width, f32),
            shape(tokens, width, bf16),
            shape(tokens, width // 2, bf16),
            shape(tokens, width // 2, bf16),
            shape(3, width, f32),
        ],
        [piece.whole(), pltpu.VMEM((tokens, width), bf16), pltpu.SemaphoreType.DMA((1,))],
        time=0.01,
    )


def weight_gradient(name, links, table, left, right, rows):
    outer, tokens = left[0].shape
    columns = right[0].shape[1]
    block = min(outer, 768)
    wide = min(columns, 512)

    def body(scalar, lm, lt, rm, rt, *refs):
        tile = refs[-1]

        def one(j, carry):
            at = aligned(j // (columns // wide) * block, block, 8)
            to = aligned(j % (columns // wide) * wide, wide, LANES)
            tile[at, to] = dot(lm[at, :], rm[:, to]) + dot(lt[at, :], rt[:, to])
            return carry

        lax.fori_loop(0, outer // block * (columns // wide), one, 0)
        place(scalar, links.dp, tile, refs[:3], rows, slice(None))

    return call(
        body,
        name,
        [table, *left, *right],
        [SMEM] + [VMEM] * 4,
        placed(links.dp, rows, columns),
        [pltpu.VMEM((outer, columns), f32)],
    )


class Shares:
    def __init__(self, refs, tokens):
        self.sent, self.kept, self.came = refs
        self.tokens = tokens

    def rows(self, ref, i):
        return ref[i * self.tokens : (i + 1) * self.tokens, :]

    def add(self, one, other):
        return (one.astype(f32) + other.astype(f32)).astype(bf16)

    def own(self):
        return [self.rows(self.kept, 0)] + [
            self.add(self.rows(self.kept, i), self.rows(self.came, 2 + i)) for i in (1, 2)
        ]

    def others(self):
        return [self.rows(self.came, 0)] + [
            self.add(self.rows(self.sent, 4 + i), self.rows(self.came, i)) for i in (1, 2)
        ]

    def partners(self):
        return [self.rows(self.sent, 0)] + [
            self.add(self.rows(self.sent, i), self.rows(self.came, 4 + i)) for i in (1, 2)
        ]


def attention_gradient(name, links, table, rows_t, groups, rows, out=None, vectors=None, folds=0, sums=()):
    width, tokens = rows_t[0].shape
    dp = links.dp
    wide = 3 * LANES
    half = width // 2
    total = wide * len(groups) + (half if out else 0) + (LANES if vectors is not None else 0)
    given = [value for group in groups for value in group]
    more = list(out or []) + ([*vectors, *sums] if vectors is not None else [])

    def body(scalar, xm, xt, *refs):
        group_refs = refs[: len(given)]
        more_refs = list(refs[len(given) : len(given) + len(more)])
        outs = refs[len(given) + len(more) :]
        sum_ref, tile = outs[3], outs[4]
        for g in range(len(groups)):
            shares = Shares(group_refs[3 * g : 3 * g + 3], tokens)
            mine = jnp.concatenate(shares.own(), axis=1)
            theirs = jnp.concatenate(shares.others(), axis=1)
            tile[:, g * wide : (g + 1) * wide] = dot(xm[...], mine) + dot(xt[...], theirs)
            sums_ = column_sums(mine.astype(f32)) + column_sums(theirs.astype(f32))
            sum_ref[g : g + 1, :] = sums_
        at = wide * len(groups)
        if out:
            mm, mt, gm, gt = more_refs[:4]
            tile[:, at : at + half] = dot(mm[...], gm[...]) + dot(mt[...], gt[...])
            at += half
        if vectors is not None:
            sums3, sums2, kept, sent, sums1, *sum_refs = more_refs
            even = scalar[4 * dp] == 0
            bias = jnp.concatenate(
                [
                    jnp.where(even, kept[...], sent[...]),
                    jnp.where(even, sent[...], kept[...]),
                ],
                axis=1,
            )
            biases = [
                jnp.concatenate(
                    [
                        bias[:, (i * folds + j) * rows : (i * folds + j + 1) * rows]
                        for i in range(dp)
                    ],
                    axis=1,
                )
                for j in range(folds)
            ]
            head = jnp.concatenate(
                [jnp.zeros((2, width), f32), sums3[...], sums2[0:3]]
                + biases
                + [sums1[...], sums2[3:4]],
                axis=0,
            )
            every = [ref[i : i + 1, :] for ref in sum_refs for i in range(ref.shape[0])]
            every += [sum_ref[g : g + 1, :] for g in range(len(groups))]
            lane = lax.broadcasted_iota(jnp.int32, (1, width), 1)
            owned = (lane // LANES) % 2 == scalar[4 * dp]
            lines = []
            for j in (0, 2):
                parts = [s[:, j * LANES : (j + 1) * LANES] for s in every for _ in range(2)]
                lines.append(jnp.where(owned, jnp.concatenate(parts, axis=1), 0.0))
            row = lax.broadcasted_iota(jnp.int32, (LANES, width), 0)
            padded = jnp.concatenate(
                [head, jnp.zeros((LANES - head.shape[0], width), f32)], axis=0
            )
            padded = jnp.where(row == 0, lines[0], jnp.where(row == 1, lines[1], padded))
            tile[:, at : at + LANES] = turned(padded)
        place(scalar, dp, tile, outs[:3], rows, slice(None))

    return call(
        body,
        name,
        [table, *rows_t, *given, *more],
        [SMEM] + [VMEM] * (2 + len(given) + len(more)),
        placed(dp, rows, total) + [shape(len(groups), wide, f32)],
        [pltpu.VMEM((width, total), f32)],
    )


def input_gradient(links, table, groups, resid, gathered, qkv_piece):
    tokens, width = resid.shape
    given = [value for group in groups for value in group]

    def body(scalar, resid_ref, *refs):
        group_refs = refs[: len(given)]
        out_ref, weight, grads, sem = refs[len(given) + 4 :]
        qkv_piece.fetch(scalar, sides(refs[len(given) :]), weight, sem.at[0])
        core = scalar[4 * links.dp]
        for g in range(len(groups)):
            shares = Shares(group_refs[3 * g : 3 * g + 3], tokens)
            for owner, values in ((core, shares.own()), (1 - core, shares.partners())):
                for j, value in enumerate(values):
                    at = j * width + (2 * g + owner) * LANES
                    grads[:, aligned(at, LANES, LANES)] = value
        qkv_piece.ready(weight, sem.at[0])
        out_ref[...] = resid_ref[...] + dot_rows(grads[...], weight[...])

    return call(
        body,
        "input_gradient",
        [table, resid, *given, *flat(gathered)],
        [SMEM] + [VMEM] * (1 + len(given)) + [ANY] * 4,
        [shape(tokens, width, f32)],
        [qkv_piece.whole(), pltpu.VMEM((tokens, 3 * width), bf16), pltpu.SemaphoreType.DMA((1,))],
        time=20,
    )[0]


def closing(links, table, early, late, folds, width):
    rows = early[0].shape[0]
    wide = 3 * LANES
    half = width // 2
    base = 8

    def body(scalar, em, et, lm, lt, *outs):
        qkv_ref, out_ref, *vec_refs, up_ref, rms_ref = outs

        def write(core):
            for owner, early_ref, late_ref in ((core, em, lm), (1 - core, et, lt)):
                groups = [(early_ref, 0), (early_ref, wide), (late_ref, 0)]
                for g, (ref, first) in enumerate(groups):
                    for j in range(3):
                        at = j * width + (2 * g + owner) * LANES
                        qkv_ref[:, at : at + LANES] = ref[
                            :, first + j * LANES : first + (j + 1) * LANES
                        ].astype(f32)
                out_ref[:, owner * half : (owner + 1) * half] = early_ref[
                    :, 2 * wide : 2 * wide + half
                ].astype(f32)

        for core in range(2):
            pl.when(scalar[4 * links.dp] == core)(lambda core=core: write(core))
        last = slice(wide, wide + LANES)
        vectors = turned(lm[:, last].astype(f32) + lt[:, last].astype(f32))
        for i, ref in enumerate(vec_refs):
            ref[...] = vectors[i : i + 1]
        for i in range(folds):
            up_ref[:, i * rows : (i + 1) * rows] = vectors[base + i : base + i + 1]
        at = base + folds
        count = vectors[at + 2 : at + 3] * width
        for i, line in enumerate((at, at + 1, at + 3)):
            value = jnp.sqrt(vectors[line : line + 1] / count + 1e-06)
            rms_ref[:, i : i + 1] = value[:, 0:1]

    return call(
        body,
        "closing",
        [table, *early, *late],
        [SMEM] + [VMEM] * 4,
        [shape(rows, 3 * width, f32), shape(rows, width, f32)]
        + [shape(1, rows, f32)] * base
        + [shape(1, folds * rows, f32), shape(1, 3, f32)],
    )


def settle(links, reduction):
    mine = reduction.finish()
    return mine, links.swap(mine)


def shards(
    tokens,
    lengths,
    qkv_weight,
    query_bias,
    value_bias,
    out_weight,
    out_bias,
    norm1_gain,
    norm1_shift,
    up_weight,
    up_bias,
    down_weight,
    down_bias,
    norm2_gain,
    norm2_shift,
    cotangent,
):
    seq_dev, ctx_tok, width = tokens.shape
    assert seq_dev == 1 and width // HEADS == LANES // 2
    scale = (width // HEADS) ** (-0.5)
    links = Links()
    dp = links.dp
    rows = tokens.reshape(ctx_tok, width)
    cot = cotangent.reshape(ctx_tok, width)
    block = lax.axis_index("ctx")
    start = block * ctx_tok
    table = links.table(lengths[0], start)

    shard = qkv_weight.shape[0]
    inner = down_weight.shape[0] * dp
    folds = down_weight.shape[0] // shard
    half = [w.shape[1] // 2 for w in (qkv_weight, out_weight, up_weight, down_weight)]
    qkv_piece = Piece(dp, shard, half[0], 0)
    vector_piece = Piece(dp, shard, LANES, half[0])
    up_piece = Piece(dp, shard, half[2], 0)
    out_piece = Piece(dp, shard, half[1], half[2])
    down_piece = Piece(dp, down_weight.shape[0], half[3], 0)
    ffn_pieces = (up_piece, down_piece)

    columns = [query_bias, value_bias, out_bias, norm1_gain, norm1_shift]
    columns += [down_bias, norm2_gain, norm2_shift]
    base = len(columns)
    columns += [up_bias[i * shard : (i + 1) * shard] for i in range(folds)]
    packed = jnp.stack(columns, axis=1)
    packed = jnp.pad(packed, ((0, 0), (0, LANES - packed.shape[1])))
    qkv_sent = jnp.concatenate([half_columns(links, qkv_weight), packed], axis=1)
    up_sent = jnp.concatenate(
        [half_columns(links, up_weight), half_columns(links, out_weight)], axis=1
    )
    down_sent = half_columns(links, down_weight)

    qkv_held = joined(links.cross(qkv_sent))
    up_held = links.cross(after(up_sent, qkv_held))
    down_sent = after(down_sent, up_held)
    qkv_held = links.first(qkv_held)
    qkv = links.second(after(qkv_held, up_held[1]), *up_held)
    up_held = after(joined(up_held), qkv[0][1])
    query, kv, vectors, up_bias_row, rows_t = project(
        links, table, after(rows, up_held), qkv, qkv_piece, vector_piece, scale, base, folds
    )
    down_held = links.cross(after(down_sent, up_held))
    up_held = links.first(up_held, query)
    kv = after(kv, up_held)
    rows_t = [rows_t, links.swap(rows_t)]
    if links.ctx == 2:
        parts = [kv, links.swap(kv)]
        starts = [start, (1 - block) * ctx_tok]
    else:
        parts = [lax.all_gather(kv, "ctx", axis=0, tiled=True)]
        starts = [jnp.int32(0)]
    groups = 3
    count = width // LANES // groups
    forward = []
    waits = [(), (), ()]
    for i in range(groups):
        given = after(query, *waits[i], *(forward[-1][1:2] if forward else ()))
        forward.append(attend(given, parts, starts, lengths[0], i * count, count))
        if i == 0:
            down_held = joined(down_held, forward[0][1])
            waits[1] = (down_held,)
    up = links.second(up_held, forward[1][1])
    down_held = links.first(after(down_held, forward[1][1]), forward[2][1])
    mixed = [f[1] for f in forward]
    hidden, low, low_t, mixed_t, normal, deviation, sums1 = after_attention(
        links, table, after(rows, down_held), mixed, vectors, up, out_piece
    )
    low_t = [low_t, links.swap(low_t)]
    mixed_t = [mixed_t, links.swap(mixed_t)]
    act, act_t, slope = feed_up(links, table, low, up_bias_row, up, up_piece)
    down = links.second(after(down_held, forward[2][1]), act)
    act_t = [act_t, links.swap(after(act_t, down[1][1]))]
    output, resid2, grad_ffn, ffn_keep, ffn_send, sums2 = feed_down(
        links, table, act, hidden, vectors, cot, down, down_piece
    )
    ffn_came = links.swap(ffn_send)
    grad_hidden, upper_send, bias_sent = feed_back(
        links, table, 1, slope, resid2, grad_ffn, up, down, ffn_pieces
    )
    upper_came = links.swap(upper_send)
    down_sum = Sum(
        links,
        weight_gradient(
            "down_gradient",
            links,
            table,
            [after(act_t[0], grad_hidden), act_t[1]],
            [ffn_keep, ffn_came],
            down_piece.rows,
        ),
    )
    given = after(grad_hidden, down_sum.prepare())
    down_sum.send()
    grad_hidden, upper_keep, bias_kept = feed_back(
        links, table, 0, slope, given, grad_ffn, up, down, ffn_pieces
    )
    up_sum = Sum(
        links,
        weight_gradient(
            "up_gradient", links, table, low_t, [upper_keep, upper_came], up_piece.rows
        ),
    )
    given = after(grad_hidden, up_sum.prepare())
    up_sum.send()
    resid1, grad_mixed, attn_keep, attn_send, sums3 = before_attention(
        links, table, given, normal, deviation, vectors, up, out_piece
    )
    out_parts = [*mixed_t, attn_keep, links.swap(attn_send)]

    def back_through(i, given):
        turned_mixed, _, weights, inverse = forward[i]
        sent, kept = attend_back(
            given,
            parts,
            grad_mixed,
            turned_mixed,
            weights,
            inverse,
            scale,
            i * count,
            links.core,
        )
        if links.ctx == 2:
            return [sent, kept, links.swap(sent)]
        whole = []
        for value in (sent, kept):
            keys, values = jnp.split(value[ctx_tok:], 2, axis=0)
            both = lax.psum_scatter(
                jnp.concatenate([keys, values], axis=1), "ctx", scatter_dimension=0, tiled=True
            )
            whole.append([value[:ctx_tok], both[:, :LANES], both[:, LANES:]])
        blank = jnp.zeros((4 * ctx_tok, LANES), bf16)
        sent = jnp.concatenate(whole[0] + [blank], axis=0)
        return [sent, jnp.concatenate(whole[1], axis=0), links.swap(sent)]

    down_sum.hold(grad_mixed)
    given = after(query, down_sum.prepare(), grad_mixed)
    down_sum.send()
    back = [back_through(0, given)]
    back.append(back_through(1, after(query, back[0][1])))
    down_sum.hold(back[1][1])
    up_sum.hold(back[1][1])
    given = after(rows_t[0], down_sum.prepare(), up_sum.prepare())
    down_sum.send()
    up_sum.send()
    *early, early_sums = attention_gradient(
        "early_gradient", links, table, [given, rows_t[1]], back[:2], shard, out=out_parts
    )
    early_sum = Sum(links, early)
    down_sum.hold(early[2])
    up_sum.hold(early[2])
    given = after(query, early_sum.prepare(), down_sum.prepare(), up_sum.prepare())
    early_sum.send()
    down_sum.send()
    up_sum.send()
    back.append(back_through(2, given))
    up_sum.hold(back[2][1])
    early_sum.hold(back[2][1])
    down_sum.hold(back[2][1])
    up_sum.hold(back[2][1])
    down_mine = down_sum.finish()
    given = after(rows_t[0], early_sum.prepare(), up_sum.prepare(), down_mine)
    early_sum.send()
    up_sum.send()
    *late, _ = attention_gradient(
        "late_gradient",
        links,
        table,
        [given, rows_t[1]],
        back[2:],
        shard,
        vectors=[sums3, sums2, bias_kept, bias_sent, sums1],
        folds=folds,
        sums=[early_sums],
    )
    late_sum = Sum(links, late, direct=True)
    early_sum.hold(late[2])
    up_sum.hold(late[2])
    up_mine = up_sum.finish()
    given = after(resid1, late_sum.prepare(), early_sum.prepare(), up_mine)
    late_sum.send()
    early_sum.send()
    input_grad = input_gradient(links, table, back, given, qkv, qkv_piece)
    late_sum.hold(input_grad)
    early_sum.hold(input_grad)
    down_grad = both_halves(links, down_mine, links.swap(down_mine))
    up_grad = both_halves(links, up_mine, links.swap(up_mine))
    early = settle(links, early_sum)
    late = settle(links, late_sum)
    qkv_grad, out_grad, *sums, up_bias_grad, stream_rms = closing(
        links, table, early, late, folds, width
    )
    sums = [value.reshape(shard) for value in sums]
    return (
        output.reshape(seq_dev, ctx_tok, width),
        input_grad.reshape(seq_dev, ctx_tok, width),
        stream_rms.reshape(3),
        qkv_grad,
        sums[0],
        sums[1],
        out_grad,
        sums[2],
        sums[3],
        sums[4],
        up_grad,
        up_bias_grad.reshape(-1),
        down_grad,
        sums[5],
        sums[6],
        sums[7],
    )


def solution(mesh):
    in_specs = (
        P("dp", "ctx", None),
        P("dp"),
        P("dp", None),
        P("dp"),
        P("dp"),
        P("dp", None),
        P("dp"),
        P("dp"),
        P("dp"),
        P("dp", None),
        P("dp"),
        P("dp", None),
        P("dp"),
        P("dp"),
        P("dp"),
        P("dp", "ctx", None),
    )
    out_specs = (
        P("dp", "ctx", None),
        P("dp", "ctx", None),
        P(),
        P("dp", None),
        P("dp"),
        P("dp"),
        P("dp", None),
        P("dp"),
        P("dp"),
        P("dp"),
        P("dp", None),
        P("dp"),
        P("dp", None),
        P("dp"),
        P("dp"),
        P("dp"),
    )
    return jax.shard_map(shards, mesh=mesh, in_specs=in_specs, out_specs=out_specs, check_vma=False)
```

```python
import math

import jax
import jax.numpy as jnp
from jax import lax
from jax.experimental import pallas as pl
from jax.experimental.pallas import tpu as pltpu
from jax.sharding import PartitionSpec as P

HEADS = 12
LANES = 128
VECTORS = 16
VMEM_BYTES = 24 << 20
FLOPS = 400_000_000
BYTES = 1_200_000

masked_score = -1e30
norm_eps = 1e-05
f32 = jnp.float32
bf16 = jnp.bfloat16


def low_precision(value):
    return lax.reduce_precision(value, exponent_bits=8, mantissa_bits=7)


class Links:
    def __init__(self):
        self.dp = lax.axis_size("dp")
        self.ctx = lax.axis_size("ctx")
        self.bits = self.dp.bit_length() - 1
        assert self.dp == 1 << self.bits and self.bits >= 2 and self.ctx % 2 == 0
        self.core = lax.axis_index("ctx") % 2
        self.me = lax.axis_index("dp")
        self.upper = []
        bit = self.bits - 1
        while bit >= 2:
            size = 2 if (bit - 1) % 2 == 0 else 1
            self.upper.append(tuple(range(bit, bit - size, -1)))
            bit -= size

    def swap(self, value):
        return lax.ppermute(value, "ctx", [(i, i ^ 1) for i in range(self.ctx)])

    def hop(self, value, mask_even, mask_odd):
        pairs = []
        for block in range(self.ctx):
            mask = mask_odd if block % 2 else mask_even
            pairs += [(block * self.dp + i, block * self.dp + (i ^ mask)) for i in range(self.dp)]
        return lax.ppermute(value, ("ctx", "dp"), pairs)

    def places(self, core):
        position = lax.iota(jnp.int32, self.dp)
        quarter = self.dp // 4
        first = (position // quarter) % 2
        second = position // (2 * quarter)
        mask = first * (1 + core) + second * (2 - core)
        for i in range(self.bits - 2):
            mask = mask + ((position >> i) % 2) * (1 << (self.bits - 1 - i))
        return jnp.bitwise_xor(self.me, mask)

    def spots(self, core):
        mask = jnp.bitwise_xor(self.me, lax.iota(jnp.int32, self.dp))
        low, high = mask % 2, (mask // 2) % 2
        first = jnp.where(core == 0, low, high)
        second = jnp.where(core == 0, high, low)
        quarter = self.dp // 4
        spot = first * quarter + second * (2 * quarter)
        for i in range(self.bits - 2):
            spot = spot + ((mask >> (self.bits - 1 - i)) % 2) * (1 << i)
        return spot

    def table(self, *more):
        parts = [self.places(self.core), self.places(1 - self.core)]
        parts += [self.spots(self.core), self.spots(1 - self.core)]
        parts += [jnp.reshape(value, (1,)) for value in (self.core,) + more]
        return jnp.concatenate(parts).astype(jnp.int32)

    def masks(self, bits):
        return [
            sum(((i >> j) & 1) << bit for j, bit in enumerate(bits)) for i in range(1 << len(bits))
        ]

    def cross(self, piece):
        held = [piece]
        for bits in self.upper:
            here = jnp.concatenate(held, axis=0) if len(held) > 1 else held[0]
            held = [here] + [self.hop(here, mask, mask) for mask in self.masks(bits)[1:]]
        return held

    def cross_slowly(self, piece, ready):
        held = piece
        masks = [1 << bit for bits in self.upper for bit in bits]
        for i, mask in enumerate(masks):
            more = self.hop(held, mask, mask)
            if i < len(masks) - 1:
                more = ready(more)
            held = [held, more]
            if i < len(masks) - 1:
                held = jnp.concatenate(held, axis=0)
        return held

    def first(self, held, *waits):
        more = self.hop(held, 1, 2)
        return jnp.concatenate([held, after(more, *waits) if waits else more], axis=0)

    def second(self, held, *waits):
        early = self.swap(held)
        more = self.hop(held, 2, 1)
        if waits:
            early, more = after((early, more), *waits)
        return [held, more], [early, self.swap(more)]


def joined(held, *waits):
    return jnp.concatenate(after(tuple(held), *waits) if waits else held, axis=0)


class Sum:
    def __init__(self, links, kept, direct=False):
        self.links = links
        self.kept = kept
        self.quarter = kept[0].shape[0]
        self.rows = 4 * self.quarter
        self.terms = []
        self.steps = [[(2, 1)], [(1, 2)]]
        for bits in reversed(links.upper):
            if direct:
                self.steps.append([(mask, mask) for mask in links.masks(bits)[1:]])
            else:
                self.steps += [[(1 << bit, 1 << bit)] for bit in reversed(bits)]
        self.ready = None

    def total(self, start, span):
        index = min(2, start // self.quarter)
        first = start - index * self.quarter
        value = self.kept[index]
        if span != value.shape[0]:
            value = lax.slice_in_dim(value, first, first + span, axis=0)
        if not self.terms:
            return value
        value = value.astype(f32)
        for term in self.terms:
            parts = [
                lax.slice_in_dim(part, start, start + span, axis=0).astype(f32) for part in term
            ]
            if len(parts) == 1:
                value = low_precision(value + parts[0])
            else:
                value = low_precision((value + parts[0]) + (parts[1] + parts[2]))
        return value.astype(bf16)

    def prepare(self):
        masks = self.steps[0]
        self.rows //= len(masks) + 1
        self.ready = [self.total((i + 1) * self.rows, self.rows) for i in range(len(masks))]
        return self.ready

    def send(self):
        if self.ready is None:
            self.prepare()
        masks = self.steps.pop(0)
        self.terms.append(
            tuple(self.links.hop(value, *mask) for value, mask in zip(self.ready, masks))
        )
        self.ready = None

    def hold(self, other):
        self.terms[-1] = tuple(after(value, other) for value in self.terms[-1])

    def finish(self):
        while self.steps:
            self.send()
        mine = self.total(0, self.rows)
        step = 2
        while step < self.links.ctx:
            pairs = [(i, i ^ step) for i in range(self.links.ctx)]
            other = lax.ppermute(mine, "ctx", pairs)
            mine = low_precision(mine.astype(f32) + other.astype(f32)).astype(bf16)
            step *= 2
        return mine


def after(value, *others):
    return lax.optimization_barrier((value, others))[0]


def half_columns(links, value):
    span = value.shape[1] // 2
    return lax.dynamic_slice_in_dim(value, links.core * span, span, 1)


def both_halves(links, mine, theirs):
    even = links.core == 0
    return jnp.concatenate(
        [jnp.where(even, mine, theirs), jnp.where(even, theirs, mine)], axis=1
    ).astype(f32)


def dot(left, right):
    return jnp.dot(left, right, preferred_element_type=f32)


def dot_rows(left, right):
    return lax.dot_general(left, right, (((1,), (1,)), ((), ())), preferred_element_type=f32)


def turned(value):
    return jnp.transpose(value)


def aligned(start, size, unit):
    return pl.ds(pl.multiple_of(start, unit), size)


SMEM = pl.BlockSpec(memory_space=pltpu.SMEM)
ANY = pl.BlockSpec(memory_space=pl.ANY)
VMEM = pl.BlockSpec(memory_space=pltpu.VMEM)


def cost(microseconds):
    return pl.CostEstimate(
        flops=int(microseconds * FLOPS), transcendentals=0, bytes_accessed=int(microseconds * BYTES)
    )


def call(body, name, sources, in_specs, outs, scratch=(), time=5):
    return pl.pallas_call(
        body,
        name=name,
        out_shape=outs,
        in_specs=in_specs,
        out_specs=[VMEM] * len(outs),
        scratch_shapes=list(scratch),
        compiler_params=pltpu.CompilerParams(vmem_limit_bytes=VMEM_BYTES),
        cost_estimate=cost(time),
    )(*sources)


def shape(rows, columns, dtype):
    return jax.ShapeDtypeStruct((rows, columns), dtype)


class Piece:
    def __init__(self, dp, rows, columns, first):
        self.dp, self.rows, self.columns, self.first = dp, rows, columns, first

    def fetch(self, scalar, sides, whole, sem):
        core = scalar[4 * self.dp]
        for side, sources in enumerate(sides):
            half = core if side == 0 else 1 - core
            count = self.dp // len(sources)
            for i, source in enumerate(sources):

                def one(position, carry, side=side, source=source, half=half, base=i * count):
                    owner = scalar[side * self.dp + base + position]
                    pltpu.make_async_copy(
                        source.at[
                            aligned(position * self.rows, self.rows, 8),
                            pl.ds(self.first, self.columns),
                        ],
                        whole.at[
                            aligned(owner * self.rows, self.rows, 8),
                            aligned(half * self.columns, self.columns, LANES),
                        ],
                        sem,
                    ).start()
                    return carry

                lax.fori_loop(0, count, one, 0)

    def fetch_side(self, scalar, side, sources, whole, sem):
        count = self.dp // len(sources)
        for i, source in enumerate(sources):

            def one(position, carry, source=source, base=i * count):
                owner = scalar[side * self.dp + base + position]
                pltpu.make_async_copy(
                    source.at[
                        aligned(position * self.rows, self.rows, 8),
                        pl.ds(self.first, self.columns),
                    ],
                    whole.at[aligned(owner * self.rows, self.rows, 8), :],
                    sem,
                ).start()
                return carry

            lax.fori_loop(0, count, one, 0)

    def fetch_rows(self, scalar, part, sides, whole, sem):
        core = scalar[4 * self.dp]
        for side, sources in enumerate(sides):
            half = core if side == 0 else 1 - core
            count = self.dp // len(sources)

            def one(i, carry, side=side, sources=sources, half=half, count=count):
                spot = scalar[(2 + side) * self.dp + part * (self.dp // 2) + i]
                for j, source in enumerate(sources):

                    @pl.when(spot // count == j)
                    def _(source=source, j=j):
                        pltpu.make_async_copy(
                            source.at[
                                aligned((spot - j * count) * self.rows, self.rows, 8),
                                pl.ds(self.first, self.columns),
                            ],
                            whole.at[
                                aligned(i * self.rows, self.rows, 8),
                                aligned(half * self.columns, self.columns, LANES),
                            ],
                            sem,
                        ).start()

                return carry

            lax.fori_loop(0, self.dp // 2, one, 0)

    def ready(self, whole, sem):
        pltpu.make_async_copy(whole, whole, sem).wait()

    def whole(self):
        return pltpu.VMEM((self.dp * self.rows, 2 * self.columns), bf16)


def place(scalar, dp, tile, outs, rows, columns):
    base = 0
    for out in outs:
        count = out.shape[0] // rows

        def one(i, carry, out=out, base=base):
            owner = scalar[base + i]
            out[aligned(i * rows, rows, 8), columns] = tile[aligned(owner * rows, rows, 8), :].astype(
                bf16
            )
            return carry

        lax.fori_loop(0, count, one, 0)
        base += count


def placed(dp, rows, columns):
    return [
        shape(rows * dp // 4, columns, bf16),
        shape(rows * dp // 4, columns, bf16),
        shape(rows * dp // 2, columns, bf16),
    ]


def in_hbm(*dims):
    *dims, dtype = dims
    return pltpu.HBM(tuple(dims), dtype)


def sides(refs):
    return (refs[:2], refs[2:4])


def far(value):
    return pltpu.with_memory_space_constraint(value, pltpu.HBM)


def flat(gathered):
    return [far(value) for value in (*gathered[0], *gathered[1])]


def project(links, table, rows, gathered, qkv_piece, vector_piece, scale, base, folds):
    tokens, width = rows.shape
    shard = width // links.dp

    def body(scalar, rows_ref, *refs):
        q_ref, kv_ref, vec_ref, bias_ref, rows_t_ref, weight, vecs, sems = refs[4:]
        pieces = sides(refs)
        vector_piece.fetch_side(scalar, 0, pieces[0], vecs, sems.at[1])
        qkv_piece.fetch(scalar, pieces, weight, sems.at[0])
        vector_piece.ready(vecs, sems.at[1])
        vectors = turned(vecs[...].astype(f32))[:VECTORS]
        vec_ref[...] = vectors
        bias_ref[...] = jnp.concatenate(
            [
                vectors[base + j : base + j + 1, i * shard : (i + 1) * shard]
                for i in range(links.dp)
                for j in range(folds)
            ],
            axis=1,
        )
        rows_t_ref[...] = turned(rows_ref[...])
        qkv_piece.ready(weight, sems.at[0])
        x = rows_ref[...]
        query = (dot(x, weight[:, :width]) + vectors[0:1]).astype(bf16)
        q_ref[...] = (query.astype(f32) * scale).astype(bf16)
        kv_ref[:, :width] = dot(x, weight[:, width : 2 * width]).astype(bf16)
        kv_ref[:, width:] = (dot(x, weight[:, 2 * width :]) + vectors[1:2]).astype(bf16)

    return call(
        body,
        "qkv",
        [table, rows, *flat(gathered)],
        [SMEM, VMEM] + [ANY] * 4,
        [
            shape(tokens, width, bf16),
            shape(tokens, 2 * width, bf16),
            shape(VECTORS, width, f32),
            shape(1, folds * width, f32),
            in_hbm(width, tokens, bf16),
        ],
        [qkv_piece.whole(), pltpu.VMEM((width, LANES), bf16), pltpu.SemaphoreType.DMA((2,))],
        time=5,
    )


def pair_specs(parts, pairs, base):
    specs = []
    for part in parts:
        rows = part.shape[0]
        specs.append(pl.BlockSpec((rows, LANES), lambda p, s: (0, base + p)))
        specs.append(pl.BlockSpec((rows, LANES), lambda p, s: (0, pairs + base + p)))
    return specs


def first_lanes(shape_, count):
    return (lax.broadcasted_iota(jnp.int32, shape_, 1) < count).astype(f32).astype(bf16)


def head_blocks(query):
    lane = lax.broadcasted_iota(jnp.int32, query.shape, 1)
    zero = jnp.zeros_like(query)
    half = LANES // 2
    return jnp.concatenate(
        [jnp.where(lane < half, query, zero), jnp.where(lane >= half, query, zero)], axis=0
    )


def attend(query, parts, starts, length, base, count):
    tokens, width = query.shape
    pairs = width // LANES
    span = sum(part.shape[0] for part in parts)
    half = LANES // 2
    chunk = min(256, tokens)
    scalars = jnp.concatenate(
        [jnp.reshape(v, (1,)).astype(jnp.int32) for v in [length, *starts]]
    )

    def body(scalar, q_ref, *refs):
        kv_refs = refs[: 2 * len(parts)]
        mixed_t_ref, mixed_ref, p_ref, inverse_ref, bias = refs[2 * len(parts) :]

        @pl.when(pl.program_id(0) == 0)
        def _():
            at = 0
            for i, part in enumerate(parts):
                rows = part.shape[0]
                position = scalar[1 + i] + lax.broadcasted_iota(jnp.int32, (rows, LANES), 0)
                lane = lax.broadcasted_iota(jnp.int32, (rows, LANES), 1)
                hidden = jnp.where(position < scalar[0], 0.0, masked_score)
                bias[at : at + rows, :] = jnp.where(lane == 0, hidden, 0.0).astype(bf16)
                at += rows

        keys = jnp.concatenate([ref[...] for ref in kv_refs[0::2]], axis=0)
        values = jnp.concatenate([ref[...] for ref in kv_refs[1::2]], axis=0)
        keys = jnp.concatenate([keys, bias[...]], axis=1)
        values_t = jnp.concatenate([turned(values), jnp.ones((16, span), bf16)], axis=0)
        queries = head_blocks(q_ref[...])
        queries = jnp.concatenate([queries, first_lanes(queries.shape, 1)], axis=1)
        for at in range(0, 2 * tokens, chunk):
            scores = dot_rows(keys, queries[at : at + chunk])
            peak = jnp.max(scores, axis=0, keepdims=True)
            weights = jnp.exp(scores - peak).astype(bf16)
            p_ref[:, at : at + chunk] = weights
        sums = dot(values_t, p_ref[...])
        inverse = 1.0 / sums[LANES : LANES + 1]
        inverse_ref[...] = inverse
        mixed_t_ref[:half, :] = sums[:half, :tokens] * inverse[:, :tokens]
        mixed_t_ref[half:, :] = sums[half:LANES, tokens:] * inverse[:, tokens:]
        mixed_ref[...] = turned(mixed_t_ref[...]).astype(bf16)

    sources = [query]
    for part in parts:
        sources += [part, part]
    return pl.pallas_call(
        body,
        name="attend",
        cost_estimate=cost(8),
        out_shape=[
            in_hbm(count * LANES, tokens, f32),
            shape(tokens, count * LANES, bf16),
            in_hbm(count, span, 2 * tokens, bf16),
            in_hbm(count, 1, 2 * tokens, f32),
        ],
        grid_spec=pltpu.PrefetchScalarGridSpec(
            num_scalar_prefetch=1,
            grid=(count,),
            in_specs=[pl.BlockSpec((tokens, LANES), lambda p, s: (0, base + p))]
            + pair_specs(parts, pairs, base),
            out_specs=[
                pl.BlockSpec((LANES, tokens), lambda p, s: (p, 0)),
                pl.BlockSpec((tokens, LANES), lambda p, s: (0, p)),
                pl.BlockSpec((None, span, 2 * tokens), lambda p, s: (p, 0, 0)),
                pl.BlockSpec((None, 1, 2 * tokens), lambda p, s: (p, 0, 0)),
            ],
            scratch_shapes=[pltpu.VMEM((span, LANES), bf16)],
        ),
        compiler_params=pltpu.CompilerParams(vmem_limit_bytes=min(56 << 20, VMEM_BYTES * max(1, span // 1024))),
    )(scalars, *sources)


def attend_back(query, parts, grad_mixed, mixed_t, weights, inverse, scale, base, core):
    tokens, width = query.shape
    pairs = width // LANES
    span = sum(part.shape[0] for part in parts)
    half = LANES // 2
    chunk = min(256, tokens)

    def body(_, q_ref, gm_ref, mt_ref, p_ref, inv_ref, *refs):
        kv_refs = refs[: 2 * len(parts)]
        send_ref, keep_ref, ds_ref = refs[2 * len(parts) :]
        keys = jnp.concatenate([ref[...] for ref in kv_refs[0::2]], axis=0)
        values = jnp.concatenate([ref[...] for ref in kv_refs[1::2]], axis=0)
        grads = turned(gm_ref[...].astype(f32))
        inv = inv_ref[...]
        product = grads * mt_ref[...]
        empty = jnp.zeros((half, tokens), bf16)
        even, odd = inv[:, :tokens], inv[:, tokens:]
        delta = jnp.concatenate(
            [
                jnp.sum(product[:half], axis=0, keepdims=True) * even,
                jnp.sum(product[half:], axis=0, keepdims=True) * odd,
            ],
            axis=1,
        )
        top = jnp.concatenate([(grads[:half] * even).astype(bf16), empty], axis=1)
        bottom = jnp.concatenate([empty, (grads[half:] * odd).astype(bf16)], axis=1)
        scaled = jnp.concatenate([top, bottom], axis=0)
        first = (-delta).astype(bf16).astype(f32)
        second = (-delta - first).astype(bf16).astype(f32)
        third = (-delta - first - second).astype(bf16).astype(f32)
        row = lax.broadcasted_iota(jnp.int32, (LANES, 2 * tokens), 0)
        limbs = jnp.where(
            row == 0, first, jnp.where(row == 1, second, jnp.where(row == 2, third, 0.0))
        ).astype(bf16)
        right = jnp.concatenate([scaled, limbs], axis=0)
        left = jnp.concatenate([values, first_lanes(values.shape, 3)], axis=1)
        for at in range(0, 2 * tokens, chunk):
            grad_probs = dot(left, right[:, at : at + chunk])
            ds_ref[:, at : at + chunk] = (
                p_ref[:, at : at + chunk].astype(f32) * grad_probs
            ).astype(bf16)
        grad_scores = ds_ref[...]
        turned_grad = dot(turned(keys), grad_scores)
        grad_query = (
            turned(
                jnp.concatenate([turned_grad[:half, :tokens], turned_grad[half:, tokens:]], axis=0)
            )
            * scale
        ).astype(bf16)
        grad_keys = dot(grad_scores, head_blocks(q_ref[...])).astype(bf16)
        grad_values = dot_rows(p_ref[...], scaled).astype(bf16)
        pieces = [grad_query]
        at = 0
        for part in parts:
            rows = part.shape[0]
            pieces += [grad_keys[at : at + rows], grad_values[at : at + rows]]
            at += rows

        def write(ref, values_, start):
            for value in values_:
                ref[start : start + value.shape[0], :] = value
                start += value.shape[0]

        @pl.when(pl.program_id(0) == 0)
        def _():
            write(send_ref, pieces, 0)

        @pl.when(pl.program_id(0) == 1)
        def _():
            write(keep_ref, pieces[:3], 0)
            write(send_ref, pieces[3:], 5 * tokens)

    local = lambda p, s: (1 - p) * (1 - s[0]) + p * s[0]
    offset = lambda p, s: (0, base + local(p, s))
    sources = [query, grad_mixed, far(mixed_t), far(weights), far(inverse)]
    in_specs = [
        pl.BlockSpec((tokens, LANES), offset),
        pl.BlockSpec((tokens, LANES), offset),
        pl.BlockSpec((LANES, tokens), lambda p, s: (local(p, s), 0)),
        pl.BlockSpec((None, span, 2 * tokens), lambda p, s: (local(p, s), 0, 0)),
        pl.BlockSpec((None, 1, 2 * tokens), lambda p, s: (local(p, s), 0, 0)),
    ]
    for part in parts:
        sources += [part, part]
        rows = part.shape[0]
        in_specs.append(pl.BlockSpec((rows, LANES), offset))
        in_specs.append(pl.BlockSpec((rows, LANES), lambda p, s: (0, pairs + base + local(p, s))))
    kept = tokens + 2 * parts[0].shape[0]
    sent = 7 * tokens if len(parts) == 2 else kept
    return pl.pallas_call(
        body,
        name="attend_back",
        cost_estimate=cost(5),
        out_shape=[shape(sent, LANES, bf16), shape(kept, LANES, bf16)],
        grid_spec=pltpu.PrefetchScalarGridSpec(
            num_scalar_prefetch=1,
            grid=(2,),
            in_specs=in_specs,
            out_specs=[
                pl.BlockSpec((sent, LANES), lambda p, s: (0, 0)),
                pl.BlockSpec((kept, LANES), lambda p, s: (0, 0)),
            ],
            scratch_shapes=[pltpu.VMEM((span, 2 * tokens), bf16)],
        ),
        compiler_params=pltpu.CompilerParams(
            vmem_limit_bytes=min(56 << 20, VMEM_BYTES * max(1, span // 1024))
        ),
    )(jnp.reshape(core, (1,)).astype(jnp.int32), *sources)


def normalize(resid):
    center = resid - jnp.mean(resid, axis=1, keepdims=True)
    inverse = lax.rsqrt(jnp.mean(center * center, axis=1, keepdims=True) + norm_eps)
    return center * inverse, inverse


def norm_back(grads, normal, inverse, gain):
    scaled = grads * gain
    return inverse * (
        scaled
        - jnp.mean(scaled, axis=1, keepdims=True)
        - normal * jnp.mean(scaled * normal, axis=1, keepdims=True)
    )


def column_sums(value):
    return jnp.sum(value, axis=0, keepdims=True)


def by_rows(tokens, body):
    rows = min(tokens, 128)

    def one(i, carry):
        body(aligned(i * rows, rows, 8), i * rows, rows)
        return carry

    lax.fori_loop(0, tokens // rows, one, 0)


def add_row(ref, row, value):
    ref[row : row + 1, :] += value


def spread_total(ref, row):
    lanes = ref[row : row + 1, :]
    ref[row : row + 1, :] = jnp.broadcast_to(jnp.sum(lanes, axis=1, keepdims=True), lanes.shape)


def masked_squares(value, valid):
    return column_sums(jnp.where(valid, value * value, 0.0))


def valid_rows(scalar, at, first, rows):
    position = scalar[at + 1] + first + lax.broadcasted_iota(jnp.int32, (rows, 1), 0)
    return position < scalar[at]


def after_attention(links, table, rows, mixed, vectors, gathered, out_piece):
    tokens, width = rows.shape
    extra = 4 * links.dp + 1
    count = len(mixed)
    part = width // count

    def body(scalar, rows_ref, vec_ref, *refs):
        mixed_refs = refs[:count]
        pieces = sides(refs[count:])
        hidden_ref, low_ref, low_t_ref, mixed_t_ref = refs[count + 4 : count + 8]
        normal_ref, inverse_ref, sums_ref, weight, sem = refs[count + 8 :]
        out_piece.fetch(scalar, pieces, weight, sem.at[0])
        out_piece.ready(weight, sem.at[0])
        for i, ref in enumerate(mixed_refs):
            product = dot(ref[...], weight[i * part : (i + 1) * part, :])
            hidden_ref[...] = product if i == 0 else hidden_ref[...] + product
        sums_ref[...] = jnp.zeros_like(sums_ref)

        def block(at, first, span):
            x = rows_ref[at, :].astype(f32)
            valid = valid_rows(scalar, extra, first, span)
            branch = hidden_ref[at, :] + vec_ref[2:3]
            add_row(sums_ref, 0, masked_squares(x, valid))
            add_row(sums_ref, 1, masked_squares(branch, valid))
            count = jnp.sum(valid.astype(f32), axis=0, keepdims=True)
            add_row(sums_ref, 2, jnp.broadcast_to(count, (1, width)))
            normal, inverse = normalize(x + branch)
            hidden = normal * vec_ref[3:4] + vec_ref[4:5]
            normal_ref[at, :] = normal
            inverse_ref[at, :] = inverse
            hidden_ref[at, :] = hidden
            low_ref[at, :] = hidden.astype(bf16)

        by_rows(tokens, block)
        spread_total(sums_ref, 0)
        spread_total(sums_ref, 1)
        low_t_ref[...] = turned(low_ref[...])
        for i, ref in enumerate(mixed_refs):
            mixed_t_ref[i * part : (i + 1) * part, :] = turned(ref[...])

    return call(
        body,
        "after_attention",
        [table, rows, vectors, *mixed, *flat(gathered)],
        [SMEM] + [VMEM] * (2 + count) + [ANY] * 4,
        [
            shape(tokens, width, f32),
            shape(tokens, width, bf16),
            shape(width, tokens, bf16),
            shape(width, tokens, bf16),
            shape(tokens, width, f32),
            shape(tokens, 1, f32),
            shape(3, width, f32),
        ],
        [out_piece.whole(), pltpu.SemaphoreType.DMA((1,))],
        time=3.5,
    )


def gelu_and_slope(u):
    phi = 0.5 * lax.erf(u * math.sqrt(0.5)) + 0.5
    bell = jnp.exp(-0.5 * (u * u)) * (1.0 / math.sqrt(2.0 * math.pi))
    return u * phi, phi + u * bell


def feed_up(links, table, low, up_bias, gathered, up_piece):
    tokens, width = low.shape
    inner = up_bias.shape[1]

    def body(scalar, low_ref, bias_ref, *refs):
        act_ref, act_t_ref, slope_ref, weight, sem = refs[4:]
        up_piece.fetch(scalar, sides(refs), weight, sem.at[0])
        up_piece.ready(weight, sem.at[0])

        def forward(j, carry):
            at = aligned(j * width, width, LANES)
            value, slope = gelu_and_slope(dot(low_ref[...], weight[:, at]) + bias_ref[:, at])
            value = value.astype(bf16)
            act_ref[:, at] = value
            act_t_ref[at, :] = turned(value)
            slope_ref[:, at] = slope.astype(bf16)
            return carry

        lax.fori_loop(0, inner // width, forward, 0)

    return call(
        body,
        "feed_up",
        [table, low, up_bias, *flat(gathered)],
        [SMEM] + [VMEM] * 2 + [ANY] * 4,
        [
            shape(tokens, inner, bf16),
            shape(inner, tokens, bf16),
            shape(tokens, inner, bf16),
        ],
        [up_piece.whole(), pltpu.SemaphoreType.DMA((1,))],
        time=8,
    )


def share(core, value, at, keep_ref, send_ref):
    span = value.shape[1] // 2
    low, high = value[:, :span], value[:, span:]
    even = core == 0
    keep_ref[at, :] = jnp.where(even, low, high)
    send_ref[at, :] = jnp.where(even, high, low)


def feed_down(links, table, act, hidden, vectors, cotangent, gathered, down_piece):
    tokens, width = hidden.shape
    inner = act.shape[1]
    extra = 4 * links.dp + 1
    dp = links.dp

    def body(scalar, act_ref, hidden_ref, vec_ref, cot_ref, *refs):
        out_ref, resid_ref, grad_ref, keep_ref, send_ref, sums_ref, weight, sem = refs[4:]
        down_piece.fetch(scalar, sides(refs), weight, sem.at[0])
        down_piece.ready(weight, sem.at[0])
        resid_ref[...] = dot(act_ref[...], weight[...])
        sums_ref[...] = jnp.zeros_like(sums_ref)

        def block(at, first, span):
            branch = resid_ref[at, :] + vec_ref[5:6]
            valid = valid_rows(scalar, extra, first, span)
            add_row(sums_ref, 3, masked_squares(branch, valid))
            normal, inverse = normalize(hidden_ref[at, :] + branch)
            out_ref[at, :] = (normal * vec_ref[6:7] + vec_ref[7:8]).astype(bf16)
            grads = cot_ref[at, :].astype(f32)
            add_row(sums_ref, 1, column_sums(grads * normal))
            add_row(sums_ref, 2, column_sums(grads))
            resid = norm_back(grads, normal, inverse, vec_ref[6:7])
            resid_ref[at, :] = resid
            grad_ffn = resid.astype(bf16)
            grad_ref[at, :] = grad_ffn
            add_row(sums_ref, 0, column_sums(grad_ffn.astype(f32)))
            share(scalar[4 * dp], grad_ffn, at, keep_ref, send_ref)

        by_rows(tokens, block)
        spread_total(sums_ref, 3)

    return call(
        body,
        "feed_down",
        [table, act, hidden, vectors, cotangent, *flat(gathered)],
        [SMEM] + [VMEM] * 4 + [ANY] * 4,
        [
            shape(tokens, width, bf16),
            shape(tokens, width, f32),
            shape(tokens, width, bf16),
            shape(tokens, width // 2, bf16),
            shape(tokens, width // 2, bf16),
            shape(4, width, f32),
        ],
        [down_piece.whole(), pltpu.SemaphoreType.DMA((1,))],
        time=6,
    )


def feed_back(links, table, side, slope, so_far, grad_ffn, up, down, pieces):
    tokens, width = so_far.shape
    up_piece, down_piece = pieces
    span = up_piece.columns
    block = width if span % width == 0 else span
    dp = links.dp

    def body(scalar, slope_ref, so_far_ref, grad_ref, um, ul, *refs):
        hidden_ref, out_ref, bias_ref, up_w, down_w, sems = refs[4:]
        core = scalar[4 * dp]
        half = core if side == 0 else 1 - core
        down_piece.fetch_rows(scalar, half, sides(refs), down_w, sems.at[1])
        up_piece.fetch_side(scalar, side, (um, ul), up_w, sems.at[0])
        hidden_ref[...] = so_far_ref[...]
        down_piece.ready(down_w, sems.at[1])
        up_piece.ready(up_w, sems.at[0])

        def backward(j, carry):
            here = aligned(j * block, block, LANES)
            at = aligned(half * span + j * block, block, LANES)
            grads = dot_rows(grad_ref[...], down_w[here, :]) * slope_ref[:, at].astype(f32)
            grads = grads.astype(bf16)
            bias_ref[:, here] = column_sums(grads.astype(f32))
            hidden_ref[...] += dot_rows(grads, up_w[:, here])
            out_ref[:, here] = grads
            return carry

        lax.fori_loop(0, span // block, backward, 0)

    return call(
        body,
        "feed_back",
        [table, slope, so_far, grad_ffn, *map(far, up[side]), *flat(down)],
        [SMEM] + [VMEM] * 3 + [ANY] * 6,
        [shape(tokens, width, f32), shape(tokens, span, bf16), shape(1, span, f32)],
        [
            pltpu.VMEM((width, span), bf16),
            pltpu.VMEM((span, width), bf16),
            pltpu.SemaphoreType.DMA((2,)),
        ],
        time=0.01,
    )


def before_attention(links, table, grad_hidden, normal, inverse, vectors, gathered, piece):
    tokens, width = normal.shape

    def body(scalar, grad_ref, normal_ref, inverse_ref, vec_ref, *refs):
        resid_ref, gm_ref, keep_ref, send_ref, sums_ref, weight, whole, sem = refs[4:]
        piece.fetch(scalar, sides(refs), weight, sem.at[0])
        sums_ref[...] = jnp.zeros_like(sums_ref)

        def block(at, first, span):
            grads = grad_ref[at, :]
            normal_ = normal_ref[at, :]
            add_row(sums_ref, 1, column_sums(grads * normal_))
            add_row(sums_ref, 2, column_sums(grads))
            resid = norm_back(grads, normal_, inverse_ref[at, :], vec_ref[3:4])
            resid_ref[at, :] = resid
            grad_attn = resid.astype(bf16)
            whole[at, :] = grad_attn
            add_row(sums_ref, 0, column_sums(grad_attn.astype(f32)))
            share(scalar[4 * links.dp], grad_attn, at, keep_ref, send_ref)

        by_rows(tokens, block)
        piece.ready(weight, sem.at[0])
        gm_ref[...] = dot_rows(whole[...], weight[...]).astype(bf16)

    return call(
        body,
        "before_attention",
        [table, grad_hidden, normal, inverse, vectors, *flat(gathered)],
        [SMEM] + [VMEM] * 4 + [ANY] * 4,
        [
            shape(tokens, width, f32),
            shape(tokens, width, bf16),
            shape(tokens, width // 2, bf16),
            shape(tokens, width // 2, bf16),
            shape(3, width, f32),
        ],
        [piece.whole(), pltpu.VMEM((tokens, width), bf16), pltpu.SemaphoreType.DMA((1,))],
        time=0.01,
    )


def weight_gradient(name, links, table, left, right, rows):
    outer, tokens = left[0].shape
    columns = right[0].shape[1]
    block = min(outer, 768)
    wide = min(columns, 512)

    def body(scalar, lm, lt, rm, rt, *refs):
        tile = refs[-1]

        def one(j, carry):
            at = aligned(j // (columns // wide) * block, block, 8)
            to = aligned(j % (columns // wide) * wide, wide, LANES)
            tile[at, to] = dot(lm[at, :], rm[:, to]) + dot(lt[at, :], rt[:, to])
            return carry

        lax.fori_loop(0, outer // block * (columns // wide), one, 0)
        place(scalar, links.dp, tile, refs[:3], rows, slice(None))

    return call(
        body,
        name,
        [table, *left, *right],
        [SMEM] + [VMEM] * 4,
        placed(links.dp, rows, columns),
        [pltpu.VMEM((outer, columns), f32)],
    )


class Shares:
    def __init__(self, refs, tokens):
        self.sent, self.kept, self.came = refs
        self.tokens = tokens

    def rows(self, ref, i):
        return ref[i * self.tokens : (i + 1) * self.tokens, :]

    def add(self, one, other):
        return (one.astype(f32) + other.astype(f32)).astype(bf16)

    def own(self):
        return [self.rows(self.kept, 0)] + [
            self.add(self.rows(self.kept, i), self.rows(self.came, 2 + i)) for i in (1, 2)
        ]

    def others(self):
        return [self.rows(self.came, 0)] + [
            self.add(self.rows(self.sent, 4 + i), self.rows(self.came, i)) for i in (1, 2)
        ]

    def partners(self):
        return [self.rows(self.sent, 0)] + [
            self.add(self.rows(self.sent, i), self.rows(self.came, 4 + i)) for i in (1, 2)
        ]


def attention_gradient(name, links, table, rows_t, groups, rows, out=None, vectors=None, folds=0, sums=()):
    width, tokens = rows_t[0].shape
    dp = links.dp
    wide = 3 * LANES
    half = width // 2
    total = wide * len(groups) + (half if out else 0) + (LANES if vectors is not None else 0)
    given = [value for group in groups for value in group]
    more = list(out or []) + ([*vectors, *sums] if vectors is not None else [])

    def body(scalar, xm, xt, *refs):
        group_refs = refs[: len(given)]
        more_refs = list(refs[len(given) : len(given) + len(more)])
        outs = refs[len(given) + len(more) :]
        sum_ref, tile = outs[3], outs[4]
        for g in range(len(groups)):
            shares = Shares(group_refs[3 * g : 3 * g + 3], tokens)
            mine = jnp.concatenate(shares.own(), axis=1)
            theirs = jnp.concatenate(shares.others(), axis=1)
            tile[:, g * wide : (g + 1) * wide] = dot(xm[...], mine) + dot(xt[...], theirs)
            sums_ = column_sums(mine.astype(f32)) + column_sums(theirs.astype(f32))
            sum_ref[g : g + 1, :] = sums_
        at = wide * len(groups)
        if out:
            mm, mt, gm, gt = more_refs[:4]
            tile[:, at : at + half] = dot(mm[...], gm[...]) + dot(mt[...], gt[...])
            at += half
        if vectors is not None:
            sums3, sums2, kept, sent, sums1, *sum_refs = more_refs
            even = scalar[4 * dp] == 0
            bias = jnp.concatenate(
                [
                    jnp.where(even, kept[...], sent[...]),
                    jnp.where(even, sent[...], kept[...]),
                ],
                axis=1,
            )
            biases = [
                jnp.concatenate(
                    [
                        bias[:, (i * folds + j) * rows : (i * folds + j + 1) * rows]
                        for i in range(dp)
                    ],
                    axis=1,
                )
                for j in range(folds)
            ]
            head = jnp.concatenate(
                [jnp.zeros((2, width), f32), sums3[...], sums2[0:3]]
                + biases
                + [sums1[...], sums2[3:4]],
                axis=0,
            )
            every = [ref[i : i + 1, :] for ref in sum_refs for i in range(ref.shape[0])]
            every += [sum_ref[g : g + 1, :] for g in range(len(groups))]
            lane = lax.broadcasted_iota(jnp.int32, (1, width), 1)
            owned = (lane // LANES) % 2 == scalar[4 * dp]
            lines = []
            for j in (0, 2):
                parts = [s[:, j * LANES : (j + 1) * LANES] for s in every for _ in range(2)]
                lines.append(jnp.where(owned, jnp.concatenate(parts, axis=1), 0.0))
            row = lax.broadcasted_iota(jnp.int32, (LANES, width), 0)
            padded = jnp.concatenate(
                [head, jnp.zeros((LANES - head.shape[0], width), f32)], axis=0
            )
            padded = jnp.where(row == 0, lines[0], jnp.where(row == 1, lines[1], padded))
            tile[:, at : at + LANES] = turned(padded)
        place(scalar, dp, tile, outs[:3], rows, slice(None))

    return call(
        body,
        name,
        [table, *rows_t, *given, *more],
        [SMEM] + [VMEM] * (2 + len(given) + len(more)),
        placed(dp, rows, total) + [shape(len(groups), wide, f32)],
        [pltpu.VMEM((width, total), f32)],
    )


def input_gradient(links, table, groups, resid, gathered, qkv_piece):
    tokens, width = resid.shape
    given = [value for group in groups for value in group]

    def body(scalar, resid_ref, *refs):
        group_refs = refs[: len(given)]
        out_ref, weight, grads, sem = refs[len(given) + 4 :]
        qkv_piece.fetch(scalar, sides(refs[len(given) :]), weight, sem.at[0])
        core = scalar[4 * links.dp]
        for g in range(len(groups)):
            shares = Shares(group_refs[3 * g : 3 * g + 3], tokens)
            for owner, values in ((core, shares.own()), (1 - core, shares.partners())):
                for j, value in enumerate(values):
                    at = j * width + (2 * g + owner) * LANES
                    grads[:, aligned(at, LANES, LANES)] = value
        qkv_piece.ready(weight, sem.at[0])
        out_ref[...] = resid_ref[...] + dot_rows(grads[...], weight[...])

    return call(
        body,
        "input_gradient",
        [table, resid, *given, *flat(gathered)],
        [SMEM] + [VMEM] * (1 + len(given)) + [ANY] * 4,
        [shape(tokens, width, f32)],
        [qkv_piece.whole(), pltpu.VMEM((tokens, 3 * width), bf16), pltpu.SemaphoreType.DMA((1,))],
        time=20,
    )[0]


def closing(links, table, early, late, folds, width):
    rows = early[0].shape[0]
    wide = 3 * LANES
    half = width // 2
    base = 8

    def body(scalar, em, et, lm, lt, *outs):
        qkv_ref, out_ref, *vec_refs, up_ref, rms_ref = outs

        def write(core):
            for owner, early_ref, late_ref in ((core, em, lm), (1 - core, et, lt)):
                groups = [(early_ref, 0), (early_ref, wide), (late_ref, 0)]
                for g, (ref, first) in enumerate(groups):
                    for j in range(3):
                        at = j * width + (2 * g + owner) * LANES
                        qkv_ref[:, at : at + LANES] = ref[
                            :, first + j * LANES : first + (j + 1) * LANES
                        ].astype(f32)
                out_ref[:, owner * half : (owner + 1) * half] = early_ref[
                    :, 2 * wide : 2 * wide + half
                ].astype(f32)

        for core in range(2):
            pl.when(scalar[4 * links.dp] == core)(lambda core=core: write(core))
        last = slice(wide, wide + LANES)
        vectors = turned(lm[:, last].astype(f32) + lt[:, last].astype(f32))
        for i, ref in enumerate(vec_refs):
            ref[...] = vectors[i : i + 1]
        for i in range(folds):
            up_ref[:, i * rows : (i + 1) * rows] = vectors[base + i : base + i + 1]
        at = base + folds
        count = vectors[at + 2 : at + 3] * width
        for i, line in enumerate((at, at + 1, at + 3)):
            value = jnp.sqrt(vectors[line : line + 1] / count + 1e-06)
            rms_ref[:, i : i + 1] = value[:, 0:1]

    return call(
        body,
        "closing",
        [table, *early, *late],
        [SMEM] + [VMEM] * 4,
        [shape(rows, 3 * width, f32), shape(rows, width, f32)]
        + [shape(1, rows, f32)] * base
        + [shape(1, folds * rows, f32), shape(1, 3, f32)],
    )


def settle(links, reduction):
    mine = reduction.finish()
    return mine, links.swap(mine)


def shards(
    tokens,
    lengths,
    qkv_weight,
    query_bias,
    value_bias,
    out_weight,
    out_bias,
    norm1_gain,
    norm1_shift,
    up_weight,
    up_bias,
    down_weight,
    down_bias,
    norm2_gain,
    norm2_shift,
    cotangent,
):
    seq_dev, ctx_tok, width = tokens.shape
    assert seq_dev == 1 and width // HEADS == LANES // 2
    scale = (width // HEADS) ** (-0.5)
    links = Links()
    dp = links.dp
    rows = tokens.reshape(ctx_tok, width)
    cot = cotangent.reshape(ctx_tok, width)
    block = lax.axis_index("ctx")
    start = block * ctx_tok
    table = links.table(lengths[0], start)

    shard = qkv_weight.shape[0]
    inner = down_weight.shape[0] * dp
    folds = down_weight.shape[0] // shard
    half = [w.shape[1] // 2 for w in (qkv_weight, out_weight, up_weight, down_weight)]
    qkv_piece = Piece(dp, shard, half[0], 0)
    vector_piece = Piece(dp, shard, LANES, half[0])
    up_piece = Piece(dp, shard, half[2], 0)
    out_piece = Piece(dp, shard, half[1], half[2])
    down_piece = Piece(dp, down_weight.shape[0], half[3], 0)
    ffn_pieces = (up_piece, down_piece)

    columns = [query_bias, value_bias, out_bias, norm1_gain, norm1_shift]
    columns += [down_bias, norm2_gain, norm2_shift]
    base = len(columns)
    columns += [up_bias[i * shard : (i + 1) * shard] for i in range(folds)]
    packed = jnp.stack(columns, axis=1)
    packed = jnp.pad(packed, ((0, 0), (0, LANES - packed.shape[1])))
    qkv_sent = jnp.concatenate([half_columns(links, qkv_weight), packed], axis=1)
    up_sent = jnp.concatenate(
        [half_columns(links, up_weight), half_columns(links, out_weight)], axis=1
    )
    down_sent = half_columns(links, down_weight)

    qkv_held = joined(links.cross(qkv_sent))
    up_held = links.cross(after(up_sent, qkv_held))
    down_sent = after(down_sent, up_held)
    qkv_held = links.first(qkv_held)
    qkv = links.second(after(qkv_held, up_held[1]), *up_held)
    up_held = after(joined(up_held), qkv[0][1])
    query, kv, vectors, up_bias_row, rows_t = project(
        links, table, after(rows, up_held), qkv, qkv_piece, vector_piece, scale, base, folds
    )
    early_steps = []

    def ready(more):
        early_steps.append(more)
        return after(more, query)

    down_held = links.cross_slowly(after(down_sent, up_held), ready)
    up_held = links.first(up_held, query)
    kv = after(kv, up_held, *early_steps)
    rows_t = [rows_t, links.swap(rows_t)]
    if links.ctx == 2:
        parts = [kv, links.swap(kv)]
        starts = [start, (1 - block) * ctx_tok]
    else:
        parts = [lax.all_gather(kv, "ctx", axis=0, tiled=True)]
        starts = [jnp.int32(0)]
    groups = 3
    count = width // LANES // groups
    forward = []
    waits = [(), (), ()]
    for i in range(groups):
        given = after(query, *waits[i], *(forward[-1][1:2] if forward else ()))
        forward.append(attend(given, parts, starts, lengths[0], i * count, count))
        if i == 0:
            down_held = joined(down_held, forward[0][1])
            waits[1] = (down_held,)
    up = links.second(up_held, forward[1][1])
    down_held = links.first(after(down_held, forward[1][1]), forward[2][1])
    mixed = [f[1] for f in forward]
    hidden, low, low_t, mixed_t, normal, deviation, sums1 = after_attention(
        links, table, after(rows, down_held), mixed, vectors, up, out_piece
    )
    low_t = [low_t, links.swap(low_t)]
    mixed_t = [mixed_t, links.swap(mixed_t)]
    act, act_t, slope = feed_up(links, table, low, up_bias_row, up, up_piece)
    down = links.second(after(down_held, forward[2][1]), act)
    act_t = [act_t, links.swap(after(act_t, down[1][1]))]
    output, resid2, grad_ffn, ffn_keep, ffn_send, sums2 = feed_down(
        links, table, act, hidden, vectors, cot, down, down_piece
    )
    ffn_came = links.swap(ffn_send)
    down_sum = Sum(
        links,
        weight_gradient(
            "down_gradient", links, table, act_t, [ffn_keep, ffn_came], down_piece.rows
        ),
    )
    given = after(resid2, down_sum.prepare())
    down_sum.send()
    grad_hidden, upper_send, bias_sent = feed_back(
        links, table, 1, slope, given, grad_ffn, up, down, ffn_pieces
    )
    upper_came = links.swap(upper_send)
    grad_hidden, upper_keep, bias_kept = feed_back(
        links, table, 0, slope, grad_hidden, grad_ffn, up, down, ffn_pieces
    )
    up_sum = Sum(
        links,
        weight_gradient(
            "up_gradient", links, table, low_t, [upper_keep, upper_came], up_piece.rows
        ),
    )
    down_sum.hold(grad_hidden)
    given = after(grad_hidden, up_sum.prepare(), down_sum.prepare())
    up_sum.send()
    down_sum.send()
    resid1, grad_mixed, attn_keep, attn_send, sums3 = before_attention(
        links, table, given, normal, deviation, vectors, up, out_piece
    )
    out_parts = [*mixed_t, attn_keep, links.swap(attn_send)]

    def back_through(i, given):
        turned_mixed, _, weights, inverse = forward[i]
        sent, kept = attend_back(
            given,
            parts,
            grad_mixed,
            turned_mixed,
            weights,
            inverse,
            scale,
            i * count,
            links.core,
        )
        if links.ctx == 2:
            return [sent, kept, links.swap(sent)]
        whole = []
        for value in (sent, kept):
            keys, values = jnp.split(value[ctx_tok:], 2, axis=0)
            both = lax.psum_scatter(
                jnp.concatenate([keys, values], axis=1), "ctx", scatter_dimension=0, tiled=True
            )
            whole.append([value[:ctx_tok], both[:, :LANES], both[:, LANES:]])
        blank = jnp.zeros((4 * ctx_tok, LANES), bf16)
        sent = jnp.concatenate(whole[0] + [blank], axis=0)
        return [sent, jnp.concatenate(whole[1], axis=0), links.swap(sent)]

    given = after(query, grad_mixed)
    back = [back_through(0, given)]
    back.append(back_through(1, after(query, back[0][1])))
    down_sum.hold(back[1][1])
    up_sum.hold(back[1][1])
    given = after(rows_t[0], down_sum.prepare(), up_sum.prepare())
    down_sum.send()
    up_sum.send()
    *early, early_sums = attention_gradient(
        "early_gradient", links, table, [given, rows_t[1]], back[:2], shard, out=out_parts
    )
    early_sum = Sum(links, early)
    down_sum.hold(early[2])
    up_sum.hold(early[2])
    given = after(query, early_sum.prepare(), down_sum.prepare(), up_sum.prepare())
    early_sum.send()
    down_sum.send()
    up_sum.send()
    back.append(back_through(2, given))
    up_sum.hold(back[2][1])
    early_sum.hold(back[2][1])
    down_sum.hold(back[2][1])
    up_sum.hold(back[2][1])
    given = after(rows_t[0], early_sum.prepare(), up_sum.prepare())
    early_sum.send()
    up_sum.send()
    *late, _ = attention_gradient(
        "late_gradient",
        links,
        table,
        [given, rows_t[1]],
        back[2:],
        shard,
        vectors=[sums3, sums2, bias_kept, bias_sent, sums1],
        folds=folds,
        sums=[early_sums],
    )
    late_sum = Sum(links, late, direct=True)
    down_sum.hold(late[2])
    down_mine = down_sum.finish()
    given = after(resid1, late_sum.prepare(), down_mine)
    late_sum.send()
    input_grad = input_gradient(links, table, back, given, qkv, qkv_piece)
    late_sum.hold(input_grad)
    early_sum.hold(input_grad)
    up_sum.hold(input_grad)
    up_mine = up_sum.finish()
    down_grad = both_halves(links, down_mine, links.swap(down_mine))
    up_grad = both_halves(links, up_mine, links.swap(up_mine))
    early = settle(links, early_sum)
    late = settle(links, late_sum)
    qkv_grad, out_grad, *sums, up_bias_grad, stream_rms = closing(
        links, table, early, late, folds, width
    )
    sums = [value.reshape(shard) for value in sums]
    return (
        output.reshape(seq_dev, ctx_tok, width),
        input_grad.reshape(seq_dev, ctx_tok, width),
        stream_rms.reshape(3),
        qkv_grad,
        sums[0],
        sums[1],
        out_grad,
        sums[2],
        sums[3],
        sums[4],
        up_grad,
        up_bias_grad.reshape(-1),
        down_grad,
        sums[5],
        sums[6],
        sums[7],
    )


def solution(mesh):
    in_specs = (
        P("dp", "ctx", None),
        P("dp"),
        P("dp", None),
        P("dp"),
        P("dp"),
        P("dp", None),
        P("dp"),
        P("dp"),
        P("dp"),
        P("dp", None),
        P("dp"),
        P("dp", None),
        P("dp"),
        P("dp"),
        P("dp"),
        P("dp", "ctx", None),
    )
    out_specs = (
        P("dp", "ctx", None),
        P("dp", "ctx", None),
        P(),
        P("dp", None),
        P("dp"),
        P("dp"),
        P("dp", None),
        P("dp"),
        P("dp"),
        P("dp"),
        P("dp", None),
        P("dp"),
        P("dp", None),
        P("dp"),
        P("dp"),
        P("dp"),
    )
    return jax.shard_map(shards, mesh=mesh, in_specs=in_specs, out_specs=out_specs, check_vma=False)
```

```python
import math

import jax
import jax.numpy as jnp
from jax import lax
from jax.experimental import pallas as pl
from jax.experimental.pallas import tpu as pltpu
from jax.sharding import PartitionSpec as P

HEADS = 12
LANES = 128
VECTORS = 16
VMEM_BYTES = 24 << 20
FLOPS = 300_000_000
BYTES = 900_000

masked_score = -1e30
norm_eps = 1e-05
f32 = jnp.float32
bf16 = jnp.bfloat16


def low_precision(value):
    return lax.reduce_precision(value, exponent_bits=8, mantissa_bits=7)


class Links:
    def __init__(self):
        self.dp = lax.axis_size("dp")
        self.ctx = lax.axis_size("ctx")
        self.bits = self.dp.bit_length() - 1
        assert self.dp == 1 << self.bits and self.bits >= 2 and self.ctx % 2 == 0
        self.core = lax.axis_index("ctx") % 2
        self.me = lax.axis_index("dp")
        self.upper = []
        bit = self.bits - 1
        while bit >= 2:
            size = 2 if (bit - 1) % 2 == 0 else 1
            self.upper.append(tuple(range(bit, bit - size, -1)))
            bit -= size

    def swap(self, value):
        return lax.ppermute(value, "ctx", [(i, i ^ 1) for i in range(self.ctx)])

    def hop(self, value, mask_even, mask_odd):
        pairs = []
        for block in range(self.ctx):
            mask = mask_odd if block % 2 else mask_even
            pairs += [(block * self.dp + i, block * self.dp + (i ^ mask)) for i in range(self.dp)]
        return lax.ppermute(value, ("ctx", "dp"), pairs)

    def places(self, core):
        position = lax.iota(jnp.int32, self.dp)
        quarter = self.dp // 4
        first = (position // quarter) % 2
        second = position // (2 * quarter)
        mask = first * (1 + core) + second * (2 - core)
        for i in range(self.bits - 2):
            mask = mask + ((position >> i) % 2) * (1 << (self.bits - 1 - i))
        return jnp.bitwise_xor(self.me, mask)

    def spots(self, core):
        mask = jnp.bitwise_xor(self.me, lax.iota(jnp.int32, self.dp))
        low, high = mask % 2, (mask // 2) % 2
        first = jnp.where(core == 0, low, high)
        second = jnp.where(core == 0, high, low)
        quarter = self.dp // 4
        spot = first * quarter + second * (2 * quarter)
        for i in range(self.bits - 2):
            spot = spot + ((mask >> (self.bits - 1 - i)) % 2) * (1 << i)
        return spot

    def table(self, *more):
        parts = [self.places(self.core), self.places(1 - self.core)]
        parts += [self.spots(self.core), self.spots(1 - self.core)]
        parts += [jnp.reshape(value, (1,)) for value in (self.core,) + more]
        return jnp.concatenate(parts).astype(jnp.int32)

    def masks(self, bits):
        return [
            sum(((i >> j) & 1) << bit for j, bit in enumerate(bits)) for i in range(1 << len(bits))
        ]

    def cross(self, piece):
        held = [piece]
        for bits in self.upper:
            here = jnp.concatenate(held, axis=0) if len(held) > 1 else held[0]
            held = [here] + [self.hop(here, mask, mask) for mask in self.masks(bits)[1:]]
        return held

    def cross_slowly(self, piece, ready):
        held = piece
        masks = [1 << bit for bits in self.upper for bit in bits]
        for i, mask in enumerate(masks):
            more = self.hop(held, mask, mask)
            if i < len(masks) - 1:
                more = ready(more)
            held = [held, more]
            if i < len(masks) - 1:
                held = jnp.concatenate(held, axis=0)
        return held

    def first(self, held, *waits):
        more = self.hop(held, 1, 2)
        return jnp.concatenate([held, after(more, *waits) if waits else more], axis=0)

    def second(self, held, *waits):
        early = self.swap(held)
        more = self.hop(held, 2, 1)
        if waits:
            early, more = after((early, more), *waits)
        return [held, more], [early, self.swap(more)]


def joined(held, *waits):
    return jnp.concatenate(after(tuple(held), *waits) if waits else held, axis=0)


class Sum:
    def __init__(self, links, kept, direct=False):
        self.links = links
        self.kept = kept
        self.quarter = kept[0].shape[0]
        self.rows = 4 * self.quarter
        self.terms = []
        self.steps = [[(2, 1)], [(1, 2)]]
        for bits in reversed(links.upper):
            if direct:
                self.steps.append([(mask, mask) for mask in links.masks(bits)[1:]])
            else:
                self.steps += [[(1 << bit, 1 << bit)] for bit in reversed(bits)]
        self.ready = None

    def total(self, start, span):
        index = min(2, start // self.quarter)
        first = start - index * self.quarter
        value = self.kept[index]
        if span != value.shape[0]:
            value = lax.slice_in_dim(value, first, first + span, axis=0)
        if not self.terms:
            return value
        value = value.astype(f32)
        for term in self.terms:
            parts = [
                lax.slice_in_dim(part, start, start + span, axis=0).astype(f32) for part in term
            ]
            if len(parts) == 1:
                value = low_precision(value + parts[0])
            else:
                value = low_precision((value + parts[0]) + (parts[1] + parts[2]))
        return value.astype(bf16)

    def prepare(self):
        masks = self.steps[0]
        self.rows //= len(masks) + 1
        self.ready = [self.total((i + 1) * self.rows, self.rows) for i in range(len(masks))]
        return self.ready

    def send(self):
        if self.ready is None:
            self.prepare()
        masks = self.steps.pop(0)
        self.terms.append(
            tuple(self.links.hop(value, *mask) for value, mask in zip(self.ready, masks))
        )
        self.ready = None

    def hold(self, other):
        self.terms[-1] = tuple(after(value, other) for value in self.terms[-1])

    def finish(self):
        while self.steps:
            self.send()
        mine = self.total(0, self.rows)
        step = 2
        while step < self.links.ctx:
            pairs = [(i, i ^ step) for i in range(self.links.ctx)]
            other = lax.ppermute(mine, "ctx", pairs)
            mine = low_precision(mine.astype(f32) + other.astype(f32)).astype(bf16)
            step *= 2
        return mine


def after(value, *others):
    return lax.optimization_barrier((value, others))[0]


def half_columns(links, value):
    span = value.shape[1] // 2
    return lax.dynamic_slice_in_dim(value, links.core * span, span, 1)


def both_halves(links, mine, theirs):
    even = links.core == 0
    return jnp.concatenate(
        [jnp.where(even, mine, theirs), jnp.where(even, theirs, mine)], axis=1
    ).astype(f32)


def dot(left, right):
    return jnp.dot(left, right, preferred_element_type=f32)


def dot_rows(left, right):
    return lax.dot_general(left, right, (((1,), (1,)), ((), ())), preferred_element_type=f32)


def turned(value):
    return jnp.transpose(value)


def aligned(start, size, unit):
    return pl.ds(pl.multiple_of(start, unit), size)


SMEM = pl.BlockSpec(memory_space=pltpu.SMEM)
ANY = pl.BlockSpec(memory_space=pl.ANY)
VMEM = pl.BlockSpec(memory_space=pltpu.VMEM)


def cost(microseconds):
    return pl.CostEstimate(
        flops=int(microseconds * FLOPS), transcendentals=0, bytes_accessed=int(microseconds * BYTES)
    )


def call(body, name, sources, in_specs, outs, scratch=(), time=5):
    return pl.pallas_call(
        body,
        name=name,
        out_shape=outs,
        in_specs=in_specs,
        out_specs=[VMEM] * len(outs),
        scratch_shapes=list(scratch),
        compiler_params=pltpu.CompilerParams(vmem_limit_bytes=VMEM_BYTES),
        cost_estimate=cost(time),
    )(*sources)


def shape(rows, columns, dtype):
    return jax.ShapeDtypeStruct((rows, columns), dtype)


class Piece:
    def __init__(self, dp, rows, columns, first):
        self.dp, self.rows, self.columns, self.first = dp, rows, columns, first

    def fetch(self, scalar, sides, whole, sem):
        core = scalar[4 * self.dp]
        for side, sources in enumerate(sides):
            half = core if side == 0 else 1 - core
            count = self.dp // len(sources)
            for i, source in enumerate(sources):

                def one(position, carry, side=side, source=source, half=half, base=i * count):
                    owner = scalar[side * self.dp + base + position]
                    pltpu.make_async_copy(
                        source.at[
                            aligned(position * self.rows, self.rows, 8),
                            pl.ds(self.first, self.columns),
                        ],
                        whole.at[
                            aligned(owner * self.rows, self.rows, 8),
                            aligned(half * self.columns, self.columns, LANES),
                        ],
                        sem,
                    ).start()
                    return carry

                lax.fori_loop(0, count, one, 0)

    def fetch_side(self, scalar, side, sources, whole, sem):
        count = self.dp // len(sources)
        for i, source in enumerate(sources):

            def one(position, carry, source=source, base=i * count):
                owner = scalar[side * self.dp + base + position]
                pltpu.make_async_copy(
                    source.at[
                        aligned(position * self.rows, self.rows, 8),
                        pl.ds(self.first, self.columns),
                    ],
                    whole.at[aligned(owner * self.rows, self.rows, 8), :],
                    sem,
                ).start()
                return carry

            lax.fori_loop(0, count, one, 0)

    def fetch_rows(self, scalar, part, sides, whole, sem):
        core = scalar[4 * self.dp]
        for side, sources in enumerate(sides):
            half = core if side == 0 else 1 - core
            count = self.dp // len(sources)

            def one(i, carry, side=side, sources=sources, half=half, count=count):
                spot = scalar[(2 + side) * self.dp + part * (self.dp // 2) + i]
                for j, source in enumerate(sources):

                    @pl.when(spot // count == j)
                    def _(source=source, j=j):
                        pltpu.make_async_copy(
                            source.at[
                                aligned((spot - j * count) * self.rows, self.rows, 8),
                                pl.ds(self.first, self.columns),
                            ],
                            whole.at[
                                aligned(i * self.rows, self.rows, 8),
                                aligned(half * self.columns, self.columns, LANES),
                            ],
                            sem,
                        ).start()

                return carry

            lax.fori_loop(0, self.dp // 2, one, 0)

    def ready(self, whole, sem):
        pltpu.make_async_copy(whole, whole, sem).wait()

    def whole(self):
        return pltpu.VMEM((self.dp * self.rows, 2 * self.columns), bf16)


def place(scalar, dp, tile, outs, rows, columns):
    base = 0
    for out in outs:
        count = out.shape[0] // rows

        def one(i, carry, out=out, base=base):
            owner = scalar[base + i]
            out[aligned(i * rows, rows, 8), columns] = tile[aligned(owner * rows, rows, 8), :].astype(
                bf16
            )
            return carry

        lax.fori_loop(0, count, one, 0)
        base += count


def placed(dp, rows, columns):
    return [
        shape(rows * dp // 4, columns, bf16),
        shape(rows * dp // 4, columns, bf16),
        shape(rows * dp // 2, columns, bf16),
    ]


def in_hbm(*dims):
    *dims, dtype = dims
    return pltpu.HBM(tuple(dims), dtype)


def sides(refs):
    return (refs[:2], refs[2:4])


def far(value):
    return pltpu.with_memory_space_constraint(value, pltpu.HBM)


def flat(gathered):
    return [far(value) for value in (*gathered[0], *gathered[1])]


def project(links, table, rows, gathered, qkv_piece, vector_piece, scale, base, folds):
    tokens, width = rows.shape
    shard = width // links.dp

    def body(scalar, rows_ref, *refs):
        q_ref, kv_ref, vec_ref, bias_ref, rows_t_ref, weight, vecs, sems = refs[4:]
        pieces = sides(refs)
        vector_piece.fetch_side(scalar, 0, pieces[0], vecs, sems.at[1])
        qkv_piece.fetch(scalar, pieces, weight, sems.at[0])
        vector_piece.ready(vecs, sems.at[1])
        vectors = turned(vecs[...].astype(f32))[:VECTORS]
        vec_ref[...] = vectors
        bias_ref[...] = jnp.concatenate(
            [
                vectors[base + j : base + j + 1, i * shard : (i + 1) * shard]
                for i in range(links.dp)
                for j in range(folds)
            ],
            axis=1,
        )
        rows_t_ref[...] = turned(rows_ref[...])
        qkv_piece.ready(weight, sems.at[0])
        x = rows_ref[...]
        query = (dot(x, weight[:, :width]) + vectors[0:1]).astype(bf16)
        q_ref[...] = (query.astype(f32) * scale).astype(bf16)
        kv_ref[:, :width] = dot(x, weight[:, width : 2 * width]).astype(bf16)
        kv_ref[:, width:] = (dot(x, weight[:, 2 * width :]) + vectors[1:2]).astype(bf16)

    return call(
        body,
        "qkv",
        [table, rows, *flat(gathered)],
        [SMEM, VMEM] + [ANY] * 4,
        [
            shape(tokens, width, bf16),
            shape(tokens, 2 * width, bf16),
            shape(VECTORS, width, f32),
            shape(1, folds * width, f32),
            in_hbm(width, tokens, bf16),
        ],
        [qkv_piece.whole(), pltpu.VMEM((width, LANES), bf16), pltpu.SemaphoreType.DMA((2,))],
        time=5,
    )


def pair_specs(parts, pairs, base):
    specs = []
    for part in parts:
        rows = part.shape[0]
        specs.append(pl.BlockSpec((rows, LANES), lambda p, s: (0, base + p)))
        specs.append(pl.BlockSpec((rows, LANES), lambda p, s: (0, pairs + base + p)))
    return specs


def first_lanes(shape_, count):
    return (lax.broadcasted_iota(jnp.int32, shape_, 1) < count).astype(f32).astype(bf16)


def head_blocks(query):
    lane = lax.broadcasted_iota(jnp.int32, query.shape, 1)
    zero = jnp.zeros_like(query)
    half = LANES // 2
    return jnp.concatenate(
        [jnp.where(lane < half, query, zero), jnp.where(lane >= half, query, zero)], axis=0
    )


def attend(query, parts, starts, length, base, count):
    tokens, width = query.shape
    pairs = width // LANES
    span = sum(part.shape[0] for part in parts)
    half = LANES // 2
    chunk = min(256, tokens)
    scalars = jnp.concatenate(
        [jnp.reshape(v, (1,)).astype(jnp.int32) for v in [length, *starts]]
    )

    def body(scalar, q_ref, *refs):
        kv_refs = refs[: 2 * len(parts)]
        mixed_t_ref, mixed_ref, p_ref, inverse_ref, bias = refs[2 * len(parts) :]

        @pl.when(pl.program_id(0) == 0)
        def _():
            at = 0
            for i, part in enumerate(parts):
                rows = part.shape[0]
                position = scalar[1 + i] + lax.broadcasted_iota(jnp.int32, (rows, LANES), 0)
                lane = lax.broadcasted_iota(jnp.int32, (rows, LANES), 1)
                hidden = jnp.where(position < scalar[0], 0.0, masked_score)
                bias[at : at + rows, :] = jnp.where(lane == 0, hidden, 0.0).astype(bf16)
                at += rows

        keys = jnp.concatenate([ref[...] for ref in kv_refs[0::2]], axis=0)
        values = jnp.concatenate([ref[...] for ref in kv_refs[1::2]], axis=0)
        keys = jnp.concatenate([keys, bias[...]], axis=1)
        values_t = jnp.concatenate([turned(values), jnp.ones((16, span), bf16)], axis=0)
        queries = head_blocks(q_ref[...])
        queries = jnp.concatenate([queries, first_lanes(queries.shape, 1)], axis=1)
        for at in range(0, 2 * tokens, chunk):
            scores = dot_rows(keys, queries[at : at + chunk])
            peak = jnp.max(scores, axis=0, keepdims=True)
            weights = jnp.exp(scores - peak).astype(bf16)
            p_ref[:, at : at + chunk] = weights
        sums = dot(values_t, p_ref[...])
        inverse = 1.0 / sums[LANES : LANES + 1]
        inverse_ref[...] = inverse
        mixed_t_ref[:half, :] = sums[:half, :tokens] * inverse[:, :tokens]
        mixed_t_ref[half:, :] = sums[half:LANES, tokens:] * inverse[:, tokens:]
        mixed_ref[...] = turned(mixed_t_ref[...]).astype(bf16)

    sources = [query]
    for part in parts:
        sources += [part, part]
    return pl.pallas_call(
        body,
        name="attend",
        cost_estimate=cost(8),
        out_shape=[
            in_hbm(count * LANES, tokens, f32),
            shape(tokens, count * LANES, bf16),
            in_hbm(count, span, 2 * tokens, bf16),
            in_hbm(count, 1, 2 * tokens, f32),
        ],
        grid_spec=pltpu.PrefetchScalarGridSpec(
            num_scalar_prefetch=1,
            grid=(count,),
            in_specs=[pl.BlockSpec((tokens, LANES), lambda p, s: (0, base + p))]
            + pair_specs(parts, pairs, base),
            out_specs=[
                pl.BlockSpec((LANES, tokens), lambda p, s: (p, 0)),
                pl.BlockSpec((tokens, LANES), lambda p, s: (0, p)),
                pl.BlockSpec((None, span, 2 * tokens), lambda p, s: (p, 0, 0)),
                pl.BlockSpec((None, 1, 2 * tokens), lambda p, s: (p, 0, 0)),
            ],
            scratch_shapes=[pltpu.VMEM((span, LANES), bf16)],
        ),
        compiler_params=pltpu.CompilerParams(vmem_limit_bytes=min(56 << 20, VMEM_BYTES * max(1, span // 1024))),
    )(scalars, *sources)


def attend_back(query, parts, grad_mixed, mixed_t, weights, inverse, scale, base, core):
    tokens, width = query.shape
    pairs = width // LANES
    span = sum(part.shape[0] for part in parts)
    half = LANES // 2
    chunk = min(256, tokens)

    def body(_, q_ref, gm_ref, mt_ref, p_ref, inv_ref, *refs):
        kv_refs = refs[: 2 * len(parts)]
        send_ref, keep_ref, ds_ref = refs[2 * len(parts) :]
        keys = jnp.concatenate([ref[...] for ref in kv_refs[0::2]], axis=0)
        values = jnp.concatenate([ref[...] for ref in kv_refs[1::2]], axis=0)
        grads = turned(gm_ref[...].astype(f32))
        inv = inv_ref[...]
        product = grads * mt_ref[...]
        empty = jnp.zeros((half, tokens), bf16)
        even, odd = inv[:, :tokens], inv[:, tokens:]
        delta = jnp.concatenate(
            [
                jnp.sum(product[:half], axis=0, keepdims=True) * even,
                jnp.sum(product[half:], axis=0, keepdims=True) * odd,
            ],
            axis=1,
        )
        top = jnp.concatenate([(grads[:half] * even).astype(bf16), empty], axis=1)
        bottom = jnp.concatenate([empty, (grads[half:] * odd).astype(bf16)], axis=1)
        scaled = jnp.concatenate([top, bottom], axis=0)
        first = (-delta).astype(bf16).astype(f32)
        second = (-delta - first).astype(bf16).astype(f32)
        third = (-delta - first - second).astype(bf16).astype(f32)
        row = lax.broadcasted_iota(jnp.int32, (LANES, 2 * tokens), 0)
        limbs = jnp.where(
            row == 0, first, jnp.where(row == 1, second, jnp.where(row == 2, third, 0.0))
        ).astype(bf16)
        right = jnp.concatenate([scaled, limbs], axis=0)
        left = jnp.concatenate([values, first_lanes(values.shape, 3)], axis=1)
        for at in range(0, 2 * tokens, chunk):
            grad_probs = dot(left, right[:, at : at + chunk])
            ds_ref[:, at : at + chunk] = (
                p_ref[:, at : at + chunk].astype(f32) * grad_probs
            ).astype(bf16)
        grad_scores = ds_ref[...]
        turned_grad = dot(turned(keys), grad_scores)
        grad_query = (
            turned(
                jnp.concatenate([turned_grad[:half, :tokens], turned_grad[half:, tokens:]], axis=0)
            )
            * scale
        ).astype(bf16)
        grad_keys = dot(grad_scores, head_blocks(q_ref[...])).astype(bf16)
        grad_values = dot_rows(p_ref[...], scaled).astype(bf16)
        pieces = [grad_query]
        at = 0
        for part in parts:
            rows = part.shape[0]
            pieces += [grad_keys[at : at + rows], grad_values[at : at + rows]]
            at += rows

        def write(ref, values_, start):
            for value in values_:
                ref[start : start + value.shape[0], :] = value
                start += value.shape[0]

        @pl.when(pl.program_id(0) == 0)
        def _():
            write(send_ref, pieces, 0)

        @pl.when(pl.program_id(0) == 1)
        def _():
            write(keep_ref, pieces[:3], 0)
            write(send_ref, pieces[3:], 5 * tokens)

    local = lambda p, s: (1 - p) * (1 - s[0]) + p * s[0]
    offset = lambda p, s: (0, base + local(p, s))
    sources = [query, grad_mixed, far(mixed_t), far(weights), far(inverse)]
    in_specs = [
        pl.BlockSpec((tokens, LANES), offset),
        pl.BlockSpec((tokens, LANES), offset),
        pl.BlockSpec((LANES, tokens), lambda p, s: (local(p, s), 0)),
        pl.BlockSpec((None, span, 2 * tokens), lambda p, s: (local(p, s), 0, 0)),
        pl.BlockSpec((None, 1, 2 * tokens), lambda p, s: (local(p, s), 0, 0)),
    ]
    for part in parts:
        sources += [part, part]
        rows = part.shape[0]
        in_specs.append(pl.BlockSpec((rows, LANES), offset))
        in_specs.append(pl.BlockSpec((rows, LANES), lambda p, s: (0, pairs + base + local(p, s))))
    kept = tokens + 2 * parts[0].shape[0]
    sent = 7 * tokens if len(parts) == 2 else kept
    return pl.pallas_call(
        body,
        name="attend_back",
        cost_estimate=cost(5),
        out_shape=[shape(sent, LANES, bf16), shape(kept, LANES, bf16)],
        grid_spec=pltpu.PrefetchScalarGridSpec(
            num_scalar_prefetch=1,
            grid=(2,),
            in_specs=in_specs,
            out_specs=[
                pl.BlockSpec((sent, LANES), lambda p, s: (0, 0)),
                pl.BlockSpec((kept, LANES), lambda p, s: (0, 0)),
            ],
            scratch_shapes=[pltpu.VMEM((span, 2 * tokens), bf16)],
        ),
        compiler_params=pltpu.CompilerParams(
            vmem_limit_bytes=min(56 << 20, VMEM_BYTES * max(1, span // 1024))
        ),
    )(jnp.reshape(core, (1,)).astype(jnp.int32), *sources)


def normalize(resid):
    center = resid - jnp.mean(resid, axis=1, keepdims=True)
    inverse = lax.rsqrt(jnp.mean(center * center, axis=1, keepdims=True) + norm_eps)
    return center * inverse, inverse


def norm_back(grads, normal, inverse, gain):
    scaled = grads * gain
    return inverse * (
        scaled
        - jnp.mean(scaled, axis=1, keepdims=True)
        - normal * jnp.mean(scaled * normal, axis=1, keepdims=True)
    )


def column_sums(value):
    return jnp.sum(value, axis=0, keepdims=True)


def by_rows(tokens, body):
    rows = min(tokens, 128)

    def one(i, carry):
        body(aligned(i * rows, rows, 8), i * rows, rows)
        return carry

    lax.fori_loop(0, tokens // rows, one, 0)


def add_row(ref, row, value):
    ref[row : row + 1, :] += value


def spread_total(ref, row):
    lanes = ref[row : row + 1, :]
    ref[row : row + 1, :] = jnp.broadcast_to(jnp.sum(lanes, axis=1, keepdims=True), lanes.shape)


def masked_squares(value, valid):
    return column_sums(jnp.where(valid, value * value, 0.0))


def valid_rows(scalar, at, first, rows):
    position = scalar[at + 1] + first + lax.broadcasted_iota(jnp.int32, (rows, 1), 0)
    return position < scalar[at]


def after_attention(links, table, rows, mixed, vectors, gathered, out_piece):
    tokens, width = rows.shape
    extra = 4 * links.dp + 1
    count = len(mixed)
    part = width // count

    def body(scalar, rows_ref, vec_ref, *refs):
        mixed_refs = refs[:count]
        pieces = sides(refs[count:])
        hidden_ref, low_ref, low_t_ref, mixed_t_ref = refs[count + 4 : count + 8]
        normal_ref, inverse_ref, sums_ref, weight, sem = refs[count + 8 :]
        out_piece.fetch(scalar, pieces, weight, sem.at[0])
        out_piece.ready(weight, sem.at[0])
        for i, ref in enumerate(mixed_refs):
            product = dot(ref[...], weight[i * part : (i + 1) * part, :])
            hidden_ref[...] = product if i == 0 else hidden_ref[...] + product
        sums_ref[...] = jnp.zeros_like(sums_ref)

        def block(at, first, span):
            x = rows_ref[at, :].astype(f32)
            valid = valid_rows(scalar, extra, first, span)
            branch = hidden_ref[at, :] + vec_ref[2:3]
            add_row(sums_ref, 0, masked_squares(x, valid))
            add_row(sums_ref, 1, masked_squares(branch, valid))
            count = jnp.sum(valid.astype(f32), axis=0, keepdims=True)
            add_row(sums_ref, 2, jnp.broadcast_to(count, (1, width)))
            normal, inverse = normalize(x + branch)
            hidden = normal * vec_ref[3:4] + vec_ref[4:5]
            normal_ref[at, :] = normal
            inverse_ref[at, :] = inverse
            hidden_ref[at, :] = hidden
            low_ref[at, :] = hidden.astype(bf16)

        by_rows(tokens, block)
        spread_total(sums_ref, 0)
        spread_total(sums_ref, 1)
        low_t_ref[...] = turned(low_ref[...])
        for i, ref in enumerate(mixed_refs):
            mixed_t_ref[i * part : (i + 1) * part, :] = turned(ref[...])

    return call(
        body,
        "after_attention",
        [table, rows, vectors, *mixed, *flat(gathered)],
        [SMEM] + [VMEM] * (2 + count) + [ANY] * 4,
        [
            shape(tokens, width, f32),
            shape(tokens, width, bf16),
            shape(width, tokens, bf16),
            shape(width, tokens, bf16),
            shape(tokens, width, f32),
            shape(tokens, 1, f32),
            shape(3, width, f32),
        ],
        [out_piece.whole(), pltpu.SemaphoreType.DMA((1,))],
        time=3.5,
    )


def gelu_and_slope(u):
    phi = 0.5 * lax.erf(u * math.sqrt(0.5)) + 0.5
    bell = jnp.exp(-0.5 * (u * u)) * (1.0 / math.sqrt(2.0 * math.pi))
    return u * phi, phi + u * bell


def feed_up(links, table, low, up_bias, gathered, up_piece):
    tokens, width = low.shape
    inner = up_bias.shape[1]

    def body(scalar, low_ref, bias_ref, *refs):
        act_ref, act_t_ref, slope_ref, weight, sem = refs[4:]
        up_piece.fetch(scalar, sides(refs), weight, sem.at[0])
        up_piece.ready(weight, sem.at[0])

        def forward(j, carry):
            at = aligned(j * width, width, LANES)
            value, slope = gelu_and_slope(dot(low_ref[...], weight[:, at]) + bias_ref[:, at])
            value = value.astype(bf16)
            act_ref[:, at] = value
            act_t_ref[at, :] = turned(value)
            slope_ref[:, at] = slope.astype(bf16)
            return carry

        lax.fori_loop(0, inner // width, forward, 0)

    return call(
        body,
        "feed_up",
        [table, low, up_bias, *flat(gathered)],
        [SMEM] + [VMEM] * 2 + [ANY] * 4,
        [
            shape(tokens, inner, bf16),
            shape(inner, tokens, bf16),
            shape(tokens, inner, bf16),
        ],
        [up_piece.whole(), pltpu.SemaphoreType.DMA((1,))],
        time=8,
    )


def share(core, value, at, keep_ref, send_ref):
    span = value.shape[1] // 2
    low, high = value[:, :span], value[:, span:]
    even = core == 0
    keep_ref[at, :] = jnp.where(even, low, high)
    send_ref[at, :] = jnp.where(even, high, low)


def feed_down(links, table, act, hidden, vectors, cotangent, gathered, down_piece):
    tokens, width = hidden.shape
    inner = act.shape[1]
    extra = 4 * links.dp + 1
    dp = links.dp

    def body(scalar, act_ref, hidden_ref, vec_ref, cot_ref, *refs):
        out_ref, resid_ref, grad_ref, keep_ref, send_ref, sums_ref, weight, sem = refs[4:]
        down_piece.fetch(scalar, sides(refs), weight, sem.at[0])
        down_piece.ready(weight, sem.at[0])
        resid_ref[...] = dot(act_ref[...], weight[...])
        sums_ref[...] = jnp.zeros_like(sums_ref)

        def block(at, first, span):
            branch = resid_ref[at, :] + vec_ref[5:6]
            valid = valid_rows(scalar, extra, first, span)
            add_row(sums_ref, 3, masked_squares(branch, valid))
            normal, inverse = normalize(hidden_ref[at, :] + branch)
            out_ref[at, :] = (normal * vec_ref[6:7] + vec_ref[7:8]).astype(bf16)
            grads = cot_ref[at, :].astype(f32)
            add_row(sums_ref, 1, column_sums(grads * normal))
            add_row(sums_ref, 2, column_sums(grads))
            resid = norm_back(grads, normal, inverse, vec_ref[6:7])
            resid_ref[at, :] = resid
            grad_ffn = resid.astype(bf16)
            grad_ref[at, :] = grad_ffn
            add_row(sums_ref, 0, column_sums(grad_ffn.astype(f32)))
            share(scalar[4 * dp], grad_ffn, at, keep_ref, send_ref)

        by_rows(tokens, block)
        spread_total(sums_ref, 3)

    return call(
        body,
        "feed_down",
        [table, act, hidden, vectors, cotangent, *flat(gathered)],
        [SMEM] + [VMEM] * 4 + [ANY] * 4,
        [
            shape(tokens, width, bf16),
            shape(tokens, width, f32),
            shape(tokens, width, bf16),
            shape(tokens, width // 2, bf16),
            shape(tokens, width // 2, bf16),
            shape(4, width, f32),
        ],
        [down_piece.whole(), pltpu.SemaphoreType.DMA((1,))],
        time=6,
    )


def feed_back(links, table, side, slope, so_far, grad_ffn, up, down, pieces):
    tokens, width = so_far.shape
    up_piece, down_piece = pieces
    span = up_piece.columns
    block = width if span % width == 0 else span
    dp = links.dp

    def body(scalar, slope_ref, so_far_ref, grad_ref, um, ul, *refs):
        hidden_ref, out_ref, bias_ref, up_w, down_w, sems = refs[4:]
        core = scalar[4 * dp]
        half = core if side == 0 else 1 - core
        down_piece.fetch_rows(scalar, half, sides(refs), down_w, sems.at[1])
        up_piece.fetch_side(scalar, side, (um, ul), up_w, sems.at[0])
        hidden_ref[...] = so_far_ref[...]
        down_piece.ready(down_w, sems.at[1])
        up_piece.ready(up_w, sems.at[0])

        def backward(j, carry):
            here = aligned(j * block, block, LANES)
            at = aligned(half * span + j * block, block, LANES)
            grads = dot_rows(grad_ref[...], down_w[here, :]) * slope_ref[:, at].astype(f32)
            grads = grads.astype(bf16)
            bias_ref[:, here] = column_sums(grads.astype(f32))
            hidden_ref[...] += dot_rows(grads, up_w[:, here])
            out_ref[:, here] = grads
            return carry

        lax.fori_loop(0, span // block, backward, 0)

    return call(
        body,
        "feed_back",
        [table, slope, so_far, grad_ffn, *map(far, up[side]), *flat(down)],
        [SMEM] + [VMEM] * 3 + [ANY] * 6,
        [shape(tokens, width, f32), shape(tokens, span, bf16), shape(1, span, f32)],
        [
            pltpu.VMEM((width, span), bf16),
            pltpu.VMEM((span, width), bf16),
            pltpu.SemaphoreType.DMA((2,)),
        ],
        time=0.01,
    )


def before_attention(links, table, grad_hidden, normal, inverse, vectors, gathered, piece):
    tokens, width = normal.shape

    def body(scalar, grad_ref, normal_ref, inverse_ref, vec_ref, *refs):
        resid_ref, gm_ref, keep_ref, send_ref, sums_ref, weight, whole, sem = refs[4:]
        piece.fetch(scalar, sides(refs), weight, sem.at[0])
        sums_ref[...] = jnp.zeros_like(sums_ref)

        def block(at, first, span):
            grads = grad_ref[at, :]
            normal_ = normal_ref[at, :]
            add_row(sums_ref, 1, column_sums(grads * normal_))
            add_row(sums_ref, 2, column_sums(grads))
            resid = norm_back(grads, normal_, inverse_ref[at, :], vec_ref[3:4])
            resid_ref[at, :] = resid
            grad_attn = resid.astype(bf16)
            whole[at, :] = grad_attn
            add_row(sums_ref, 0, column_sums(grad_attn.astype(f32)))
            share(scalar[4 * links.dp], grad_attn, at, keep_ref, send_ref)

        by_rows(tokens, block)
        piece.ready(weight, sem.at[0])
        gm_ref[...] = dot_rows(whole[...], weight[...]).astype(bf16)

    return call(
        body,
        "before_attention",
        [table, grad_hidden, normal, inverse, vectors, *flat(gathered)],
        [SMEM] + [VMEM] * 4 + [ANY] * 4,
        [
            shape(tokens, width, f32),
            shape(tokens, width, bf16),
            shape(tokens, width // 2, bf16),
            shape(tokens, width // 2, bf16),
            shape(3, width, f32),
        ],
        [piece.whole(), pltpu.VMEM((tokens, width), bf16), pltpu.SemaphoreType.DMA((1,))],
        time=0.01,
    )


def weight_gradient(name, links, table, left, right, rows):
    outer, tokens = left[0].shape
    columns = right[0].shape[1]
    block = min(outer, 768)
    wide = min(columns, 512)

    def body(scalar, lm, lt, rm, rt, *refs):
        tile = refs[-1]

        def one(j, carry):
            at = aligned(j // (columns // wide) * block, block, 8)
            to = aligned(j % (columns // wide) * wide, wide, LANES)
            tile[at, to] = dot(lm[at, :], rm[:, to]) + dot(lt[at, :], rt[:, to])
            return carry

        lax.fori_loop(0, outer // block * (columns // wide), one, 0)
        place(scalar, links.dp, tile, refs[:3], rows, slice(None))

    return call(
        body,
        name,
        [table, *left, *right],
        [SMEM] + [VMEM] * 4,
        placed(links.dp, rows, columns),
        [pltpu.VMEM((outer, columns), f32)],
    )


class Shares:
    def __init__(self, refs, tokens):
        self.sent, self.kept, self.came = refs
        self.tokens = tokens

    def rows(self, ref, i):
        return ref[i * self.tokens : (i + 1) * self.tokens, :]

    def add(self, one, other):
        return (one.astype(f32) + other.astype(f32)).astype(bf16)

    def own(self):
        return [self.rows(self.kept, 0)] + [
            self.add(self.rows(self.kept, i), self.rows(self.came, 2 + i)) for i in (1, 2)
        ]

    def others(self):
        return [self.rows(self.came, 0)] + [
            self.add(self.rows(self.sent, 4 + i), self.rows(self.came, i)) for i in (1, 2)
        ]

    def partners(self):
        return [self.rows(self.sent, 0)] + [
            self.add(self.rows(self.sent, i), self.rows(self.came, 4 + i)) for i in (1, 2)
        ]


def attention_gradient(name, links, table, rows_t, groups, rows, out=None, vectors=None, folds=0, sums=()):
    width, tokens = rows_t[0].shape
    dp = links.dp
    wide = 3 * LANES
    half = width // 2
    total = wide * len(groups) + (half if out else 0) + (LANES if vectors is not None else 0)
    given = [value for group in groups for value in group]
    more = list(out or []) + ([*vectors, *sums] if vectors is not None else [])

    def body(scalar, xm, xt, *refs):
        group_refs = refs[: len(given)]
        more_refs = list(refs[len(given) : len(given) + len(more)])
        outs = refs[len(given) + len(more) :]
        sum_ref, tile = outs[3], outs[4]
        for g in range(len(groups)):
            shares = Shares(group_refs[3 * g : 3 * g + 3], tokens)
            mine = jnp.concatenate(shares.own(), axis=1)
            theirs = jnp.concatenate(shares.others(), axis=1)
            tile[:, g * wide : (g + 1) * wide] = dot(xm[...], mine) + dot(xt[...], theirs)
            sums_ = column_sums(mine.astype(f32)) + column_sums(theirs.astype(f32))
            sum_ref[g : g + 1, :] = sums_
        at = wide * len(groups)
        if out:
            mm, mt, gm, gt = more_refs[:4]
            tile[:, at : at + half] = dot(mm[...], gm[...]) + dot(mt[...], gt[...])
            at += half
        if vectors is not None:
            sums3, sums2, kept, sent, sums1, *sum_refs = more_refs
            even = scalar[4 * dp] == 0
            bias = jnp.concatenate(
                [
                    jnp.where(even, kept[...], sent[...]),
                    jnp.where(even, sent[...], kept[...]),
                ],
                axis=1,
            )
            biases = [
                jnp.concatenate(
                    [
                        bias[:, (i * folds + j) * rows : (i * folds + j + 1) * rows]
                        for i in range(dp)
                    ],
                    axis=1,
                )
                for j in range(folds)
            ]
            head = jnp.concatenate(
                [jnp.zeros((2, width), f32), sums3[...], sums2[0:3]]
                + biases
                + [sums1[...], sums2[3:4]],
                axis=0,
            )
            every = [ref[i : i + 1, :] for ref in sum_refs for i in range(ref.shape[0])]
            every += [sum_ref[g : g + 1, :] for g in range(len(groups))]
            lane = lax.broadcasted_iota(jnp.int32, (1, width), 1)
            owned = (lane // LANES) % 2 == scalar[4 * dp]
            lines = []
            for j in (0, 2):
                parts = [s[:, j * LANES : (j + 1) * LANES] for s in every for _ in range(2)]
                lines.append(jnp.where(owned, jnp.concatenate(parts, axis=1), 0.0))
            row = lax.broadcasted_iota(jnp.int32, (LANES, width), 0)
            padded = jnp.concatenate(
                [head, jnp.zeros((LANES - head.shape[0], width), f32)], axis=0
            )
            padded = jnp.where(row == 0, lines[0], jnp.where(row == 1, lines[1], padded))
            tile[:, at : at + LANES] = turned(padded)
        place(scalar, dp, tile, outs[:3], rows, slice(None))

    return call(
        body,
        name,
        [table, *rows_t, *given, *more],
        [SMEM] + [VMEM] * (2 + len(given) + len(more)),
        placed(dp, rows, total) + [shape(len(groups), wide, f32)],
        [pltpu.VMEM((width, total), f32)],
    )


def input_gradient(links, table, groups, resid, gathered, qkv_piece):
    tokens, width = resid.shape
    given = [value for group in groups for value in group]

    def body(scalar, resid_ref, *refs):
        group_refs = refs[: len(given)]
        out_ref, weight, grads, sem = refs[len(given) + 4 :]
        qkv_piece.fetch(scalar, sides(refs[len(given) :]), weight, sem.at[0])
        core = scalar[4 * links.dp]
        for g in range(len(groups)):
            shares = Shares(group_refs[3 * g : 3 * g + 3], tokens)
            for owner, values in ((core, shares.own()), (1 - core, shares.partners())):
                for j, value in enumerate(values):
                    at = j * width + (2 * g + owner) * LANES
                    grads[:, aligned(at, LANES, LANES)] = value
        qkv_piece.ready(weight, sem.at[0])
        out_ref[...] = resid_ref[...] + dot_rows(grads[...], weight[...])

    return call(
        body,
        "input_gradient",
        [table, resid, *given, *flat(gathered)],
        [SMEM] + [VMEM] * (1 + len(given)) + [ANY] * 4,
        [shape(tokens, width, f32)],
        [qkv_piece.whole(), pltpu.VMEM((tokens, 3 * width), bf16), pltpu.SemaphoreType.DMA((1,))],
        time=20,
    )[0]


def closing(links, table, early, late, folds, width):
    rows = early[0].shape[0]
    wide = 3 * LANES
    half = width // 2
    base = 8

    def body(scalar, em, et, lm, lt, *outs):
        qkv_ref, out_ref, *vec_refs, up_ref, rms_ref = outs

        def write(core):
            for owner, early_ref, late_ref in ((core, em, lm), (1 - core, et, lt)):
                groups = [(early_ref, 0), (early_ref, wide), (late_ref, 0)]
                for g, (ref, first) in enumerate(groups):
                    for j in range(3):
                        at = j * width + (2 * g + owner) * LANES
                        qkv_ref[:, at : at + LANES] = ref[
                            :, first + j * LANES : first + (j + 1) * LANES
                        ].astype(f32)
                out_ref[:, owner * half : (owner + 1) * half] = early_ref[
                    :, 2 * wide : 2 * wide + half
                ].astype(f32)

        for core in range(2):
            pl.when(scalar[4 * links.dp] == core)(lambda core=core: write(core))
        last = slice(wide, wide + LANES)
        vectors = turned(lm[:, last].astype(f32) + lt[:, last].astype(f32))
        for i, ref in enumerate(vec_refs):
            ref[...] = vectors[i : i + 1]
        for i in range(folds):
            up_ref[:, i * rows : (i + 1) * rows] = vectors[base + i : base + i + 1]
        at = base + folds
        count = vectors[at + 2 : at + 3] * width
        for i, line in enumerate((at, at + 1, at + 3)):
            value = jnp.sqrt(vectors[line : line + 1] / count + 1e-06)
            rms_ref[:, i : i + 1] = value[:, 0:1]

    return call(
        body,
        "closing",
        [table, *early, *late],
        [SMEM] + [VMEM] * 4,
        [shape(rows, 3 * width, f32), shape(rows, width, f32)]
        + [shape(1, rows, f32)] * base
        + [shape(1, folds * rows, f32), shape(1, 3, f32)],
    )


def settle(links, reduction):
    mine = reduction.finish()
    return mine, links.swap(mine)


def shards(
    tokens,
    lengths,
    qkv_weight,
    query_bias,
    value_bias,
    out_weight,
    out_bias,
    norm1_gain,
    norm1_shift,
    up_weight,
    up_bias,
    down_weight,
    down_bias,
    norm2_gain,
    norm2_shift,
    cotangent,
):
    seq_dev, ctx_tok, width = tokens.shape
    assert seq_dev == 1 and width // HEADS == LANES // 2
    scale = (width // HEADS) ** (-0.5)
    links = Links()
    dp = links.dp
    rows = tokens.reshape(ctx_tok, width)
    cot = cotangent.reshape(ctx_tok, width)
    block = lax.axis_index("ctx")
    start = block * ctx_tok
    table = links.table(lengths[0], start)

    shard = qkv_weight.shape[0]
    inner = down_weight.shape[0] * dp
    folds = down_weight.shape[0] // shard
    half = [w.shape[1] // 2 for w in (qkv_weight, out_weight, up_weight, down_weight)]
    qkv_piece = Piece(dp, shard, half[0], 0)
    vector_piece = Piece(dp, shard, LANES, half[0])
    up_piece = Piece(dp, shard, half[2], 0)
    out_piece = Piece(dp, shard, half[1], half[2])
    down_piece = Piece(dp, down_weight.shape[0], half[3], 0)
    ffn_pieces = (up_piece, down_piece)

    columns = [query_bias, value_bias, out_bias, norm1_gain, norm1_shift]
    columns += [down_bias, norm2_gain, norm2_shift]
    base = len(columns)
    columns += [up_bias[i * shard : (i + 1) * shard] for i in range(folds)]
    packed = jnp.stack(columns, axis=1)
    packed = jnp.pad(packed, ((0, 0), (0, LANES - packed.shape[1])))
    qkv_sent = jnp.concatenate([half_columns(links, qkv_weight), packed], axis=1)
    up_sent = jnp.concatenate(
        [half_columns(links, up_weight), half_columns(links, out_weight)], axis=1
    )
    down_sent = half_columns(links, down_weight)

    qkv_held = joined(links.cross(qkv_sent))
    up_held = links.cross(after(up_sent, qkv_held))
    down_sent = after(down_sent, up_held)
    qkv_held = links.first(qkv_held)
    qkv = links.second(after(qkv_held, up_held[1]), *up_held)
    up_held = after(joined(up_held), qkv[0][1])
    query, kv, vectors, up_bias_row, rows_t = project(
        links, table, after(rows, up_held), qkv, qkv_piece, vector_piece, scale, base, folds
    )
    early_steps = []

    def ready(more):
        early_steps.append(more)
        return after(more, query)

    down_held = links.cross_slowly(after(down_sent, up_held), ready)
    up_held = links.first(up_held, query)
    kv = after(kv, up_held, *early_steps)
    rows_t = [rows_t, links.swap(rows_t)]
    if links.ctx == 2:
        parts = [kv, links.swap(kv)]
        starts = [start, (1 - block) * ctx_tok]
    else:
        parts = [lax.all_gather(kv, "ctx", axis=0, tiled=True)]
        starts = [jnp.int32(0)]
    groups = 3
    count = width // LANES // groups
    forward = []
    waits = [(), (), ()]
    for i in range(groups):
        given = after(query, *waits[i], *(forward[-1][1:2] if forward else ()))
        forward.append(attend(given, parts, starts, lengths[0], i * count, count))
        if i == 0:
            down_held = joined(down_held, forward[0][1])
            waits[1] = (down_held,)
    up = links.second(up_held, forward[1][1])
    down_held = links.first(after(down_held, forward[1][1]), forward[2][1])
    mixed = [f[1] for f in forward]
    hidden, low, low_t, mixed_t, normal, deviation, sums1 = after_attention(
        links, table, after(rows, down_held), mixed, vectors, up, out_piece
    )
    low_t = [low_t, links.swap(low_t)]
    mixed_t = [mixed_t, links.swap(mixed_t)]
    act, act_t, slope = feed_up(links, table, low, up_bias_row, up, up_piece)
    down = links.second(after(down_held, forward[2][1]), act)
    act_t = [act_t, links.swap(after(act_t, down[1][1]))]
    output, resid2, grad_ffn, ffn_keep, ffn_send, sums2 = feed_down(
        links, table, act, hidden, vectors, cot, down, down_piece
    )
    ffn_came = links.swap(ffn_send)
    down_sum = Sum(
        links,
        weight_gradient(
            "down_gradient", links, table, act_t, [ffn_keep, ffn_came], down_piece.rows
        ),
    )
    given = after(resid2, down_sum.prepare())
    down_sum.send()
    grad_hidden, upper_send, bias_sent = feed_back(
        links, table, 1, slope, given, grad_ffn, up, down, ffn_pieces
    )
    upper_came = links.swap(upper_send)
    grad_hidden, upper_keep, bias_kept = feed_back(
        links, table, 0, slope, grad_hidden, grad_ffn, up, down, ffn_pieces
    )
    up_sum = Sum(
        links,
        weight_gradient(
            "up_gradient", links, table, low_t, [upper_keep, upper_came], up_piece.rows
        ),
    )
    down_sum.hold(grad_hidden)
    given = after(grad_hidden, up_sum.prepare(), down_sum.prepare())
    up_sum.send()
    down_sum.send()
    resid1, grad_mixed, attn_keep, attn_send, sums3 = before_attention(
        links, table, given, normal, deviation, vectors, up, out_piece
    )
    out_parts = [*mixed_t, attn_keep, links.swap(attn_send)]

    def back_through(i, given):
        turned_mixed, _, weights, inverse = forward[i]
        sent, kept = attend_back(
            given,
            parts,
            grad_mixed,
            turned_mixed,
            weights,
            inverse,
            scale,
            i * count,
            links.core,
        )
        if links.ctx == 2:
            return [sent, kept, links.swap(sent)]
        whole = []
        for value in (sent, kept):
            keys, values = jnp.split(value[ctx_tok:], 2, axis=0)
            both = lax.psum_scatter(
                jnp.concatenate([keys, values], axis=1), "ctx", scatter_dimension=0, tiled=True
            )
            whole.append([value[:ctx_tok], both[:, :LANES], both[:, LANES:]])
        blank = jnp.zeros((4 * ctx_tok, LANES), bf16)
        sent = jnp.concatenate(whole[0] + [blank], axis=0)
        return [sent, jnp.concatenate(whole[1], axis=0), links.swap(sent)]

    given = after(query, grad_mixed)
    back = [back_through(0, given)]
    back.append(back_through(1, after(query, back[0][1])))
    down_sum.hold(back[1][1])
    up_sum.hold(back[1][1])
    given = after(rows_t[0], down_sum.prepare(), up_sum.prepare())
    down_sum.send()
    up_sum.send()
    *early, early_sums = attention_gradient(
        "early_gradient", links, table, [given, rows_t[1]], back[:2], shard, out=out_parts
    )
    early_sum = Sum(links, early)
    down_sum.hold(early[2])
    up_sum.hold(early[2])
    given = after(query, early_sum.prepare(), down_sum.prepare(), up_sum.prepare())
    early_sum.send()
    down_sum.send()
    up_sum.send()
    back.append(back_through(2, given))
    up_sum.hold(back[2][1])
    early_sum.hold(back[2][1])
    down_sum.hold(back[2][1])
    up_sum.hold(back[2][1])
    given = after(rows_t[0], early_sum.prepare(), up_sum.prepare())
    early_sum.send()
    up_sum.send()
    *late, _ = attention_gradient(
        "late_gradient",
        links,
        table,
        [given, rows_t[1]],
        back[2:],
        shard,
        vectors=[sums3, sums2, bias_kept, bias_sent, sums1],
        folds=folds,
        sums=[early_sums],
    )
    late_sum = Sum(links, late)
    down_sum.hold(late[2])
    down_mine = down_sum.finish()
    given = after(resid1, late_sum.prepare(), down_mine)
    late_sum.send()
    input_grad = input_gradient(links, table, back, given, qkv, qkv_piece)
    late_sum.hold(input_grad)
    early_sum.hold(input_grad)
    up_sum.hold(input_grad)
    up_mine = up_sum.finish()
    down_grad = both_halves(links, down_mine, links.swap(down_mine))
    up_grad = both_halves(links, up_mine, links.swap(up_mine))
    early = settle(links, early_sum)
    late = settle(links, late_sum)
    qkv_grad, out_grad, *sums, up_bias_grad, stream_rms = closing(
        links, table, early, late, folds, width
    )
    sums = [value.reshape(shard) for value in sums]
    return (
        output.reshape(seq_dev, ctx_tok, width),
        input_grad.reshape(seq_dev, ctx_tok, width),
        stream_rms.reshape(3),
        qkv_grad,
        sums[0],
        sums[1],
        out_grad,
        sums[2],
        sums[3],
        sums[4],
        up_grad,
        up_bias_grad.reshape(-1),
        down_grad,
        sums[5],
        sums[6],
        sums[7],
    )


def solution(mesh):
    in_specs = (
        P("dp", "ctx", None),
        P("dp"),
        P("dp", None),
        P("dp"),
        P("dp"),
        P("dp", None),
        P("dp"),
        P("dp"),
        P("dp"),
        P("dp", None),
        P("dp"),
        P("dp", None),
        P("dp"),
        P("dp"),
        P("dp"),
        P("dp", "ctx", None),
    )
    out_specs = (
        P("dp", "ctx", None),
        P("dp", "ctx", None),
        P(),
        P("dp", None),
        P("dp"),
        P("dp"),
        P("dp", None),
        P("dp"),
        P("dp"),
        P("dp"),
        P("dp", None),
        P("dp"),
        P("dp", None),
        P("dp"),
        P("dp"),
        P("dp"),
    )
    return jax.shard_map(shards, mesh=mesh, in_specs=in_specs, out_specs=out_specs, check_vma=False)
```

```python
import math

import jax
import jax.numpy as jnp
from jax import lax
from jax.experimental import pallas as pl
from jax.experimental.pallas import tpu as pltpu
from jax.sharding import PartitionSpec as P

HEADS = 12
LANES = 128
VECTORS = 16
VMEM_BYTES = 24 << 20
FLOPS = 250_000_000
BYTES = 750_000

masked_score = -1e30
norm_eps = 1e-05
f32 = jnp.float32
bf16 = jnp.bfloat16


def low_precision(value):
    return lax.reduce_precision(value, exponent_bits=8, mantissa_bits=7)


class Links:
    def __init__(self):
        self.dp = lax.axis_size("dp")
        self.ctx = lax.axis_size("ctx")
        self.bits = self.dp.bit_length() - 1
        assert self.dp == 1 << self.bits and self.bits >= 2 and self.ctx % 2 == 0
        self.core = lax.axis_index("ctx") % 2
        self.me = lax.axis_index("dp")
        self.upper = []
        bit = self.bits - 1
        while bit >= 2:
            size = 2 if (bit - 1) % 2 == 0 else 1
            self.upper.append(tuple(range(bit, bit - size, -1)))
            bit -= size

    def swap(self, value):
        return lax.ppermute(value, "ctx", [(i, i ^ 1) for i in range(self.ctx)])

    def hop(self, value, mask_even, mask_odd):
        pairs = []
        for block in range(self.ctx):
            mask = mask_odd if block % 2 else mask_even
            pairs += [(block * self.dp + i, block * self.dp + (i ^ mask)) for i in range(self.dp)]
        return lax.ppermute(value, ("ctx", "dp"), pairs)

    def places(self, core):
        position = lax.iota(jnp.int32, self.dp)
        quarter = self.dp // 4
        first = (position // quarter) % 2
        second = position // (2 * quarter)
        mask = first * (1 + core) + second * (2 - core)
        for i in range(self.bits - 2):
            mask = mask + ((position >> i) % 2) * (1 << (self.bits - 1 - i))
        return jnp.bitwise_xor(self.me, mask)

    def spots(self, core):
        mask = jnp.bitwise_xor(self.me, lax.iota(jnp.int32, self.dp))
        low, high = mask % 2, (mask // 2) % 2
        first = jnp.where(core == 0, low, high)
        second = jnp.where(core == 0, high, low)
        quarter = self.dp // 4
        spot = first * quarter + second * (2 * quarter)
        for i in range(self.bits - 2):
            spot = spot + ((mask >> (self.bits - 1 - i)) % 2) * (1 << i)
        return spot

    def table(self, *more):
        parts = [self.places(self.core), self.places(1 - self.core)]
        parts += [self.spots(self.core), self.spots(1 - self.core)]
        parts += [jnp.reshape(value, (1,)) for value in (self.core,) + more]
        return jnp.concatenate(parts).astype(jnp.int32)

    def masks(self, bits):
        return [
            sum(((i >> j) & 1) << bit for j, bit in enumerate(bits)) for i in range(1 << len(bits))
        ]

    def cross(self, piece):
        held = [piece]
        for bits in self.upper:
            here = jnp.concatenate(held, axis=0) if len(held) > 1 else held[0]
            held = [here] + [self.hop(here, mask, mask) for mask in self.masks(bits)[1:]]
        return held

    def cross_slowly(self, piece, ready):
        held = piece
        masks = [1 << bit for bits in self.upper for bit in bits]
        for i, mask in enumerate(masks):
            more = self.hop(held, mask, mask)
            if i < len(masks) - 1:
                more = ready(more)
            held = [held, more]
            if i < len(masks) - 1:
                held = jnp.concatenate(held, axis=0)
        return held

    def first(self, held, *waits):
        more = self.hop(held, 1, 2)
        return jnp.concatenate([held, after(more, *waits) if waits else more], axis=0)

    def second(self, held, *waits):
        early = self.swap(held)
        more = self.hop(held, 2, 1)
        if waits:
            early, more = after((early, more), *waits)
        return [held, more], [early, self.swap(more)]


def joined(held, *waits):
    return jnp.concatenate(after(tuple(held), *waits) if waits else held, axis=0)


class Sum:
    def __init__(self, links, kept, direct=False):
        self.links = links
        self.kept = kept
        self.quarter = kept[0].shape[0]
        self.rows = 4 * self.quarter
        self.terms = []
        self.steps = [[(2, 1)], [(1, 2)]]
        for bits in reversed(links.upper):
            if direct:
                self.steps.append([(mask, mask) for mask in links.masks(bits)[1:]])
            else:
                self.steps += [[(1 << bit, 1 << bit)] for bit in reversed(bits)]
        self.ready = None

    def total(self, start, span):
        index = min(2, start // self.quarter)
        first = start - index * self.quarter
        value = self.kept[index]
        if span != value.shape[0]:
            value = lax.slice_in_dim(value, first, first + span, axis=0)
        if not self.terms:
            return value
        value = value.astype(f32)
        for term in self.terms:
            parts = [
                lax.slice_in_dim(part, start, start + span, axis=0).astype(f32) for part in term
            ]
            if len(parts) == 1:
                value = low_precision(value + parts[0])
            else:
                value = low_precision((value + parts[0]) + (parts[1] + parts[2]))
        return value.astype(bf16)

    def prepare(self):
        masks = self.steps[0]
        self.rows //= len(masks) + 1
        self.ready = [self.total((i + 1) * self.rows, self.rows) for i in range(len(masks))]
        return self.ready

    def send(self):
        if self.ready is None:
            self.prepare()
        masks = self.steps.pop(0)
        self.terms.append(
            tuple(self.links.hop(value, *mask) for value, mask in zip(self.ready, masks))
        )
        self.ready = None

    def hold(self, other):
        self.terms[-1] = tuple(after(value, other) for value in self.terms[-1])

    def finish(self):
        while self.steps:
            self.send()
        mine = self.total(0, self.rows)
        step = 2
        while step < self.links.ctx:
            pairs = [(i, i ^ step) for i in range(self.links.ctx)]
            other = lax.ppermute(mine, "ctx", pairs)
            mine = low_precision(mine.astype(f32) + other.astype(f32)).astype(bf16)
            step *= 2
        return mine


def after(value, *others):
    return lax.optimization_barrier((value, others))[0]


def half_columns(links, value):
    span = value.shape[1] // 2
    return lax.dynamic_slice_in_dim(value, links.core * span, span, 1)


def both_halves(links, mine, theirs):
    even = links.core == 0
    return jnp.concatenate(
        [jnp.where(even, mine, theirs), jnp.where(even, theirs, mine)], axis=1
    ).astype(f32)


def dot(left, right):
    return jnp.dot(left, right, preferred_element_type=f32)


def dot_rows(left, right):
    return lax.dot_general(left, right, (((1,), (1,)), ((), ())), preferred_element_type=f32)


def turned(value):
    return jnp.transpose(value)


def aligned(start, size, unit):
    return pl.ds(pl.multiple_of(start, unit), size)


SMEM = pl.BlockSpec(memory_space=pltpu.SMEM)
ANY = pl.BlockSpec(memory_space=pl.ANY)
VMEM = pl.BlockSpec(memory_space=pltpu.VMEM)


def cost(microseconds):
    return pl.CostEstimate(
        flops=int(microseconds * FLOPS), transcendentals=0, bytes_accessed=int(microseconds * BYTES)
    )


def call(body, name, sources, in_specs, outs, scratch=(), time=5):
    return pl.pallas_call(
        body,
        name=name,
        out_shape=outs,
        in_specs=in_specs,
        out_specs=[VMEM] * len(outs),
        scratch_shapes=list(scratch),
        compiler_params=pltpu.CompilerParams(vmem_limit_bytes=VMEM_BYTES),
        cost_estimate=cost(time),
    )(*sources)


def shape(rows, columns, dtype):
    return jax.ShapeDtypeStruct((rows, columns), dtype)


class Piece:
    def __init__(self, dp, rows, columns, first):
        self.dp, self.rows, self.columns, self.first = dp, rows, columns, first

    def fetch(self, scalar, sides, whole, sem):
        core = scalar[4 * self.dp]
        for side, sources in enumerate(sides):
            half = core if side == 0 else 1 - core
            count = self.dp // len(sources)
            for i, source in enumerate(sources):

                def one(position, carry, side=side, source=source, half=half, base=i * count):
                    owner = scalar[side * self.dp + base + position]
                    pltpu.make_async_copy(
                        source.at[
                            aligned(position * self.rows, self.rows, 8),
                            pl.ds(self.first, self.columns),
                        ],
                        whole.at[
                            aligned(owner * self.rows, self.rows, 8),
                            aligned(half * self.columns, self.columns, LANES),
                        ],
                        sem,
                    ).start()
                    return carry

                lax.fori_loop(0, count, one, 0)

    def fetch_side(self, scalar, side, sources, whole, sem):
        count = self.dp // len(sources)
        for i, source in enumerate(sources):

            def one(position, carry, source=source, base=i * count):
                owner = scalar[side * self.dp + base + position]
                pltpu.make_async_copy(
                    source.at[
                        aligned(position * self.rows, self.rows, 8),
                        pl.ds(self.first, self.columns),
                    ],
                    whole.at[aligned(owner * self.rows, self.rows, 8), :],
                    sem,
                ).start()
                return carry

            lax.fori_loop(0, count, one, 0)

    def fetch_rows(self, scalar, part, sides, whole, sem):
        core = scalar[4 * self.dp]
        for side, sources in enumerate(sides):
            half = core if side == 0 else 1 - core
            count = self.dp // len(sources)

            def one(i, carry, side=side, sources=sources, half=half, count=count):
                spot = scalar[(2 + side) * self.dp + part * (self.dp // 2) + i]
                for j, source in enumerate(sources):

                    @pl.when(spot // count == j)
                    def _(source=source, j=j):
                        pltpu.make_async_copy(
                            source.at[
                                aligned((spot - j * count) * self.rows, self.rows, 8),
                                pl.ds(self.first, self.columns),
                            ],
                            whole.at[
                                aligned(i * self.rows, self.rows, 8),
                                aligned(half * self.columns, self.columns, LANES),
                            ],
                            sem,
                        ).start()

                return carry

            lax.fori_loop(0, self.dp // 2, one, 0)

    def ready(self, whole, sem):
        pltpu.make_async_copy(whole, whole, sem).wait()

    def whole(self):
        return pltpu.VMEM((self.dp * self.rows, 2 * self.columns), bf16)


def place(scalar, dp, tile, outs, rows, columns):
    base = 0
    for out in outs:
        count = out.shape[0] // rows

        def one(i, carry, out=out, base=base):
            owner = scalar[base + i]
            out[aligned(i * rows, rows, 8), columns] = tile[aligned(owner * rows, rows, 8), :].astype(
                bf16
            )
            return carry

        lax.fori_loop(0, count, one, 0)
        base += count


def placed(dp, rows, columns):
    return [
        shape(rows * dp // 4, columns, bf16),
        shape(rows * dp // 4, columns, bf16),
        shape(rows * dp // 2, columns, bf16),
    ]


def in_hbm(*dims):
    *dims, dtype = dims
    return pltpu.HBM(tuple(dims), dtype)


def sides(refs):
    return (refs[:2], refs[2:4])


def far(value):
    return pltpu.with_memory_space_constraint(value, pltpu.HBM)


def flat(gathered):
    return [far(value) for value in (*gathered[0], *gathered[1])]


def project(links, table, rows, gathered, qkv_piece, vector_piece, scale, base, folds):
    tokens, width = rows.shape
    shard = width // links.dp

    def body(scalar, rows_ref, *refs):
        q_ref, kv_ref, vec_ref, bias_ref, rows_t_ref, weight, vecs, sems = refs[4:]
        pieces = sides(refs)
        vector_piece.fetch_side(scalar, 0, pieces[0], vecs, sems.at[1])
        qkv_piece.fetch(scalar, pieces, weight, sems.at[0])
        vector_piece.ready(vecs, sems.at[1])
        vectors = turned(vecs[...].astype(f32))[:VECTORS]
        vec_ref[...] = vectors
        bias_ref[...] = jnp.concatenate(
            [
                vectors[base + j : base + j + 1, i * shard : (i + 1) * shard]
                for i in range(links.dp)
                for j in range(folds)
            ],
            axis=1,
        )
        rows_t_ref[...] = turned(rows_ref[...])
        qkv_piece.ready(weight, sems.at[0])
        x = rows_ref[...]
        query = (dot(x, weight[:, :width]) + vectors[0:1]).astype(bf16)
        q_ref[...] = (query.astype(f32) * scale).astype(bf16)
        kv_ref[:, :width] = dot(x, weight[:, width : 2 * width]).astype(bf16)
        kv_ref[:, width:] = (dot(x, weight[:, 2 * width :]) + vectors[1:2]).astype(bf16)

    return call(
        body,
        "qkv",
        [table, rows, *flat(gathered)],
        [SMEM, VMEM] + [ANY] * 4,
        [
            shape(tokens, width, bf16),
            shape(tokens, 2 * width, bf16),
            shape(VECTORS, width, f32),
            shape(1, folds * width, f32),
            in_hbm(width, tokens, bf16),
        ],
        [qkv_piece.whole(), pltpu.VMEM((width, LANES), bf16), pltpu.SemaphoreType.DMA((2,))],
        time=5,
    )


def pair_specs(parts, pairs, base):
    specs = []
    for part in parts:
        rows = part.shape[0]
        specs.append(pl.BlockSpec((rows, LANES), lambda p, s: (0, base + p)))
        specs.append(pl.BlockSpec((rows, LANES), lambda p, s: (0, pairs + base + p)))
    return specs


def first_lanes(shape_, count):
    return (lax.broadcasted_iota(jnp.int32, shape_, 1) < count).astype(f32).astype(bf16)


def head_blocks(query):
    lane = lax.broadcasted_iota(jnp.int32, query.shape, 1)
    zero = jnp.zeros_like(query)
    half = LANES // 2
    return jnp.concatenate(
        [jnp.where(lane < half, query, zero), jnp.where(lane >= half, query, zero)], axis=0
    )


def attend(query, parts, starts, length, base, count):
    tokens, width = query.shape
    pairs = width // LANES
    span = sum(part.shape[0] for part in parts)
    half = LANES // 2
    chunk = min(256, tokens)
    scalars = jnp.concatenate(
        [jnp.reshape(v, (1,)).astype(jnp.int32) for v in [length, *starts]]
    )

    def body(scalar, q_ref, *refs):
        kv_refs = refs[: 2 * len(parts)]
        mixed_t_ref, mixed_ref, p_ref, inverse_ref, bias = refs[2 * len(parts) :]

        @pl.when(pl.program_id(0) == 0)
        def _():
            at = 0
            for i, part in enumerate(parts):
                rows = part.shape[0]
                position = scalar[1 + i] + lax.broadcasted_iota(jnp.int32, (rows, LANES), 0)
                lane = lax.broadcasted_iota(jnp.int32, (rows, LANES), 1)
                hidden = jnp.where(position < scalar[0], 0.0, masked_score)
                bias[at : at + rows, :] = jnp.where(lane == 0, hidden, 0.0).astype(bf16)
                at += rows

        keys = jnp.concatenate([ref[...] for ref in kv_refs[0::2]], axis=0)
        values = jnp.concatenate([ref[...] for ref in kv_refs[1::2]], axis=0)
        keys = jnp.concatenate([keys, bias[...]], axis=1)
        values_t = jnp.concatenate([turned(values), jnp.ones((16, span), bf16)], axis=0)
        queries = head_blocks(q_ref[...])
        queries = jnp.concatenate([queries, first_lanes(queries.shape, 1)], axis=1)
        for at in range(0, 2 * tokens, chunk):
            scores = dot_rows(keys, queries[at : at + chunk])
            peak = jnp.max(scores, axis=0, keepdims=True)
            weights = jnp.exp(scores - peak).astype(bf16)
            p_ref[:, at : at + chunk] = weights
        sums = dot(values_t, p_ref[...])
        inverse = 1.0 / sums[LANES : LANES + 1]
        inverse_ref[...] = inverse
        mixed_t_ref[:half, :] = sums[:half, :tokens] * inverse[:, :tokens]
        mixed_t_ref[half:, :] = sums[half:LANES, tokens:] * inverse[:, tokens:]
        mixed_ref[...] = turned(mixed_t_ref[...]).astype(bf16)

    sources = [query]
    for part in parts:
        sources += [part, part]
    return pl.pallas_call(
        body,
        name="attend",
        cost_estimate=cost(8),
        out_shape=[
            in_hbm(count * LANES, tokens, f32),
            shape(tokens, count * LANES, bf16),
            in_hbm(count, span, 2 * tokens, bf16),
            in_hbm(count, 1, 2 * tokens, f32),
        ],
        grid_spec=pltpu.PrefetchScalarGridSpec(
            num_scalar_prefetch=1,
            grid=(count,),
            in_specs=[pl.BlockSpec((tokens, LANES), lambda p, s: (0, base + p))]
            + pair_specs(parts, pairs, base),
            out_specs=[
                pl.BlockSpec((LANES, tokens), lambda p, s: (p, 0)),
                pl.BlockSpec((tokens, LANES), lambda p, s: (0, p)),
                pl.BlockSpec((None, span, 2 * tokens), lambda p, s: (p, 0, 0)),
                pl.BlockSpec((None, 1, 2 * tokens), lambda p, s: (p, 0, 0)),
            ],
            scratch_shapes=[pltpu.VMEM((span, LANES), bf16)],
        ),
        compiler_params=pltpu.CompilerParams(vmem_limit_bytes=min(56 << 20, VMEM_BYTES * max(1, span // 1024))),
    )(scalars, *sources)


def attend_back(query, parts, grad_mixed, mixed_t, weights, inverse, scale, base, core):
    tokens, width = query.shape
    pairs = width // LANES
    span = sum(part.shape[0] for part in parts)
    half = LANES // 2
    chunk = min(256, tokens)

    def body(_, q_ref, gm_ref, mt_ref, p_ref, inv_ref, *refs):
        kv_refs = refs[: 2 * len(parts)]
        send_ref, keep_ref, ds_ref = refs[2 * len(parts) :]
        keys = jnp.concatenate([ref[...] for ref in kv_refs[0::2]], axis=0)
        values = jnp.concatenate([ref[...] for ref in kv_refs[1::2]], axis=0)
        grads = turned(gm_ref[...].astype(f32))
        inv = inv_ref[...]
        product = grads * mt_ref[...]
        empty = jnp.zeros((half, tokens), bf16)
        even, odd = inv[:, :tokens], inv[:, tokens:]
        delta = jnp.concatenate(
            [
                jnp.sum(product[:half], axis=0, keepdims=True) * even,
                jnp.sum(product[half:], axis=0, keepdims=True) * odd,
            ],
            axis=1,
        )
        top = jnp.concatenate([(grads[:half] * even).astype(bf16), empty], axis=1)
        bottom = jnp.concatenate([empty, (grads[half:] * odd).astype(bf16)], axis=1)
        scaled = jnp.concatenate([top, bottom], axis=0)
        first = (-delta).astype(bf16).astype(f32)
        second = (-delta - first).astype(bf16).astype(f32)
        third = (-delta - first - second).astype(bf16).astype(f32)
        row = lax.broadcasted_iota(jnp.int32, (LANES, 2 * tokens), 0)
        limbs = jnp.where(
            row == 0, first, jnp.where(row == 1, second, jnp.where(row == 2, third, 0.0))
        ).astype(bf16)
        right = jnp.concatenate([scaled, limbs], axis=0)
        left = jnp.concatenate([values, first_lanes(values.shape, 3)], axis=1)
        for at in range(0, 2 * tokens, chunk):
            grad_probs = dot(left, right[:, at : at + chunk])
            ds_ref[:, at : at + chunk] = (
                p_ref[:, at : at + chunk].astype(f32) * grad_probs
            ).astype(bf16)
        grad_scores = ds_ref[...]
        turned_grad = dot(turned(keys), grad_scores)
        grad_query = (
            turned(
                jnp.concatenate([turned_grad[:half, :tokens], turned_grad[half:, tokens:]], axis=0)
            )
            * scale
        ).astype(bf16)
        grad_keys = dot(grad_scores, head_blocks(q_ref[...])).astype(bf16)
        grad_values = dot_rows(p_ref[...], scaled).astype(bf16)
        pieces = [grad_query]
        at = 0
        for part in parts:
            rows = part.shape[0]
            pieces += [grad_keys[at : at + rows], grad_values[at : at + rows]]
            at += rows

        def write(ref, values_, start):
            for value in values_:
                ref[start : start + value.shape[0], :] = value
                start += value.shape[0]

        @pl.when(pl.program_id(0) == 0)
        def _():
            write(send_ref, pieces, 0)

        @pl.when(pl.program_id(0) == 1)
        def _():
            write(keep_ref, pieces[:3], 0)
            write(send_ref, pieces[3:], 5 * tokens)

    local = lambda p, s: (1 - p) * (1 - s[0]) + p * s[0]
    offset = lambda p, s: (0, base + local(p, s))
    sources = [query, grad_mixed, far(mixed_t), far(weights), far(inverse)]
    in_specs = [
        pl.BlockSpec((tokens, LANES), offset),
        pl.BlockSpec((tokens, LANES), offset),
        pl.BlockSpec((LANES, tokens), lambda p, s: (local(p, s), 0)),
        pl.BlockSpec((None, span, 2 * tokens), lambda p, s: (local(p, s), 0, 0)),
        pl.BlockSpec((None, 1, 2 * tokens), lambda p, s: (local(p, s), 0, 0)),
    ]
    for part in parts:
        sources += [part, part]
        rows = part.shape[0]
        in_specs.append(pl.BlockSpec((rows, LANES), offset))
        in_specs.append(pl.BlockSpec((rows, LANES), lambda p, s: (0, pairs + base + local(p, s))))
    kept = tokens + 2 * parts[0].shape[0]
    sent = 7 * tokens if len(parts) == 2 else kept
    return pl.pallas_call(
        body,
        name="attend_back",
        cost_estimate=cost(2),
        out_shape=[shape(sent, LANES, bf16), shape(kept, LANES, bf16)],
        grid_spec=pltpu.PrefetchScalarGridSpec(
            num_scalar_prefetch=1,
            grid=(2,),
            in_specs=in_specs,
            out_specs=[
                pl.BlockSpec((sent, LANES), lambda p, s: (0, 0)),
                pl.BlockSpec((kept, LANES), lambda p, s: (0, 0)),
            ],
            scratch_shapes=[pltpu.VMEM((span, 2 * tokens), bf16)],
        ),
        compiler_params=pltpu.CompilerParams(
            vmem_limit_bytes=min(56 << 20, VMEM_BYTES * max(1, span // 1024))
        ),
    )(jnp.reshape(core, (1,)).astype(jnp.int32), *sources)


def normalize(resid):
    center = resid - jnp.mean(resid, axis=1, keepdims=True)
    inverse = lax.rsqrt(jnp.mean(center * center, axis=1, keepdims=True) + norm_eps)
    return center * inverse, inverse


def norm_back(grads, normal, inverse, gain):
    scaled = grads * gain
    return inverse * (
        scaled
        - jnp.mean(scaled, axis=1, keepdims=True)
        - normal * jnp.mean(scaled * normal, axis=1, keepdims=True)
    )


def column_sums(value):
    return jnp.sum(value, axis=0, keepdims=True)


def by_rows(tokens, body):
    rows = min(tokens, 128)

    def one(i, carry):
        body(aligned(i * rows, rows, 8), i * rows, rows)
        return carry

    lax.fori_loop(0, tokens // rows, one, 0)


def add_row(ref, row, value):
    ref[row : row + 1, :] += value


def spread_total(ref, row):
    lanes = ref[row : row + 1, :]
    ref[row : row + 1, :] = jnp.broadcast_to(jnp.sum(lanes, axis=1, keepdims=True), lanes.shape)


def masked_squares(value, valid):
    return column_sums(jnp.where(valid, value * value, 0.0))


def valid_rows(scalar, at, first, rows):
    position = scalar[at + 1] + first + lax.broadcasted_iota(jnp.int32, (rows, 1), 0)
    return position < scalar[at]


def after_attention(links, table, rows, mixed, vectors, gathered, out_piece):
    tokens, width = rows.shape
    extra = 4 * links.dp + 1
    count = len(mixed)
    part = width // count

    def body(scalar, rows_ref, vec_ref, *refs):
        mixed_refs = refs[:count]
        pieces = sides(refs[count:])
        hidden_ref, low_ref, low_t_ref, mixed_t_ref = refs[count + 4 : count + 8]
        normal_ref, inverse_ref, sums_ref, weight, sem = refs[count + 8 :]
        out_piece.fetch(scalar, pieces, weight, sem.at[0])
        out_piece.ready(weight, sem.at[0])
        for i, ref in enumerate(mixed_refs):
            product = dot(ref[...], weight[i * part : (i + 1) * part, :])
            hidden_ref[...] = product if i == 0 else hidden_ref[...] + product
        sums_ref[...] = jnp.zeros_like(sums_ref)

        def block(at, first, span):
            x = rows_ref[at, :].astype(f32)
            valid = valid_rows(scalar, extra, first, span)
            branch = hidden_ref[at, :] + vec_ref[2:3]
            add_row(sums_ref, 0, masked_squares(x, valid))
            add_row(sums_ref, 1, masked_squares(branch, valid))
            count = jnp.sum(valid.astype(f32), axis=0, keepdims=True)
            add_row(sums_ref, 2, jnp.broadcast_to(count, (1, width)))
            normal, inverse = normalize(x + branch)
            hidden = normal * vec_ref[3:4] + vec_ref[4:5]
            normal_ref[at, :] = normal
            inverse_ref[at, :] = inverse
            hidden_ref[at, :] = hidden
            low_ref[at, :] = hidden.astype(bf16)

        by_rows(tokens, block)
        spread_total(sums_ref, 0)
        spread_total(sums_ref, 1)
        low_t_ref[...] = turned(low_ref[...])
        for i, ref in enumerate(mixed_refs):
            mixed_t_ref[i * part : (i + 1) * part, :] = turned(ref[...])

    return call(
        body,
        "after_attention",
        [table, rows, vectors, *mixed, *flat(gathered)],
        [SMEM] + [VMEM] * (2 + count) + [ANY] * 4,
        [
            shape(tokens, width, f32),
            shape(tokens, width, bf16),
            shape(width, tokens, bf16),
            shape(width, tokens, bf16),
            shape(tokens, width, f32),
            shape(tokens, 1, f32),
            shape(3, width, f32),
        ],
        [out_piece.whole(), pltpu.SemaphoreType.DMA((1,))],
        time=3.5,
    )


def gelu_and_slope(u):
    phi = 0.5 * lax.erf(u * math.sqrt(0.5)) + 0.5
    bell = jnp.exp(-0.5 * (u * u)) * (1.0 / math.sqrt(2.0 * math.pi))
    return u * phi, phi + u * bell


def feed_up(links, table, low, up_bias, gathered, up_piece):
    tokens, width = low.shape
    inner = up_bias.shape[1]

    def body(scalar, low_ref, bias_ref, *refs):
        act_ref, act_t_ref, slope_ref, weight, sem = refs[4:]
        up_piece.fetch(scalar, sides(refs), weight, sem.at[0])
        up_piece.ready(weight, sem.at[0])

        def forward(j, carry):
            at = aligned(j * width, width, LANES)
            value, slope = gelu_and_slope(dot(low_ref[...], weight[:, at]) + bias_ref[:, at])
            value = value.astype(bf16)
            act_ref[:, at] = value
            act_t_ref[at, :] = turned(value)
            slope_ref[:, at] = slope.astype(bf16)
            return carry

        lax.fori_loop(0, inner // width, forward, 0)

    return call(
        body,
        "feed_up",
        [table, low, up_bias, *flat(gathered)],
        [SMEM] + [VMEM] * 2 + [ANY] * 4,
        [
            shape(tokens, inner, bf16),
            shape(inner, tokens, bf16),
            shape(tokens, inner, bf16),
        ],
        [up_piece.whole(), pltpu.SemaphoreType.DMA((1,))],
        time=8,
    )


def share(core, value, at, keep_ref, send_ref):
    span = value.shape[1] // 2
    low, high = value[:, :span], value[:, span:]
    even = core == 0
    keep_ref[at, :] = jnp.where(even, low, high)
    send_ref[at, :] = jnp.where(even, high, low)


def feed_down(links, table, act, hidden, vectors, cotangent, gathered, down_piece):
    tokens, width = hidden.shape
    inner = act.shape[1]
    extra = 4 * links.dp + 1
    dp = links.dp

    def body(scalar, act_ref, hidden_ref, vec_ref, cot_ref, *refs):
        out_ref, resid_ref, grad_ref, keep_ref, send_ref, sums_ref, weight, sem = refs[4:]
        down_piece.fetch(scalar, sides(refs), weight, sem.at[0])
        down_piece.ready(weight, sem.at[0])
        resid_ref[...] = dot(act_ref[...], weight[...])
        sums_ref[...] = jnp.zeros_like(sums_ref)

        def block(at, first, span):
            branch = resid_ref[at, :] + vec_ref[5:6]
            valid = valid_rows(scalar, extra, first, span)
            add_row(sums_ref, 3, masked_squares(branch, valid))
            normal, inverse = normalize(hidden_ref[at, :] + branch)
            out_ref[at, :] = (normal * vec_ref[6:7] + vec_ref[7:8]).astype(bf16)
            grads = cot_ref[at, :].astype(f32)
            add_row(sums_ref, 1, column_sums(grads * normal))
            add_row(sums_ref, 2, column_sums(grads))
            resid = norm_back(grads, normal, inverse, vec_ref[6:7])
            resid_ref[at, :] = resid
            grad_ffn = resid.astype(bf16)
            grad_ref[at, :] = grad_ffn
            add_row(sums_ref, 0, column_sums(grad_ffn.astype(f32)))
            share(scalar[4 * dp], grad_ffn, at, keep_ref, send_ref)

        by_rows(tokens, block)
        spread_total(sums_ref, 3)

    return call(
        body,
        "feed_down",
        [table, act, hidden, vectors, cotangent, *flat(gathered)],
        [SMEM] + [VMEM] * 4 + [ANY] * 4,
        [
            shape(tokens, width, bf16),
            shape(tokens, width, f32),
            shape(tokens, width, bf16),
            shape(tokens, width // 2, bf16),
            shape(tokens, width // 2, bf16),
            shape(4, width, f32),
        ],
        [down_piece.whole(), pltpu.SemaphoreType.DMA((1,))],
        time=6,
    )


def feed_back(links, table, side, slope, so_far, grad_ffn, up, down, pieces):
    tokens, width = so_far.shape
    up_piece, down_piece = pieces
    span = up_piece.columns
    block = width if span % width == 0 else span
    dp = links.dp

    def body(scalar, slope_ref, so_far_ref, grad_ref, um, ul, *refs):
        hidden_ref, out_ref, bias_ref, up_w, down_w, sems = refs[4:]
        core = scalar[4 * dp]
        half = core if side == 0 else 1 - core
        down_piece.fetch_rows(scalar, half, sides(refs), down_w, sems.at[1])
        up_piece.fetch_side(scalar, side, (um, ul), up_w, sems.at[0])
        hidden_ref[...] = so_far_ref[...]
        down_piece.ready(down_w, sems.at[1])
        up_piece.ready(up_w, sems.at[0])

        def backward(j, carry):
            here = aligned(j * block, block, LANES)
            at = aligned(half * span + j * block, block, LANES)
            grads = dot_rows(grad_ref[...], down_w[here, :]) * slope_ref[:, at].astype(f32)
            grads = grads.astype(bf16)
            bias_ref[:, here] = column_sums(grads.astype(f32))
            hidden_ref[...] += dot_rows(grads, up_w[:, here])
            out_ref[:, here] = grads
            return carry

        lax.fori_loop(0, span // block, backward, 0)

    return call(
        body,
        "feed_back",
        [table, slope, so_far, grad_ffn, *map(far, up[side]), *flat(down)],
        [SMEM] + [VMEM] * 3 + [ANY] * 6,
        [shape(tokens, width, f32), shape(tokens, span, bf16), shape(1, span, f32)],
        [
            pltpu.VMEM((width, span), bf16),
            pltpu.VMEM((span, width), bf16),
            pltpu.SemaphoreType.DMA((2,)),
        ],
        time=0.01,
    )


def before_attention(links, table, grad_hidden, normal, inverse, vectors, gathered, piece):
    tokens, width = normal.shape

    def body(scalar, grad_ref, normal_ref, inverse_ref, vec_ref, *refs):
        resid_ref, gm_ref, keep_ref, send_ref, sums_ref, weight, whole, sem = refs[4:]
        piece.fetch(scalar, sides(refs), weight, sem.at[0])
        sums_ref[...] = jnp.zeros_like(sums_ref)

        def block(at, first, span):
            grads = grad_ref[at, :]
            normal_ = normal_ref[at, :]
            add_row(sums_ref, 1, column_sums(grads * normal_))
            add_row(sums_ref, 2, column_sums(grads))
            resid = norm_back(grads, normal_, inverse_ref[at, :], vec_ref[3:4])
            resid_ref[at, :] = resid
            grad_attn = resid.astype(bf16)
            whole[at, :] = grad_attn
            add_row(sums_ref, 0, column_sums(grad_attn.astype(f32)))
            share(scalar[4 * links.dp], grad_attn, at, keep_ref, send_ref)

        by_rows(tokens, block)
        piece.ready(weight, sem.at[0])
        gm_ref[...] = dot_rows(whole[...], weight[...]).astype(bf16)

    return call(
        body,
        "before_attention",
        [table, grad_hidden, normal, inverse, vectors, *flat(gathered)],
        [SMEM] + [VMEM] * 4 + [ANY] * 4,
        [
            shape(tokens, width, f32),
            shape(tokens, width, bf16),
            shape(tokens, width // 2, bf16),
            shape(tokens, width // 2, bf16),
            shape(3, width, f32),
        ],
        [piece.whole(), pltpu.VMEM((tokens, width), bf16), pltpu.SemaphoreType.DMA((1,))],
        time=0.01,
    )


def weight_gradient(name, links, table, left, right, rows):
    outer, tokens = left[0].shape
    columns = right[0].shape[1]
    block = min(outer, 768)
    wide = min(columns, 512)

    def body(scalar, lm, lt, rm, rt, *refs):
        tile = refs[-1]

        def one(j, carry):
            at = aligned(j // (columns // wide) * block, block, 8)
            to = aligned(j % (columns // wide) * wide, wide, LANES)
            tile[at, to] = dot(lm[at, :], rm[:, to]) + dot(lt[at, :], rt[:, to])
            return carry

        lax.fori_loop(0, outer // block * (columns // wide), one, 0)
        place(scalar, links.dp, tile, refs[:3], rows, slice(None))

    return call(
        body,
        name,
        [table, *left, *right],
        [SMEM] + [VMEM] * 4,
        placed(links.dp, rows, columns),
        [pltpu.VMEM((outer, columns), f32)],
    )


class Shares:
    def __init__(self, refs, tokens):
        self.sent, self.kept, self.came = refs
        self.tokens = tokens

    def rows(self, ref, i):
        return ref[i * self.tokens : (i + 1) * self.tokens, :]

    def add(self, one, other):
        return (one.astype(f32) + other.astype(f32)).astype(bf16)

    def own(self):
        return [self.rows(self.kept, 0)] + [
            self.add(self.rows(self.kept, i), self.rows(self.came, 2 + i)) for i in (1, 2)
        ]

    def others(self):
        return [self.rows(self.came, 0)] + [
            self.add(self.rows(self.sent, 4 + i), self.rows(self.came, i)) for i in (1, 2)
        ]

    def partners(self):
        return [self.rows(self.sent, 0)] + [
            self.add(self.rows(self.sent, i), self.rows(self.came, 4 + i)) for i in (1, 2)
        ]


def attention_gradient(name, links, table, rows_t, groups, rows, out=None, vectors=None, folds=0, sums=()):
    width, tokens = rows_t[0].shape
    dp = links.dp
    wide = 3 * LANES
    half = width // 2
    total = wide * len(groups) + (half if out else 0) + (LANES if vectors is not None else 0)
    given = [value for group in groups for value in group]
    more = list(out or []) + ([*vectors, *sums] if vectors is not None else [])

    def body(scalar, xm, xt, *refs):
        group_refs = refs[: len(given)]
        more_refs = list(refs[len(given) : len(given) + len(more)])
        outs = refs[len(given) + len(more) :]
        sum_ref, tile = outs[3], outs[4]
        for g in range(len(groups)):
            shares = Shares(group_refs[3 * g : 3 * g + 3], tokens)
            mine = jnp.concatenate(shares.own(), axis=1)
            theirs = jnp.concatenate(shares.others(), axis=1)
            tile[:, g * wide : (g + 1) * wide] = dot(xm[...], mine) + dot(xt[...], theirs)
            sums_ = column_sums(mine.astype(f32)) + column_sums(theirs.astype(f32))
            sum_ref[g : g + 1, :] = sums_
        at = wide * len(groups)
        if out:
            mm, mt, gm, gt = more_refs[:4]
            tile[:, at : at + half] = dot(mm[...], gm[...]) + dot(mt[...], gt[...])
            at += half
        if vectors is not None:
            sums3, sums2, kept, sent, sums1, *sum_refs = more_refs
            even = scalar[4 * dp] == 0
            bias = jnp.concatenate(
                [
                    jnp.where(even, kept[...], sent[...]),
                    jnp.where(even, sent[...], kept[...]),
                ],
                axis=1,
            )
            biases = [
                jnp.concatenate(
                    [
                        bias[:, (i * folds + j) * rows : (i * folds + j + 1) * rows]
                        for i in range(dp)
                    ],
                    axis=1,
                )
                for j in range(folds)
            ]
            head = jnp.concatenate(
                [jnp.zeros((2, width), f32), sums3[...], sums2[0:3]]
                + biases
                + [sums1[...], sums2[3:4]],
                axis=0,
            )
            every = [ref[i : i + 1, :] for ref in sum_refs for i in range(ref.shape[0])]
            every += [sum_ref[g : g + 1, :] for g in range(len(groups))]
            lane = lax.broadcasted_iota(jnp.int32, (1, width), 1)
            owned = (lane // LANES) % 2 == scalar[4 * dp]
            lines = []
            for j in (0, 2):
                parts = [s[:, j * LANES : (j + 1) * LANES] for s in every for _ in range(2)]
                lines.append(jnp.where(owned, jnp.concatenate(parts, axis=1), 0.0))
            row = lax.broadcasted_iota(jnp.int32, (LANES, width), 0)
            padded = jnp.concatenate(
                [head, jnp.zeros((LANES - head.shape[0], width), f32)], axis=0
            )
            padded = jnp.where(row == 0, lines[0], jnp.where(row == 1, lines[1], padded))
            tile[:, at : at + LANES] = turned(padded)
        place(scalar, dp, tile, outs[:3], rows, slice(None))

    return call(
        body,
        name,
        [table, *rows_t, *given, *more],
        [SMEM] + [VMEM] * (2 + len(given) + len(more)),
        placed(dp, rows, total) + [shape(len(groups), wide, f32)],
        [pltpu.VMEM((width, total), f32)],
    )


def input_gradient(links, table, groups, resid, gathered, qkv_piece):
    tokens, width = resid.shape
    given = [value for group in groups for value in group]

    def body(scalar, resid_ref, *refs):
        group_refs = refs[: len(given)]
        out_ref, weight, grads, sem = refs[len(given) + 4 :]
        qkv_piece.fetch(scalar, sides(refs[len(given) :]), weight, sem.at[0])
        core = scalar[4 * links.dp]
        for g in range(len(groups)):
            shares = Shares(group_refs[3 * g : 3 * g + 3], tokens)
            for owner, values in ((core, shares.own()), (1 - core, shares.partners())):
                for j, value in enumerate(values):
                    at = j * width + (2 * g + owner) * LANES
                    grads[:, aligned(at, LANES, LANES)] = value
        qkv_piece.ready(weight, sem.at[0])
        out_ref[...] = resid_ref[...] + dot_rows(grads[...], weight[...])

    return call(
        body,
        "input_gradient",
        [table, resid, *given, *flat(gathered)],
        [SMEM] + [VMEM] * (1 + len(given)) + [ANY] * 4,
        [shape(tokens, width, f32)],
        [qkv_piece.whole(), pltpu.VMEM((tokens, 3 * width), bf16), pltpu.SemaphoreType.DMA((1,))],
        time=20,
    )[0]


def closing(links, table, early, late, folds, width):
    rows = early[0].shape[0]
    wide = 3 * LANES
    half = width // 2
    base = 8

    def body(scalar, em, et, lm, lt, *outs):
        qkv_ref, out_ref, *vec_refs, up_ref, rms_ref = outs

        def write(core):
            for owner, early_ref, late_ref in ((core, em, lm), (1 - core, et, lt)):
                groups = [(early_ref, 0), (early_ref, wide), (late_ref, 0)]
                for g, (ref, first) in enumerate(groups):
                    for j in range(3):
                        at = j * width + (2 * g + owner) * LANES
                        qkv_ref[:, at : at + LANES] = ref[
                            :, first + j * LANES : first + (j + 1) * LANES
                        ].astype(f32)
                out_ref[:, owner * half : (owner + 1) * half] = early_ref[
                    :, 2 * wide : 2 * wide + half
                ].astype(f32)

        for core in range(2):
            pl.when(scalar[4 * links.dp] == core)(lambda core=core: write(core))
        last = slice(wide, wide + LANES)
        vectors = turned(lm[:, last].astype(f32) + lt[:, last].astype(f32))
        for i, ref in enumerate(vec_refs):
            ref[...] = vectors[i : i + 1]
        for i in range(folds):
            up_ref[:, i * rows : (i + 1) * rows] = vectors[base + i : base + i + 1]
        at = base + folds
        count = vectors[at + 2 : at + 3] * width
        for i, line in enumerate((at, at + 1, at + 3)):
            value = jnp.sqrt(vectors[line : line + 1] / count + 1e-06)
            rms_ref[:, i : i + 1] = value[:, 0:1]

    return call(
        body,
        "closing",
        [table, *early, *late],
        [SMEM] + [VMEM] * 4,
        [shape(rows, 3 * width, f32), shape(rows, width, f32)]
        + [shape(1, rows, f32)] * base
        + [shape(1, folds * rows, f32), shape(1, 3, f32)],
    )


def settle(links, reduction):
    mine = reduction.finish()
    return mine, links.swap(mine)


def shards(
    tokens,
    lengths,
    qkv_weight,
    query_bias,
    value_bias,
    out_weight,
    out_bias,
    norm1_gain,
    norm1_shift,
    up_weight,
    up_bias,
    down_weight,
    down_bias,
    norm2_gain,
    norm2_shift,
    cotangent,
):
    seq_dev, ctx_tok, width = tokens.shape
    assert seq_dev == 1 and width // HEADS == LANES // 2
    scale = (width // HEADS) ** (-0.5)
    links = Links()
    dp = links.dp
    rows = tokens.reshape(ctx_tok, width)
    cot = cotangent.reshape(ctx_tok, width)
    block = lax.axis_index("ctx")
    start = block * ctx_tok
    table = links.table(lengths[0], start)

    shard = qkv_weight.shape[0]
    inner = down_weight.shape[0] * dp
    folds = down_weight.shape[0] // shard
    half = [w.shape[1] // 2 for w in (qkv_weight, out_weight, up_weight, down_weight)]
    qkv_piece = Piece(dp, shard, half[0], 0)
    vector_piece = Piece(dp, shard, LANES, half[0])
    up_piece = Piece(dp, shard, half[2], 0)
    out_piece = Piece(dp, shard, half[1], half[2])
    down_piece = Piece(dp, down_weight.shape[0], half[3], 0)
    ffn_pieces = (up_piece, down_piece)

    columns = [query_bias, value_bias, out_bias, norm1_gain, norm1_shift]
    columns += [down_bias, norm2_gain, norm2_shift]
    base = len(columns)
    columns += [up_bias[i * shard : (i + 1) * shard] for i in range(folds)]
    packed = jnp.stack(columns, axis=1)
    packed = jnp.pad(packed, ((0, 0), (0, LANES - packed.shape[1])))
    qkv_sent = jnp.concatenate([half_columns(links, qkv_weight), packed], axis=1)
    up_sent = jnp.concatenate(
        [half_columns(links, up_weight), half_columns(links, out_weight)], axis=1
    )
    down_sent = half_columns(links, down_weight)

    qkv_held = joined(links.cross(qkv_sent))
    up_steps = []
    up_held = links.cross_slowly(
        after(up_sent, qkv_held), lambda more: (up_steps.append(more), more)[1]
    )
    down_sent = after(down_sent, up_held)
    qkv_held = links.first(qkv_held)
    qkv = links.second(after(qkv_held, *up_steps), *up_held)
    up_held = after(joined(up_held), qkv[0][1])
    query, kv, vectors, up_bias_row, rows_t = project(
        links, table, after(rows, up_held), qkv, qkv_piece, vector_piece, scale, base, folds
    )
    early_steps = []

    def ready(more):
        early_steps.append(more)
        return after(more, query)

    down_held = links.cross_slowly(after(down_sent, up_held), ready)
    up_held = links.first(up_held, query)
    kv = after(kv, up_held, *early_steps)
    rows_t = [rows_t, links.swap(rows_t)]
    if links.ctx == 2:
        parts = [kv, links.swap(kv)]
        starts = [start, (1 - block) * ctx_tok]
    else:
        parts = [lax.all_gather(kv, "ctx", axis=0, tiled=True)]
        starts = [jnp.int32(0)]
    groups = 3
    count = width // LANES // groups
    forward = []
    waits = [(), (), ()]
    for i in range(groups):
        given = after(query, *waits[i], *(forward[-1][1:2] if forward else ()))
        forward.append(attend(given, parts, starts, lengths[0], i * count, count))
        if i == 0:
            down_held = joined(down_held, forward[0][1])
            waits[1] = (down_held,)
    up = links.second(up_held, forward[1][1])
    down_held = links.first(after(down_held, forward[1][1]), forward[2][1])
    mixed = [f[1] for f in forward]
    hidden, low, low_t, mixed_t, normal, deviation, sums1 = after_attention(
        links, table, after(rows, down_held), mixed, vectors, up, out_piece
    )
    low_t = [low_t, links.swap(low_t)]
    mixed_t = [mixed_t, links.swap(mixed_t)]
    act, act_t, slope = feed_up(links, table, low, up_bias_row, up, up_piece)
    down = links.second(after(down_held, forward[2][1]), act)
    act_t = [act_t, links.swap(after(act_t, down[1][1]))]
    output, resid2, grad_ffn, ffn_keep, ffn_send, sums2 = feed_down(
        links, table, act, hidden, vectors, cot, down, down_piece
    )
    ffn_came = links.swap(ffn_send)
    down_sum = Sum(
        links,
        weight_gradient(
            "down_gradient", links, table, act_t, [ffn_keep, ffn_came], down_piece.rows
        ),
    )
    given = after(resid2, down_sum.prepare())
    down_sum.send()
    grad_hidden, upper_send, bias_sent = feed_back(
        links, table, 1, slope, given, grad_ffn, up, down, ffn_pieces
    )
    upper_came = links.swap(upper_send)
    grad_hidden, upper_keep, bias_kept = feed_back(
        links, table, 0, slope, grad_hidden, grad_ffn, up, down, ffn_pieces
    )
    up_sum = Sum(
        links,
        weight_gradient(
            "up_gradient", links, table, low_t, [upper_keep, upper_came], up_piece.rows
        ),
    )
    down_sum.hold(grad_hidden)
    given = after(grad_hidden, up_sum.prepare(), down_sum.prepare())
    up_sum.send()
    down_sum.send()
    resid1, grad_mixed, attn_keep, attn_send, sums3 = before_attention(
        links, table, given, normal, deviation, vectors, up, out_piece
    )
    out_parts = [*mixed_t, attn_keep, links.swap(attn_send)]

    def back_through(i, given):
        turned_mixed, _, weights, inverse = forward[i]
        sent, kept = attend_back(
            given,
            parts,
            grad_mixed,
            turned_mixed,
            weights,
            inverse,
            scale,
            i * count,
            links.core,
        )
        if links.ctx == 2:
            return [sent, kept, links.swap(sent)]
        whole = []
        for value in (sent, kept):
            keys, values = jnp.split(value[ctx_tok:], 2, axis=0)
            both = lax.psum_scatter(
                jnp.concatenate([keys, values], axis=1), "ctx", scatter_dimension=0, tiled=True
            )
            whole.append([value[:ctx_tok], both[:, :LANES], both[:, LANES:]])
        blank = jnp.zeros((4 * ctx_tok, LANES), bf16)
        sent = jnp.concatenate(whole[0] + [blank], axis=0)
        return [sent, jnp.concatenate(whole[1], axis=0), links.swap(sent)]

    given = after(query, grad_mixed)
    back = [back_through(0, given)]
    back.append(back_through(1, after(query, back[0][1])))
    down_sum.hold(back[1][1])
    up_sum.hold(back[1][1])
    given = after(rows_t[0], down_sum.prepare(), up_sum.prepare())
    down_sum.send()
    up_sum.send()
    *early, early_sums = attention_gradient(
        "early_gradient", links, table, [given, rows_t[1]], back[:2], shard, out=out_parts
    )
    early_sum = Sum(links, early)
    down_sum.hold(early[2])
    up_sum.hold(early[2])
    given = after(query, early_sum.prepare(), down_sum.prepare(), up_sum.prepare())
    early_sum.send()
    down_sum.send()
    up_sum.send()
    back.append(back_through(2, given))
    up_sum.hold(back[2][1])
    early_sum.hold(back[2][1])
    down_sum.hold(back[2][1])
    up_sum.hold(back[2][1])
    given = after(rows_t[0], early_sum.prepare(), up_sum.prepare())
    early_sum.send()
    up_sum.send()
    *late, _ = attention_gradient(
        "late_gradient",
        links,
        table,
        [given, rows_t[1]],
        back[2:],
        shard,
        vectors=[sums3, sums2, bias_kept, bias_sent, sums1],
        folds=folds,
        sums=[early_sums],
    )
    late_sum = Sum(links, late)
    down_sum.hold(late[2])
    down_mine = down_sum.finish()
    given = after(resid1, late_sum.prepare(), down_mine)
    late_sum.send()
    input_grad = input_gradient(links, table, back, given, qkv, qkv_piece)
    late_sum.hold(input_grad)
    early_sum.hold(input_grad)
    up_sum.hold(input_grad)
    up_mine = up_sum.finish()
    down_grad = both_halves(links, down_mine, links.swap(down_mine))
    up_grad = both_halves(links, up_mine, links.swap(up_mine))
    early = settle(links, early_sum)
    late = settle(links, late_sum)
    qkv_grad, out_grad, *sums, up_bias_grad, stream_rms = closing(
        links, table, early, late, folds, width
    )
    sums = [value.reshape(shard) for value in sums]
    return (
        output.reshape(seq_dev, ctx_tok, width),
        input_grad.reshape(seq_dev, ctx_tok, width),
        stream_rms.reshape(3),
        qkv_grad,
        sums[0],
        sums[1],
        out_grad,
        sums[2],
        sums[3],
        sums[4],
        up_grad,
        up_bias_grad.reshape(-1),
        down_grad,
        sums[5],
        sums[6],
        sums[7],
    )


def solution(mesh):
    in_specs = (
        P("dp", "ctx", None),
        P("dp"),
        P("dp", None),
        P("dp"),
        P("dp"),
        P("dp", None),
        P("dp"),
        P("dp"),
        P("dp"),
        P("dp", None),
        P("dp"),
        P("dp", None),
        P("dp"),
        P("dp"),
        P("dp"),
        P("dp", "ctx", None),
    )
    out_specs = (
        P("dp", "ctx", None),
        P("dp", "ctx", None),
        P(),
        P("dp", None),
        P("dp"),
        P("dp"),
        P("dp", None),
        P("dp"),
        P("dp"),
        P("dp"),
        P("dp", None),
        P("dp"),
        P("dp", None),
        P("dp"),
        P("dp"),
        P("dp"),
    )
    return jax.shard_map(shards, mesh=mesh, in_specs=in_specs, out_specs=out_specs, check_vma=False)
```
